32 devices in a mesh: dp: 8 (over z, x), tensor: 4 (over y, core).
Axes of the slice: x: 2, y: 2, z: 4, core: 2. Of those that a mesh axis runs over, the one named last changes fastest.
Arguments:
- prompt_tokens: bfloat16 [16, 1024, 768], P('dp', 'tensor'), may hold values from -6 to 6
- continuation_tokens: bfloat16 [128, 128, 768], P('dp', 'tensor'), may hold values from -6 to 6
- prompt_index: int32 [128], P('dp'), may hold values from 0 to 1, as said below
- attention_gain: bfloat16 [768], P('dp'), may hold values from 0.25 to 1.75
- query_weight: bfloat16 [768, 768], P('dp', 'tensor'), may hold values from -0.3125 to 0.3125
- key_weight: bfloat16 [768, 768], P('dp', 'tensor'), may hold values from -0.3125 to 0.3125
- value_weight: bfloat16 [768, 768], P('dp', 'tensor'), may hold values from -0.21875 to 0.21875
- output_weight: bfloat16 [768, 768], P('tensor', 'dp'), may hold values from -1.25 to 1.25
- feedforward_gain: bfloat16 [768], P('dp'), may hold values from 0.25 to 1.75
- gate_weight: bfloat16 [768, 2048], P('dp', 'tensor'), may hold values from -0.21875 to 0.21875
- up_weight: bfloat16 [768, 2048], P('dp', 'tensor'), may hold values from -0.21875 to 0.21875
- down_weight: bfloat16 [2048, 768], P('tensor', 'dp'), may hold values from -0.1875 to 0.1875
- prompt_cotangent: bfloat16 [16, 1024, 768], P('dp', 'tensor'), may hold values from -6 to 6
- continuation_cotangent: bfloat16 [128, 128, 768], P('dp', 'tensor'), may hold values from -6 to 6
Outputs:
- out_prompt: bfloat16 [16, 1024, 768], P('dp', 'tensor')
- out_continuation: bfloat16 [128, 128, 768], P('dp', 'tensor')
- input_grad_prompt: float32 [16, 1024, 768], P('dp', 'tensor')
- input_grad_continuation: float32 [128, 128, 768], P('dp', 'tensor')
- attention_gain_grad: float32 [768], P('dp')
- query_grad: float32 [768, 768], P('dp', 'tensor')
- key_grad: float32 [768, 768], P('dp', 'tensor')
- value_grad: float32 [768, 768], P('dp', 'tensor')
- output_grad: float32 [768, 768], P('tensor', 'dp')
- feedforward_gain_grad: float32 [768], P('dp')
- gate_grad: float32 [768, 2048], P('dp', 'tensor')
- up_grad: float32 [768, 2048], P('dp', 'tensor')
- down_grad: float32 [2048, 768], P('tensor', 'dp')
The draws below stay inside these ranges and needn't reach their ends.
Inputs may be any that keep to these rules, and one draw needn't show every extreme that they name: `prompt_index`: among the 16 continuations held by one index of dp, each of that index's 2 prompts is named by exactly 8.
All inputs are finite; a program needn't handle non-finite values.
Results may differ from the reference program's by a relative error of at most 0.022.
Values may be sent and summed in bfloat16 or wider, within the bound.
No kernel may reach another device: no remote copies, remote signals or barrier semaphores. Data moves between devices by JAX's collectives and lax.ppermute only.
A program may use at most 192 MiB of HBM per device.

```python
import math
import jax
import jax.numpy as jnp
from jax import lax

D = 768
HEADS = 12
HDIM = 64
FF = 2048
PLEN = 1024
CLEN = 128
CONTS = 8
NP_DEV = 2
NP = 16
NC = 128


def draw_prompt_index(key, part):
    blocks = NP // NP_DEV
    count = NP_DEV * CONTS

    def one_block(number):
        order = jax.random.permutation(jax.random.fold_in(key, number), count)
        return order // CONTS
    return jax.vmap(one_block)(jnp.arange(blocks)).reshape(NC).astype(jnp.int32)


def block_scale(key, dims, shards, smallest, top_value):
    loudness = 1.0
    for axis_at, blocks in shards:
        draws = jax.random.uniform(jax.random.fold_in(jax.random.fold_in(key, 6), axis_at), (blocks,), jnp.float32, smallest / len(shards), top_value / len(shards))
        loudness = loudness * jnp.repeat(jnp.exp(draws), dims[axis_at] // blocks).reshape((-1,) + (1,) * (len(dims) - 1 - axis_at))
    return loudness


def noise(stream_key, extent, width, limit, cuts=(), held_as=jnp.bfloat16):
    level = block_scale(stream_key, extent, cuts, -0.22, 0.18) if cuts else 1.0
    values = jax.random.normal(stream_key, extent, jnp.float32) * width * level
    return jnp.minimum(jnp.maximum(values, -limit), limit).astype(held_as)


def setup_inputs(seed: int = 0) -> dict:
    key_list = jax.random.split(jax.random.key(seed), 15)
    return {
        "prompt_tokens": noise(key_list[0], (NP, PLEN, D), 1.0, 6.0, ((0, 8), (1, 4))),
        "continuation_tokens": noise(key_list[1], (NC, CLEN, D), 1.0, 6.0, ((0, 8), (1, 4))),
        "prompt_index": draw_prompt_index(jax.random.fold_in(key_list[14], 71), 0),
        "attention_gain": jnp.clip(1.0 + 0.15 * jax.random.normal(key_list[3], (D,), jnp.float32), 0.25, 1.75).astype(jnp.bfloat16),
        "query_weight": noise(key_list[4], (D, D), (D // 2) ** -0.5, 0.3125, ((0, 8), (1, 4))),
        "key_weight": noise(key_list[5], (D, D), (D // 2) ** -0.5, 0.3125, ((0, 8), (1, 4))),
        "value_weight": noise(key_list[6], (D, D), D ** -0.5, 0.21875, ((0, 8), (1, 4))),
        "output_weight": noise(key_list[7], (D, D), (D // 32) ** -0.5, 1.25, ((0, 4), (1, 8))),
        "feedforward_gain": jnp.clip(1.0 + 0.15 * jax.random.normal(key_list[8], (D,), jnp.float32), 0.25, 1.75).astype(jnp.bfloat16),
        "gate_weight": noise(key_list[9], (D, FF), D ** -0.5, 0.21875, ((0, 8), (1, 4))),
        "up_weight": noise(key_list[10], (D, FF), D ** -0.5, 0.21875, ((0, 8), (1, 4))),
        "down_weight": noise(key_list[11], (FF, D), (FF // 2) ** -0.5, 0.1875, ((0, 4), (1, 8))),
        "prompt_cotangent": noise(key_list[12], (NP, PLEN, D), 1.0, 6.0, ((0, 8), (1, 4))),
        "continuation_cotangent": noise(key_list[13], (NC, CLEN, D), 1.0, 6.0, ((0, 8), (1, 4))),
    }


@jax.custom_vjp
def low(v):
    return lax.optimization_barrier(v.astype(jnp.bfloat16)).astype(jnp.float32)

@jax.custom_vjp
def low_back(v):
    return v

def low_keep(v):
    return (low(v), None)

def low_pass(kept, grad):
    return (grad,)

def back_keep(v):
    return (v, None)

def back_low(kept, grad):
    return (low(grad),)
low.defvjp(low_keep, low_pass)
low_back.defvjp(back_keep, back_low)
NEGATIVE = -1e+30
EPSILON = 1e-06
HIGHEST = lax.Precision.HIGHEST

def matmul(left, right):
    return jnp.dot(left, right, precision=HIGHEST, preferred_element_type=jnp.float32)

def rotation_tables():
    half = HDIM // 2
    places = jnp.concatenate([jnp.arange(PLEN, dtype=jnp.float32), PLEN + jnp.tile(jnp.arange(CLEN, dtype=jnp.float32), CONTS)])
    frequency = 10000.0 ** (-jnp.arange(half, dtype=jnp.float32) / half)
    angles = places[:, None] * frequency[None, :]
    return (jnp.cos(angles)[:, None, :], jnp.sin(angles)[:, None, :])

def rotate(field, cosine, sine):
    half = field.shape[-1] // 2
    first = field[..., :half]
    second = field[..., half:]
    return jnp.concatenate([first * cosine - second * sine, second * cosine + first * sine], -1)

def rms_norm(field, gain):
    return field * lax.rsqrt(lax.optimization_barrier(jnp.mean(field * field, -1, keepdims=True)) + EPSILON) * gain

def attention(query, key, value, segment, scale):
    total = query.shape[0]
    block = min(512, total)
    places = jnp.arange(total, dtype=jnp.int32)

    def one_block(start):
        rows = lax.dynamic_slice_in_dim(query, start, block, 0)
        row_places = start + jnp.arange(block, dtype=jnp.int32)
        row_segment = lax.dynamic_slice_in_dim(segment, start, block, 0)
        scores = low_back(jnp.einsum('qhe,khe->hqk', rows, key, precision=HIGHEST) * scale)
        allowed = (places[None, :] <= row_places[:, None]) & ((segment[None, :] == 0) | (segment[None, :] == row_segment[:, None]))
        scores = jnp.where(allowed[None], scores, NEGATIVE)
        highest = lax.optimization_barrier(jnp.max(scores, -1, keepdims=True))
        raised = jnp.exp(scores - highest)
        shares = low(raised / lax.optimization_barrier(jnp.sum(raised, -1, keepdims=True)))
        return jnp.einsum('hqk,khe->qhe', shares, value, precision=HIGHEST)
    starts = jnp.arange(0, total, block, dtype=jnp.int32)
    pieces = lax.map(jax.checkpoint(one_block), starts)
    return pieces.reshape(total, query.shape[1], query.shape[2])

def group_forward(tokens, weights):
    attention_gain, query_weight, key_weight, value_weight, output_weight, feedforward_gain, gate_weight, up_weight, down_weight = weights
    total = tokens.shape[0]
    cosine, sine = rotation_tables()
    segment = jnp.concatenate([jnp.zeros((PLEN,), jnp.int32), 1 + jnp.repeat(jnp.arange(CONTS, dtype=jnp.int32), CLEN)])
    query = low(rotate(low_back(matmul(tokens, query_weight)).reshape(total, HEADS, HDIM), cosine, sine))
    key = low(rotate(low_back(matmul(tokens, key_weight)).reshape(total, HEADS, HDIM), cosine, sine))
    value = low(low_back(matmul(tokens, value_weight)).reshape(total, HEADS, HDIM))
    mixed = attention(query, key, value, segment, 1.0 / math.sqrt(HDIM)).reshape(total, D)
    mixed = low(low_back(mixed))
    attended = low_back(matmul(mixed, output_weight))
    normed = rms_norm(tokens + attended, attention_gain)
    normed_low = low(normed)
    gate = low_back(matmul(normed_low, gate_weight))
    up_part = low_back(matmul(normed_low, up_weight))
    hidden = low(jax.nn.silu(gate) * up_part)
    fed = low_back(matmul(hidden, down_weight))
    return rms_norm(normed + fed, feedforward_gain)

def reference(prompt_tokens, continuation_tokens, prompt_index, attention_gain, query_weight, key_weight, value_weight, output_weight, feedforward_gain, gate_weight, up_weight, down_weight, prompt_cotangent, continuation_cotangent):
    weights = (attention_gain.astype(jnp.float32), query_weight.astype(jnp.float32), key_weight.astype(jnp.float32), value_weight.astype(jnp.float32), output_weight.astype(jnp.float32), feedforward_gain.astype(jnp.float32), gate_weight.astype(jnp.float32), up_weight.astype(jnp.float32), down_weight.astype(jnp.float32))
    block_count = NP_DEV * CONTS
    global_prompt = jnp.arange(NC, dtype=jnp.int32) // block_count * NP_DEV + prompt_index.astype(jnp.int32)
    order = jnp.argsort(global_prompt, stable=True).astype(jnp.int32).reshape(NP, CONTS)

    def one_group(totals, number):
        members = order[number]
        tokens = jnp.concatenate([prompt_tokens[number].astype(jnp.float32), continuation_tokens[members].astype(jnp.float32).reshape(CONTS * CLEN, D)], 0)
        cotangent = jnp.concatenate([prompt_cotangent[number].astype(jnp.float32), continuation_cotangent[members].astype(jnp.float32).reshape(CONTS * CLEN, D)], 0)
        output, pullback = jax.vjp(group_forward, tokens, weights)
        grad_tokens, grad_weights = pullback(cotangent)
        totals = jax.tree.map(jnp.add, totals, grad_weights)
        return (totals, (output[:PLEN], output[PLEN:].reshape(CONTS, CLEN, D), grad_tokens[:PLEN], grad_tokens[PLEN:].reshape(CONTS, CLEN, D)))
    initial = tuple((jnp.zeros_like(weight) for weight in weights))
    totals, (out_first, out_rest, grad_first, grad_rest) = lax.scan(one_group, initial, jnp.arange(NP, dtype=jnp.int32))
    flat = order.reshape(NC)
    out_cont = jnp.zeros((NC, CLEN, D), jnp.float32).at[flat].set(out_rest.reshape(NC, CLEN, D))
    grad_cont = jnp.zeros((NC, CLEN, D), jnp.float32).at[flat].set(grad_rest.reshape(NC, CLEN, D))
    return (out_first.astype(jnp.bfloat16), out_cont.astype(jnp.bfloat16), grad_first, grad_cont, totals[0], totals[1], totals[2], totals[3], totals[4], totals[5], totals[6], totals[7], totals[8])
```

```python
import functools
import math

import jax
import jax.numpy as jnp
from jax import lax
from jax.experimental import pallas as pl
from jax.experimental.pallas import tpu as pltpu
from jax.sharding import Mesh
from jax.sharding import PartitionSpec as P

HDIM = 64
NEGATIVE = -1e30
EPSILON = 1e-06
BF16 = jnp.bfloat16
F32 = jnp.float32
LAST = ((1,), (1,))
FIRST = ((0,), (0,))
LIMIT = 64000 * 1024


def dotf(left, right, contract=((1,), (0,))):
    return lax.dot_general(left, right, (contract, ((), ())), preferred_element_type=F32)


def whole(shape=None, space=pltpu.VMEM):
    return pl.BlockSpec(memory_space=space)


def params(limit=LIMIT, **more):
    return pltpu.CompilerParams(vmem_limit_bytes=limit, **more)


def fill_order(index_ref, order_ref, count_ref, groups, total):
    count_ref[0] = 0
    count_ref[1] = 0

    def place(number, carry):
        prompt = index_ref[number]
        seen = count_ref[prompt]
        order_ref[prompt * groups + seen] = number
        count_ref[prompt] = seen + 1
        return carry

    lax.fori_loop(0, total, place, 0)


def pack_kernel(groups, place, index, prompt_x, cont_x, prompt_dy, cont_dy, x_own, x_send, dy_own, dy_send, order, count):
    rows = prompt_x.shape[1]
    step = cont_x.shape[1]
    fill_order(index, order, count, groups, cont_x.shape[0])
    mine = place[2]
    for prompt, cont, own, send in ((prompt_x, cont_x, x_own, x_send), (prompt_dy, cont_dy, dy_own, dy_send)):
        for which, out in ((mine, own), (1 - mine, send)):
            out[0:rows, :] = prompt[which]
            for slot in range(groups):
                out[rows + slot * step : rows + (slot + 1) * step, :] = cont[order[which * groups + slot]]


def pack(place, index, prompt_x, cont_x, prompt_dy, cont_dy):
    groups = cont_x.shape[0] // prompt_x.shape[0]
    count = prompt_x.shape[1] + groups * cont_x.shape[1]
    rows = jax.ShapeDtypeStruct((count, prompt_x.shape[2]), BF16)
    return pl.pallas_call(
        functools.partial(pack_kernel, groups),
        out_shape=(rows,) * 4,
        in_specs=[whole(space=pltpu.SMEM)] * 2 + [whole()] * 4,
        out_specs=(whole(),) * 4,
        scratch_shapes=[pltpu.SMEM((2 * groups,), jnp.int32), pltpu.SMEM((2,), jnp.int32)],
        compiler_params=params(),
        name="pack_rows",
    )(place, index, prompt_x, cont_x, prompt_dy, cont_dy)


def unpack_kernel(groups, place, index, own, back, prompt_out, cont_out, order, count):
    rows = prompt_out.shape[1]
    step = cont_out.shape[1]
    fill_order(index, order, count, groups, cont_out.shape[0])
    mine = place[2]
    for which, source in ((mine, own), (1 - mine, back)):
        prompt_out[which] = source[0:rows, :].astype(prompt_out.dtype)
        for slot in range(groups):
            piece = source[rows + slot * step : rows + (slot + 1) * step, :]
            cont_out[order[which * groups + slot]] = piece.astype(cont_out.dtype)


def unpack(place, index, own, back, rows, step, dtype):
    conts = index.shape[0]
    groups = conts // 2
    width = own.shape[1]
    return pl.pallas_call(
        functools.partial(unpack_kernel, groups),
        out_shape=(
            jax.ShapeDtypeStruct((2, rows, width), dtype),
            jax.ShapeDtypeStruct((conts, step, width), dtype),
        ),
        in_specs=[whole(space=pltpu.SMEM)] * 2 + [whole()] * 2,
        out_specs=(whole(),) * 2,
        scratch_shapes=[pltpu.SMEM((2 * groups,), jnp.int32), pltpu.SMEM((2,), jnp.int32)],
        compiler_params=params(),
        name="unpack_rows",
    )(place, index, own, back)


def blocks(fast, place, rows, model):
    if not fast:
        return [(0, (t,), t, 0, model) for t in range(4)]
    z, x, y, c = place[0], place[1], place[2], place[3]
    found = []
    for dc in range(2):
        for kx in range(2):
            for ky in range(2):
                for kz in range(4):
                    t = 2 * (y ^ ky) + (c ^ dc)
                    row = ((z ^ kz) * 2 + (x ^ kx)) * rows
                    found.append((2 * dc + kx, (ky, kz), t, row, rows))
    return found


def load_weights(fast, place, pieces, held, sems, rows, model):
    copies = []
    for number, (piece, at, t, row, count) in enumerate(blocks(fast, place, rows, model)):
        if fast:
            row = pl.multiple_of(row, rows)
        copy = pltpu.make_async_copy(pieces[piece].at[at], held.at[t, pl.ds(row, count), :], sems.at[number])
        copy.start()
        copies.append(copy)
    return copies


def store_grads(fast, place, held, outs, sems, rows, model):
    copies = []
    for number, (piece, at, t, row, count) in enumerate(blocks(fast, place, rows, model)):
        if fast:
            row = pl.multiple_of(row, rows)
            target = outs[piece // 2].at[(piece % 2,) + at]
        else:
            target = outs[0].at[at]
        copy = pltpu.make_async_copy(held.at[t, pl.ds(row, count), :], target, sems.at[number])
        copy.start()
        copies.append(copy)
    for copy in copies:
        copy.wait()


def n_blocks(fast):
    return 32 if fast else 4


def grad_shapes(fast, rows, model, columns):
    if fast:
        return (jax.ShapeDtypeStruct((2, 2, 4, rows, columns), BF16),) * 2
    return (jax.ShapeDtypeStruct((4, model, columns), BF16),)


SWAP = [(0, 1), (1, 0)]


def over(axis, data):
    return lax.ppermute(data, axis, SWAP)


def over_z(data, k):
    return lax.ppermute(data, "z", [(i, i ^ k) for i in range(4)])


def gather(fast, shard):
    if not fast:
        flat = lax.all_gather(shard, ("z", "x"), axis=0, tiled=True)
        return (lax.all_gather(flat, ("y", "c"), axis=0, tiled=False),)
    line = jnp.stack([shard] + [over_z(shard, k) for k in (1, 2, 3)])
    plane = jnp.stack([line, over("y", line)])
    far = over("x", plane)
    return (plane, far, over("c", plane), over("c", far))


def reduce_grads(fast, outs):
    if not fast:
        mine = lax.psum_scatter(outs[0], ("y", "c"), scatter_dimension=0, tiled=False)
        return lax.psum_scatter(mine, ("z", "x"), scatter_dimension=0, tiled=True).astype(F32)
    keep, send = outs
    terms = [keep, over("c", send)]

    def total(items):
        return functools.reduce(jnp.add, [item.astype(F32) for item in items])

    got = over("x", total([term[1] for term in terms]).astype(BF16))
    terms = [term[0] for term in terms] + [got]
    got = over("y", total([term[1] for term in terms]).astype(BF16))
    terms = [term[0] for term in terms] + [got]
    got = [over_z(total([term[k] for term in terms]).astype(BF16), k) for k in (1, 2, 3)]
    return total([term[0] for term in terms] + got)


def turn(field, first):
    width = field.shape[-1]
    return jnp.where(first, pltpu.roll(field, width - HDIM // 2, 1), pltpu.roll(field, HDIM // 2, 1))


def first_half(shape):
    return lax.broadcasted_iota(jnp.int32, shape, 1) % HDIM < HDIM // 2


def qkv_kernel(fast, n_pieces, place, x_own, x_recv, cosine, sine, *refs):
    pieces = refs[:n_pieces]
    q, k, v, gains, held, sems = refs[n_pieces:]
    rows, model = x_own.shape
    per = held.shape[1] // 8 if fast else held.shape[1]
    for copy in load_weights(fast, place, pieces, held, sems, per, model):
        copy.wait()
    gains[...] = jnp.transpose(held[0, :, 512:640].astype(F32))[64:72, :]
    side = place[2]
    first = first_half((rows, 256))
    inside = lax.broadcasted_iota(jnp.int32, (rows, 256), 1) < 192
    for x, half in ((x_own, side), (x_recv, 1 - side)):
        at = pl.ds(pl.multiple_of(half * rows, rows), rows)

        def one(t, carry, x=x, at=at):
            made = dotf(x[...], held[t])
            u = made[:, 0:256]
            q[t, at, :] = ((u * cosine[at, :] + turn(u, first) * sine[at, :]).astype(BF16) * 0.125).astype(BF16)
            u = made[:, 384:640]
            k[t, at, :] = (u * cosine[at, :] + turn(u, first) * sine[at, :]).astype(BF16)
            u = pltpu.roll(made[:, 128:384], 192, 1)
            v[t, at, :] = jnp.where(inside, u, 0.0).astype(BF16)
            return carry

        lax.fori_loop(0, 4, one, 0)


def project(fast, place, x_own, x_recv, cosine, sine, pieces):
    rows, model = x_own.shape
    field = jax.ShapeDtypeStruct((4, 2 * rows, 256), BF16)
    return pl.pallas_call(
        functools.partial(qkv_kernel, fast, len(pieces)),
        out_shape=(field,) * 3 + (jax.ShapeDtypeStruct((8, model), F32),),
        in_specs=[whole(space=pltpu.SMEM)] + [whole()] * 4 + [whole(space=pl.ANY)] * len(pieces),
        out_specs=(whole(),) * 4,
        scratch_shapes=[pltpu.VMEM((4, model, 640), BF16), pltpu.SemaphoreType.DMA((n_blocks(fast),))],
        compiler_params=params(),
        name="project_qkv",
    )(place, x_own, x_recv, cosine, sine, *pieces)


class Layout:
    def __init__(self, rows, prompt, step):
        self.rows = rows
        self.prompt = prompt
        self.step = step
        self.pair = 2 * step
        self.cont_blocks = (rows - prompt) // (4 * step)
        self.width = 8 * step


def pair_rows(ref, lay, start):
    return (ref[pl.ds(start, lay.pair), :], ref[pl.ds(lay.rows + start, lay.pair), :])


def pair_start(lay, block, pair):
    return pl.multiple_of(lay.prompt + (2 * block + pair) * lay.pair, lay.pair)


def cont_query(ref, lay, block):
    parts = []
    for pair in range(2):
        parts += pair_rows(ref, lay, pair_start(lay, block, pair))
    return jnp.concatenate(parts, 0)


def cont_keys(own, other, lay, block, pair):
    start = pair_start(lay, block, pair)
    return jnp.concatenate(pair_rows(own, lay, start) + pair_rows(other, lay, start), 0)


def causal(count):
    key = lax.broadcasted_iota(jnp.int32, (count, count), 0)
    row = lax.broadcasted_iota(jnp.int32, (count, count), 1)
    return jnp.where(key <= row, 0.0, NEGATIVE)


def prompt_segments(lay, inner):
    low, high = 0, lay.rows
    if inner:
        return [[(1, low, 0), (0, low, 1)], [(1, low, 0), (0, low, 0), (0, high, 1)]]
    return [[(0, low, 1)], [(0, low, 0), (1, low, 0), (1, high, 0), (0, high, 1)]]


def shared_segments(lay):
    return [(0, 0), (0, lay.rows), (1, 0), (1, lay.rows)]


def attend_kernel(lay, place, q_ref, ko, vo, kp, vp, own_mask, mixed, lse):
    inner = place[2] != place[3]
    q, keys, values, out = q_ref.at[0], (ko.at[0], kp.at[0]), (vo.at[0], vp.at[0]), mixed.at[0]
    count = lay.prompt
    lane = lax.broadcasted_iota(jnp.int32, (1, 256), 1) // HDIM
    out[...] = jnp.zeros_like(out)

    def soften(scores):
        highest = functools.reduce(jnp.maximum, [jnp.max(s, 0, keepdims=True) for s in scores])
        raised = [jnp.exp(s - highest) for s in scores]
        total = functools.reduce(jnp.add, [jnp.sum(r, 0, keepdims=True) for r in raised])
        inverse = 1.0 / total
        return [(r * inverse).astype(BF16) for r in raised], highest + jnp.log(total)

    def head(j, carry):
        chosen = lane == j

        def pick(block):
            return jnp.where(chosen, block, jnp.zeros_like(block))

        def add(at, made):
            out[at, :] = out[at, :] + pick(made).astype(BF16)

        def prompt_block(number, segments):
            at = pl.ds(number * lay.rows, count)
            query = pick(q[at, :])
            scores = []
            for other, start, masked in segments:
                s = dotf(keys[other][pl.ds(start, count), :], query, LAST)
                scores.append(s + causal(count) if masked else s)
            low, kept = soften(scores)
            lse[0, pl.ds(j, 1), number * count : (number + 1) * count] = kept
            made = functools.reduce(
                jnp.add,
                [dotf(w, values[o][pl.ds(start, count), :], FIRST) for w, (o, start, _) in zip(low, segments)],
            )
            add(at, made)

        for kind in (False, True):

            @pl.when(inner == kind)
            def _(kind=kind):
                for number, segments in enumerate(prompt_segments(lay, kind)):
                    prompt_block(number, segments)

        def cont_block(block, carry):
            query = pick(cont_query(q, lay, block))
            scores = [dotf(keys[o][pl.ds(start, count), :], query, LAST) for o, start in shared_segments(lay)]
            own = []
            half = lay.width // 2
            for pair in range(2):
                rows = query[pair * half : (pair + 1) * half, :]
                own.append(dotf(cont_keys(keys[0], keys[1], lay, block, pair), rows, LAST) + own_mask[...])
            scores.append(jnp.concatenate(own, 1))
            low, kept = soften(scores)
            lse[0, pl.ds(j, 1), pl.ds(pl.multiple_of(2 * count + block * lay.width, 128), lay.width)] = kept
            made = functools.reduce(
                jnp.add,
                [dotf(w, values[o][pl.ds(start, count), :], FIRST) for w, (o, start) in zip(low, shared_segments(lay))],
            )
            for pair in range(2):
                seen = cont_keys(values[0], values[1], lay, block, pair)
                part = made[pair * half : (pair + 1) * half, :] + dotf(
                    low[-1][:, pair * half : (pair + 1) * half], seen, FIRST
                )
                start = pair_start(lay, block, pair)
                add(pl.ds(start, lay.pair), part[: lay.pair, :])
                add(pl.ds(lay.rows + start, lay.pair), part[lay.pair :, :])
            return carry

        lax.fori_loop(0, lay.cont_blocks, cont_block, 0)
        return carry

    lax.fori_loop(0, 3, head, 0)


def attend(lay, place, q, ko, vo, kp, vp, own_mask):
    total = q.shape[1]
    field = pl.BlockSpec((1, total, 256), lambda t, place: (t, 0, 0))
    return pl.pallas_call(
        functools.partial(attend_kernel, lay),
        out_shape=(jax.ShapeDtypeStruct(q.shape, BF16), jax.ShapeDtypeStruct((4, 8, total), F32)),
        grid_spec=pltpu.PrefetchScalarGridSpec(
            num_scalar_prefetch=1,
            grid=(4,),
            in_specs=[field] * 5 + [pl.BlockSpec(own_mask.shape, lambda t, place: (0, 0))],
            out_specs=(field, pl.BlockSpec((1, 8, total), lambda t, place: (t, 0, 0))),
        ),
        compiler_params=params(),
        name="attend",
    )(place, q, ko, vo, kp, vp, own_mask)


def attend_back_kernel(
    lay, place, q_ref, ko, vo, kp, vp, mixed, up_ref, lse, own_mask, dq_ref, dko, dvo, dkp, dvp, kacc, vacc
):
    inner = place[2] != place[3]
    q, keys, values, upstream, dq = q_ref.at[0], (ko.at[0], kp.at[0]), (vo.at[0], vp.at[0]), up_ref.at[0], dq_ref.at[0]
    result = mixed.at[0]
    count = lay.prompt
    lane = lax.broadcasted_iota(jnp.int32, (1, 256), 1) // HDIM
    kacc[...] = jnp.zeros_like(kacc)
    vacc[...] = jnp.zeros_like(vacc)
    dq[...] = jnp.zeros_like(dq)

    def head(j, carry):
        chosen = lane == j
        marked = jnp.where(lax.broadcasted_iota(jnp.int32, (8, 256), 1) // HDIM == j, 1.0, 0.0)

        def pick(block):
            return jnp.where(chosen, block, jnp.zeros_like(block))

        def spread(grads, made):
            product = grads.astype(F32) * made.astype(F32)
            return lax.dot_general(
                marked, product, (LAST, ((), ())), precision=lax.Precision.HIGHEST, preferred_element_type=F32
            )[0:1, :]

        def back(key, value, query, grads, mask, log_total, delta):
            s = dotf(key, query, LAST)
            if mask is not None:
                s = s + mask
            share = jnp.exp(s - log_total)
            d = share * (dotf(value, grads, LAST) - delta)
            return share.astype(BF16), d.astype(BF16)

        def gather_block(number, at, segments):
            query, grads = pick(q[at, :]), pick(upstream[at, :])
            log_total = lse[0, pl.ds(j, 1), number * count : (number + 1) * count]
            delta = spread(grads, result[at, :])
            total = None
            for other, start, masked in segments:
                spot = pl.ds(start, count)
                key = keys[other][spot, :]
                share, d = back(
                    key, values[other][spot, :], query, grads, causal(count) if masked else None, log_total, delta
                )
                vacc[other, spot, :] += dotf(share, grads)
                kacc[other, spot, :] += dotf(d, query)
                made = dotf(d, key, FIRST)
                total = made if total is None else total + made
            dq[at, :] = dq[at, :] + pick(total * 0.125).astype(BF16)

        for kind in (False, True):

            @pl.when(inner == kind)
            def _(kind=kind):
                for number, segments in enumerate(prompt_segments(lay, kind)):
                    gather_block(number, pl.ds(number * lay.rows, count), segments)

        def cont_block(block, carry):
            query, grads = pick(cont_query(q, lay, block)), pick(cont_query(upstream, lay, block))
            at = pl.ds(pl.multiple_of(2 * count + block * lay.width, 128), lay.width)
            log_total = lse[0, pl.ds(j, 1), at]
            delta = spread(grads, cont_query(result, lay, block))
            total = jnp.zeros((lay.width, 256), F32)
            for other, start in shared_segments(lay):
                spot = pl.ds(start, count)
                key = keys[other][spot, :]
                share, d = back(key, values[other][spot, :], query, grads, None, log_total, delta)
                vacc[other, spot, :] += dotf(share, grads)
                kacc[other, spot, :] += dotf(d, query)
                total = total + dotf(d, key, FIRST)
            half = lay.width // 2
            for pair in range(2):
                cut = slice(pair * half, (pair + 1) * half)
                key = cont_keys(keys[0], keys[1], lay, block, pair)
                value = cont_keys(values[0], values[1], lay, block, pair)
                share, d = back(
                    key, value, query[cut, :], grads[cut, :], own_mask[...], log_total[:, cut], delta[:, cut]
                )
                dv = dotf(share, grads[cut, :])
                dk = dotf(d, query[cut, :])
                start = pair_start(lay, block, pair)
                for part in range(4):
                    spot = pl.ds((part % 2) * lay.rows + start, lay.pair)
                    piece = slice(part * lay.pair, (part + 1) * lay.pair)
                    vacc[part // 2, spot, :] += dv[piece, :]
                    kacc[part // 2, spot, :] += dk[piece, :]
                made = (total[cut, :] + dotf(d, key, FIRST)) * 0.125
                for part in range(2):
                    spot = pl.ds(part * lay.rows + start, lay.pair)
                    piece = slice(part * lay.pair, (part + 1) * lay.pair)
                    dq[spot, :] = dq[spot, :] + pick(made[piece, :]).astype(BF16)
            return carry

        lax.fori_loop(0, lay.cont_blocks, cont_block, 0)
        return carry

    lax.fori_loop(0, 3, head, 0)
    dko[0] = kacc[0].astype(BF16)
    dkp[0] = kacc[1].astype(BF16)
    dvo[0] = vacc[0].astype(BF16)
    dvp[0] = vacc[1].astype(BF16)


def attend_back(lay, place, q, ko, vo, kp, vp, mixed, upstream, lse, own_mask):
    total = q.shape[1]
    field = pl.BlockSpec((1, total, 256), lambda t, place: (t, 0, 0))
    shape = jax.ShapeDtypeStruct(q.shape, BF16)
    return pl.pallas_call(
        functools.partial(attend_back_kernel, lay),
        out_shape=(shape,) * 5,
        grid_spec=pltpu.PrefetchScalarGridSpec(
            num_scalar_prefetch=1,
            grid=(4,),
            in_specs=[field] * 7
            + [
                pl.BlockSpec((1, 8, total), lambda t, place: (t, 0, 0)),
                pl.BlockSpec(own_mask.shape, lambda t, place: (0, 0)),
            ],
            out_specs=(field,) * 5,
            scratch_shapes=[pltpu.VMEM((2, total, 256), F32)] * 2,
        ),
        compiler_params=params(),
        name="attend_back",
    )(place, q, ko, vo, kp, vp, mixed, upstream, lse, own_mask)


def middle_kernel(fast, n_pieces, n_grads, hid, place, mixed, xo, xr, dyo, dyr, gains, *refs):
    pieces = refs[:n_pieces]
    out_own, out_send, dhp, dmixed = refs[n_pieces : n_pieces + 4]
    grads = refs[n_pieces + 4 : n_pieces + 4 + n_grads]
    held, acc, gate_s, up_s, hid_s, gain_acc, sems = refs[n_pieces + 4 + n_grads :]
    step = pl.program_id(0)
    last = pl.num_programs(0) - 1
    model = held.shape[1]
    per = model // 8 if fast else model
    G, U, D, O = slice(0, hid), slice(hid, 2 * hid), slice(2 * hid, 3 * hid), slice(3 * hid, 3 * hid + 256)

    @pl.when(step == 0)
    def _():
        copies = load_weights(fast, place, pieces, held, sems, per, model)
        acc[...] = jnp.zeros_like(acc)
        gain_acc[...] = jnp.zeros_like(gain_acc)
        for copy in copies:
            copy.wait()

    own = step < pl.num_programs(0) // 2
    x = jnp.where(own, xo[...], xr[...]).astype(F32)
    dy = jnp.where(own, dyo[...], dyr[...]).astype(F32)
    gain_a = gains[0:1, :]
    gain_f = gains[1:2, :]
    att = dotf(mixed[0], held[0, :, O], LAST)
    for t in range(1, 4):
        att = att + dotf(mixed[t], held[t, :, O], LAST)
    pre = x + att
    scale1 = lax.rsqrt(jnp.mean(pre * pre, -1, keepdims=True) + EPSILON)
    norm1 = pre * scale1
    normed = norm1 * gain_a
    low = normed.astype(BF16)

    def forward(t, fed):
        gate = dotf(low, held[t, :, G])
        up = dotf(low, held[t, :, U])
        hidden = (gate * jax.nn.sigmoid(gate) * up).astype(BF16)
        gate_s[t] = gate
        up_s[t] = up
        hid_s[t] = hidden
        return fed + dotf(hidden, held[t, :, D], LAST)

    resid = lax.fori_loop(0, 4, forward, normed)
    scale2 = lax.rsqrt(jnp.mean(resid * resid, -1, keepdims=True) + EPSILON)
    norm2 = resid * scale2
    result = (norm2 * gain_f).astype(BF16)

    @pl.when(own)
    def _():
        out_own[...] = result

    @pl.when(jnp.logical_not(own))
    def _():
        out_send[...] = result

    gain_acc[1:2, :] += jnp.sum(dy * norm2, 0, keepdims=True)
    e2 = dy * gain_f
    d_resid = scale2 * (e2 - norm2 * jnp.mean(e2 * norm2, -1, keepdims=True))
    d_fed = d_resid.astype(BF16)
    d_fed_t = jnp.transpose(d_fed)
    low_t = jnp.transpose(low)

    def backward(t, d_normed):
        gate, up, hidden = gate_s[t], up_s[t], hid_s[t]
        d_hidden = dotf(d_fed, held[t, :, D])
        sig = jax.nn.sigmoid(gate)
        d_gate = (d_hidden * up * sig * (1.0 + gate * (1.0 - sig))).astype(BF16)
        d_up = (d_hidden * gate * sig).astype(BF16)
        acc[t, :, D] += dotf(d_fed_t, hidden)
        acc[t, :, G] += dotf(low_t, d_gate)
        acc[t, :, U] += dotf(low_t, d_up)
        return d_normed + dotf(d_gate, held[t, :, G], LAST) + dotf(d_up, held[t, :, U], LAST)

    d_normed = lax.fori_loop(0, 4, backward, d_resid)
    gain_acc[0:1, :] += jnp.sum(d_normed * norm1, 0, keepdims=True)
    e1 = d_normed * gain_a
    d_pre = scale1 * (e1 - norm1 * jnp.mean(e1 * norm1, -1, keepdims=True))
    dhp[...] = d_pre
    d_att = d_pre.astype(BF16)
    d_att_t = jnp.transpose(d_att)
    for t in range(4):
        acc[t, :, O] += dotf(d_att_t, mixed[t])
        dmixed[t] = dotf(d_att, held[t, :, O]).astype(BF16)

    @pl.when(step == last)
    def _():
        columns = jnp.transpose(jnp.broadcast_to(gain_acc[0:8, :], (8, model)))
        spot = lax.broadcasted_iota(jnp.int32, (model, 128), 1)
        extra = jnp.where(spot == 64, columns[:, 0:1], jnp.where(spot == 65, columns[:, 1:2], 0.0))
        for t in range(4):
            acc[t, :, 3 * hid + 128 : 3 * hid + 256] += extra

            def convert(i, carry, t=t):
                at = pl.ds(pl.multiple_of(i * 96, 96), 96)
                held[t, at, :] = acc[t, at, :].astype(BF16)
                return carry

            lax.fori_loop(0, model // 96, convert, 0)
        store_grads(fast, place, held, grads, sems, per, model)


def middle(fast, place, mixed, xo, xr, dyo, dyr, gains, pieces, hid, block):
    rows, model = xo.shape
    columns = 3 * hid + 256
    halves = rows // block
    steps = 2 * halves
    grads = grad_shapes(fast, model // 8 if fast else model, model, columns)

    def own_at(i, place):
        return (jnp.minimum(i, halves - 1), 0)

    def recv_at(i, place):
        return (jnp.maximum(i - halves, 0), 0)

    def mixed_at(i, place):
        side = jnp.where(i < halves, place[2], 1 - place[2])
        return (0, side * halves + lax.rem(i, halves), 0)

    own_spec, recv_spec = pl.BlockSpec((block, model), own_at), pl.BlockSpec((block, model), recv_at)
    field = pl.BlockSpec((4, block, 256), mixed_at)
    return pl.pallas_call(
        functools.partial(middle_kernel, fast, len(pieces), len(grads), hid),
        out_shape=(
            jax.ShapeDtypeStruct((rows, model), BF16),
            jax.ShapeDtypeStruct((rows, model), BF16),
            jax.ShapeDtypeStruct((2 * rows, model), F32),
            jax.ShapeDtypeStruct(mixed.shape, BF16),
        )
        + grads,
        grid_spec=pltpu.PrefetchScalarGridSpec(
            num_scalar_prefetch=1,
            grid=(steps,),
            in_specs=[field, own_spec, recv_spec, own_spec, recv_spec, pl.BlockSpec((8, model), lambda i, place: (0, 0))]
            + [whole(space=pl.ANY)] * len(pieces),
            out_specs=(own_spec, recv_spec, pl.BlockSpec((block, model), lambda i, place: (i, 0)), field)
            + (whole(space=pl.ANY),) * len(grads),
            scratch_shapes=[
                pltpu.VMEM((4, model, columns), BF16),
                pltpu.VMEM((4, model, columns), F32),
                pltpu.VMEM((4, block, hid), F32),
                pltpu.VMEM((4, block, hid), F32),
                pltpu.VMEM((4, block, hid), BF16),
                pltpu.VMEM((8, model), F32),
                pltpu.SemaphoreType.DMA((n_blocks(fast),)),
            ],
        ),
        compiler_params=params(),
        name="middle",
    )(place, mixed, xo, xr, dyo, dyr, gains, *pieces)


def qkv_back_kernel(
    fast, n_pieces, n_grads, place, x_own, x_recv, cosine, sine, dhp, dq, dko, dvo, dkr, dvr, *refs
):
    pieces = refs[:n_pieces]
    dx_own, dx_send = refs[n_pieces : n_pieces + 2]
    grads = refs[n_pieces + 2 : n_pieces + 2 + n_grads]
    held, acc, sems = refs[n_pieces + 2 + n_grads :]
    rows, model = x_own.shape
    per = model // 8 if fast else model
    copies = load_weights(fast, place, pieces, held, sems, per, model)
    acc[...] = jnp.zeros_like(acc)
    for copy in copies:
        copy.wait()
    side = place[2]
    first = first_half((rows, 256))
    for number, (x, half) in enumerate(((x_own, side), (x_recv, 1 - side))):
        at = pl.ds(pl.multiple_of(half * rows, rows), rows)
        x_t = jnp.transpose(x[...])

        def one(t, dx, at=at, x_t=x_t):
            u = dq[t, at, :].astype(F32)
            query = u * cosine[at, :] - turn(u, first) * sine[at, :]
            u = dko[t, at, :].astype(F32) + dkr[t, at, :].astype(F32)
            key = u * cosine[at, :] - turn(u, first) * sine[at, :]
            value = dvo[t, at, :].astype(F32) + dvr[t, at, :].astype(F32)
            gap = jnp.zeros((rows, 128), F32)
            front = jnp.concatenate([query, gap], 1) + pltpu.roll(jnp.concatenate([value, gap], 1), 192, 1)
            joined = jnp.concatenate([front, key], 1).astype(BF16)
            acc[t] += dotf(x_t, joined)
            return dx + dotf(joined, held[t], LAST)

        dx = lax.fori_loop(0, 4, one, dhp[number * rows : (number + 1) * rows, :])
        if number == 0:
            dx_own[...] = dx
        else:
            dx_send[...] = dx.astype(BF16)
    for t in range(4):

        def convert(i, carry, t=t):
            spot = pl.ds(pl.multiple_of(i * 96, 96), 96)
            held[t, spot, :] = acc[t, spot, :].astype(BF16)
            return carry

        lax.fori_loop(0, model // 96, convert, 0)
    store_grads(fast, place, held, grads, sems, per, model)


def project_back(fast, place, x_own, x_recv, cosine, sine, dhp, dq, dko, dvo, dkr, dvr, pieces):
    rows, model = x_own.shape
    grads = grad_shapes(fast, model // 8 if fast else model, model, 640)
    return pl.pallas_call(
        functools.partial(qkv_back_kernel, fast, len(pieces), len(grads)),
        out_shape=(jax.ShapeDtypeStruct((rows, model), F32), jax.ShapeDtypeStruct((rows, model), BF16)) + grads,
        in_specs=[whole(space=pltpu.SMEM)] + [whole()] * 10 + [whole(space=pl.ANY)] * len(pieces),
        out_specs=(whole(), whole()) + (whole(space=pl.ANY),) * len(grads),
        scratch_shapes=[
            pltpu.VMEM((4, model, 640), BF16),
            pltpu.VMEM((4, model, 640), F32),
            pltpu.SemaphoreType.DMA((n_blocks(fast),)),
        ],
        compiler_params=params(),
        name="project_back",
    )(place, x_own, x_recv, cosine, sine, dhp, dq, dko, dvo, dkr, dvr, *pieces)


def tables(quarters, prompt, step, groups, plen):
    half = HDIM // 2
    frequency = 10000.0 ** (-jnp.arange(half, dtype=F32) / half)
    cosines, sines = [], []
    for quarter in quarters:
        own = (quarter * prompt + jnp.arange(prompt)).astype(F32)
        cont = jnp.tile((plen + quarter * step + jnp.arange(step)).astype(F32), groups)
        angle = jnp.concatenate([own, cont])[:, None] * frequency[None, :]
        cosines.append(jnp.cos(angle))
        sines.append(jnp.sin(angle))
    cosine, sine = jnp.concatenate(cosines), jnp.concatenate(sines)
    pad = jnp.zeros((cosine.shape[0], HDIM), F32)
    return (
        jnp.concatenate([cosine] * 6 + [pad], 1),
        jnp.concatenate([-sine, sine] * 3 + [pad], 1),
    )


def own_continuation_mask(quarters, step):
    offset = jnp.arange(2 * step) % step
    cont = jnp.arange(2 * step) // step
    places = jnp.concatenate([quarter * step + offset for quarter in quarters])
    number = jnp.tile(cont, 4)
    rows = 4 * step
    allowed = (places[:, None] <= places[None, :rows]) & (number[:, None] == number[None, :rows])
    return jnp.where(allowed, 0.0, NEGATIVE).astype(F32)


def on_device(
    fast,
    prompt_tokens,
    continuation_tokens,
    prompt_index,
    attention_gain,
    query_weight,
    key_weight,
    value_weight,
    output_weight,
    feedforward_gain,
    gate_weight,
    up_weight,
    down_weight,
    prompt_cotangent,
    continuation_cotangent,
):
    z, x, y, c = [lax.axis_index(name).astype(jnp.int32) for name in ("z", "x", "y", "c")]
    place = jnp.stack([z, x, y, c])
    prompts, prompt_rows, model = prompt_tokens.shape
    conts, step, _ = continuation_tokens.shape
    groups = conts // prompts
    plen = 4 * prompt_rows
    rows = prompt_rows + groups * step
    lay = Layout(rows, prompt_rows, step)
    shard_rows, columns = query_weight.shape
    hid = gate_weight.shape[1]
    local = 2 * y + c
    other = 2 * y + (1 - c)
    quarters = [jnp.minimum(t, 3 - t) if low else jnp.maximum(t, 3 - t) for t in (local, other) for low in (1, 0)]

    first = jnp.concatenate(
        [
            query_weight,
            value_weight,
            key_weight,
            attention_gain[:, None],
            feedforward_gain[:, None],
            jnp.zeros((shard_rows, 62), BF16),
        ],
        1,
    )
    rest = jnp.concatenate(
        [gate_weight, up_weight, down_weight.T, output_weight.T, jnp.zeros((shard_rows, 64), BF16)], 1
    )
    x_own, x_send, dy_own, dy_send = pack(
        place, prompt_index, prompt_tokens, continuation_tokens, prompt_cotangent, continuation_cotangent
    )

    def swap(data):
        return lax.ppermute(data, ("y", "c"), [(0, 3), (3, 0), (1, 2), (2, 1)])

    x_recv = swap(x_send)
    first_pieces = gather(fast, first)
    dy_recv = swap(dy_send)
    rest_pieces = gather(fast, rest)
    cosine, sine = tables(quarters[:2], prompt_rows, step, groups, plen)
    own_mask = own_continuation_mask(quarters, step)
    q, k, v, gains = project(fast, place, x_own, x_recv, cosine, sine, first_pieces)
    k_other, v_other = over("c", k), over("c", v)
    mixed, lse = attend(lay, place, q, k, v, k_other, v_other, own_mask)
    made = middle(fast, place, mixed, x_own, x_recv, dy_own, dy_recv, gains, rest_pieces, hid, min(256, rows))
    out_own, out_send, dhp, dmixed = made[:4]
    out_recv = swap(out_send)
    rest_grad = reduce_grads(fast, made[4:])
    dq, dk, dv, dk_send, dv_send = attend_back(lay, place, q, k, v, k_other, v_other, mixed, dmixed, lse, own_mask)
    dk_recv, dv_recv = over("c", dk_send), over("c", dv_send)
    made = project_back(
        fast, place, x_own, x_recv, cosine, sine, dhp, dq, dk, dv, dk_recv, dv_recv, first_pieces
    )
    dx_own, dx_send = made[:2]
    dx_recv = swap(dx_send)
    first_grad = reduce_grads(fast, made[2:])
    out_prompt, out_cont = unpack(place, prompt_index, out_own, out_recv, prompt_rows, step, BF16)
    dx_prompt, dx_cont = unpack(place, prompt_index, dx_own, dx_recv, prompt_rows, step, F32)
    start = 3 * hid
    return (
        out_prompt,
        out_cont,
        dx_prompt,
        dx_cont,
        rest_grad[:, start + columns],
        first_grad[:, :columns],
        first_grad[:, 2 * columns : 3 * columns],
        first_grad[:, columns : 2 * columns],
        rest_grad[:, start : start + columns].T,
        rest_grad[:, start + columns + 1],
        rest_grad[:, :hid],
        rest_grad[:, hid : 2 * hid],
        rest_grad[:, 2 * hid : start].T,
    )


def solution(mesh):
    parts = mesh.shape["dp"]
    grid = Mesh(mesh.devices.reshape(parts // 2, 2, 2, 2), ("z", "x", "y", "c"))
    dp, tensor = ("z", "x"), ("y", "c")
    fast = parts == 8
    tokens, columns, rows, vector = P(dp, tensor, None), P(dp, tensor), P(tensor, dp), P(dp)
    in_specs = (
        tokens,
        tokens,
        vector,
        vector,
        columns,
        columns,
        columns,
        rows,
        vector,
        columns,
        columns,
        rows,
        tokens,
        tokens,
    )
    out_specs = (
        tokens,
        tokens,
        tokens,
        tokens,
        vector,
        columns,
        columns,
        columns,
        rows,
        vector,
        columns,
        columns,
        rows,
    )
    return jax.shard_map(
        functools.partial(on_device, fast), mesh=grid, in_specs=in_specs, out_specs=out_specs, check_vma=False
    )
```

```python
import functools
import math

import jax
import jax.numpy as jnp
from jax import lax
from jax.experimental import pallas as pl
from jax.experimental.pallas import tpu as pltpu
from jax.sharding import Mesh
from jax.sharding import PartitionSpec as P

HDIM = 64
NEGATIVE = -1e30
EPSILON = 1e-06
BF16 = jnp.bfloat16
F32 = jnp.float32
LAST = ((1,), (1,))
FIRST = ((0,), (0,))
LIMIT = 64000 * 1024


def dotf(left, right, contract=((1,), (0,))):
    return lax.dot_general(left, right, (contract, ((), ())), preferred_element_type=F32)


def whole(shape=None, space=pltpu.VMEM):
    return pl.BlockSpec(memory_space=space)


def params(limit=LIMIT, **more):
    return pltpu.CompilerParams(vmem_limit_bytes=limit, **more)


def fill_order(index_ref, order_ref, count_ref, groups, total):
    count_ref[0] = 0
    count_ref[1] = 0

    def place(number, carry):
        prompt = index_ref[number]
        seen = count_ref[prompt]
        order_ref[prompt * groups + seen] = number
        count_ref[prompt] = seen + 1
        return carry

    lax.fori_loop(0, total, place, 0)


def pack_kernel(groups, place, index, prompt_x, cont_x, x_own, x_send, order, count):
    rows = prompt_x.shape[1]
    step = cont_x.shape[1]
    fill_order(index, order, count, groups, cont_x.shape[0])
    mine = place[2]
    for which, out in ((1 - mine, x_send), (mine, x_own)):
        out[0:rows, :] = prompt_x[which]
        for slot in range(groups):
            out[rows + slot * step : rows + (slot + 1) * step, :] = cont_x[order[which * groups + slot]]


def pack(place, index, prompt_x, cont_x):
    groups = cont_x.shape[0] // prompt_x.shape[0]
    count = prompt_x.shape[1] + groups * cont_x.shape[1]
    rows = jax.ShapeDtypeStruct((count, prompt_x.shape[2]), BF16)
    return pl.pallas_call(
        functools.partial(pack_kernel, groups),
        out_shape=(rows,) * 2,
        in_specs=[whole(space=pltpu.SMEM)] * 2 + [whole()] * 2,
        out_specs=(whole(),) * 2,
        scratch_shapes=[pltpu.SMEM((2 * groups,), jnp.int32), pltpu.SMEM((2,), jnp.int32)],
        compiler_params=params(),
        name="pack_rows",
    )(place, index, prompt_x, cont_x)


def unpack_kernel(groups, place, index, own, back, prompt_out, cont_out, order, count):
    rows = prompt_out.shape[1]
    step = cont_out.shape[1]
    fill_order(index, order, count, groups, cont_out.shape[0])
    mine = place[2]
    for which, source in ((mine, own), (1 - mine, back)):
        prompt_out[which] = source[0:rows, :].astype(prompt_out.dtype)
        for slot in range(groups):
            piece = source[rows + slot * step : rows + (slot + 1) * step, :]
            cont_out[order[which * groups + slot]] = piece.astype(cont_out.dtype)


def unpack(place, index, own, back, rows, step, dtype):
    conts = index.shape[0]
    groups = conts // 2
    width = own.shape[1]
    return pl.pallas_call(
        functools.partial(unpack_kernel, groups),
        out_shape=(
            jax.ShapeDtypeStruct((2, rows, width), dtype),
            jax.ShapeDtypeStruct((conts, step, width), dtype),
        ),
        in_specs=[whole(space=pltpu.SMEM)] * 2 + [whole()] * 2,
        out_specs=(whole(),) * 2,
        scratch_shapes=[pltpu.SMEM((2 * groups,), jnp.int32), pltpu.SMEM((2,), jnp.int32)],
        compiler_params=params(),
        name="unpack_rows",
    )(place, index, own, back)


def blocks(fast, place, rows, model):
    if not fast:
        return [(0, (t,), t, 0, model) for t in range(4)]
    z, x, y, c = place[0], place[1], place[2], place[3]
    found = []
    for dc in range(2):
        for half in range(2):
            for near in range(2):
                for far in range(2):
                    kx, ky = (near, far) if half == 0 else (far, near)
                    for k in range(2):
                        t = 2 * (y ^ ky) + (c ^ dc)
                        row = ((z ^ (2 * half + k)) * 2 + (x ^ kx)) * rows
                        found.append((4 * dc + 2 * half + far, (near, k), t, row, rows))
    return found


def load_weights(fast, place, pieces, held, sems, rows, model):
    copies = []
    for number, (piece, at, t, row, count) in enumerate(blocks(fast, place, rows, model)):
        if fast:
            row = pl.multiple_of(row, rows)
        copy = pltpu.make_async_copy(pieces[piece].at[at], held.at[t, pl.ds(row, count), :], sems.at[number])
        copy.start()
        copies.append(copy)
    return copies


def store_grads(fast, place, held, outs, sems, rows, model):
    copies = []
    for number, (piece, at, t, row, count) in enumerate(blocks(fast, place, rows, model)):
        if fast:
            row = pl.multiple_of(row, rows)
            target = outs[2 * ((piece % 4) // 2) + piece // 4].at[(piece % 2,) + at]
        else:
            target = outs[0].at[at]
        copy = pltpu.make_async_copy(held.at[t, pl.ds(row, count), :], target, sems.at[number])
        copy.start()
        copies.append(copy)
    return copies


def n_blocks(fast):
    return 32 if fast else 4


def n_pieces(fast):
    return 8 if fast else 1


def n_grads(fast):
    return 4 if fast else 1


def grad_shapes(fast, rows, model, columns):
    if fast:
        return (jax.ShapeDtypeStruct((2, 2, 2, rows, columns), BF16),) * 4
    return (jax.ShapeDtypeStruct((4, model, columns), BF16),)


SWAP = [(0, 1), (1, 0)]


def over(axis, data):
    return lax.ppermute(data, axis, SWAP)


def over_z(data, k):
    return lax.ppermute(data, "z", [(i, i ^ k) for i in range(4)])


def after(data, *others):
    return lax.optimization_barrier((data,) + others)[0]


def gather_line(shard):
    return [over_z(shard, k) for k in (1, 2, 3)]


def stack_line(shard, got):
    return (jnp.stack([shard, got[0]]), jnp.stack([got[1], got[2]]))


def gather_near(line):
    return (over("x", line[0]), over("y", line[1]))


def stack_near(line, got):
    return tuple(jnp.stack([a, b]) for a, b in zip(line, got))


def gather_far(plane):
    return (over("y", plane[0]), over("x", plane[1]))


def gather_core(plane, far):
    mine = (plane[0], far[0], plane[1], far[1])
    return mine + tuple(over("c", piece) for piece in mine)


def gather_any(shard):
    flat = lax.all_gather(shard, ("z", "x"), axis=0, tiled=True)
    return (lax.all_gather(flat, ("y", "c"), axis=0, tiled=False),)


def total(items):
    return functools.reduce(jnp.add, [item.astype(F32) for item in items])


class Reduction:
    def __init__(self, grads):
        self.parts = [[grads[2 * half], over("c", grads[2 * half + 1])] for half in range(2)]

    def gate(self, *others):
        self.got = after(self.got, *others)

    def far_sum(self, half):
        return total([p[1] for p in self.parts[half]]).astype(BF16)

    def far(self, sums):
        self.got = [over(axis, s) for axis, s in zip(("y", "x"), sums)]

    def near_sums(self):
        self.from_far = self.got
        return [total([p[0, 1] for p in self.parts[h]] + [self.from_far[h][1]]).astype(BF16) for h in range(2)]

    def near(self, sums):
        self.got = [over(axis, s) for axis, s in zip(("x", "y"), sums)]

    def block(self, half, k):
        return [p[0, 0, k] for p in self.parts[half]] + [self.from_far[half][0, k], self.from_near[half][k]]

    def line_sums(self):
        self.from_near = self.got
        return [total(self.block(half, k)).astype(BF16) for half, k in ((0, 1), (1, 0), (1, 1))]

    def line(self, sums):
        self.got = [over_z(s, k) for k, s in zip((1, 2, 3), sums)]

    def result(self):
        return total(self.block(0, 0) + self.got)


def reduce_any(out):
    mine = lax.psum_scatter(out, ("y", "c"), scatter_dimension=0, tiled=False)
    return lax.psum_scatter(mine, ("z", "x"), scatter_dimension=0, tiled=True).astype(F32)


def left_lanes(rows):
    return lax.broadcasted_iota(jnp.int32, (rows, 128), 1) < HDIM


def flip(tile):
    return pltpu.roll(tile, HDIM, 1)


def tile(data, number):
    return data[:, number * 128 : (number + 1) * 128]


def join_first(even, odd):
    left = left_lanes(even.shape[0])
    e = [tile(even, i) for i in range(5)]
    o = [tile(odd, i) for i in range(5)]
    query = [e[0], jnp.where(left, e[1], o[0]), o[1]]
    key = [e[3], jnp.where(left, e[4], o[3]), o[4]]
    e1, e2, o2, o3 = flip(e[1]), flip(e[2]), flip(o[2]), flip(o[3])
    value = [jnp.where(left, e1, e2), jnp.where(left, e2, o2), jnp.where(left, o2, o3)]
    return query + key + value


def split_first(query, key, value):
    left = left_lanes(query[0].shape[0])
    none = jnp.zeros_like(query[0])
    v = [flip(t) for t in value]
    even = [
        query[0],
        jnp.where(left, query[1], v[0]),
        jnp.where(left, v[0], v[1]),
        key[0],
        jnp.where(left, key[1], none),
    ]
    odd = [
        jnp.where(left, none, query[1]),
        query[2],
        jnp.where(left, v[1], v[2]),
        jnp.where(left, v[2], key[1]),
        key[2],
    ]
    return even, odd


def turn(field, first):
    width = field.shape[-1]
    return jnp.where(first, pltpu.roll(field, width - HDIM // 2, 1), pltpu.roll(field, HDIM // 2, 1))


def first_half(shape):
    return lax.broadcasted_iota(jnp.int32, shape, 1) % HDIM < HDIM // 2


def qkv_kernel(fast, place, x_own, x_recv, cosine, sine, *refs):
    pieces = refs[: n_pieces(fast)]
    q, k, v = refs[-10:-8], refs[-8:-6], refs[-6:-4]
    gains, weights, held, sems = refs[-4:]
    rows, model = x_own.shape
    per = model // 8 if fast else model
    for copy in load_weights(fast, place, pieces, held, sems, per, model):
        copy.wait()
    gains[...] = jnp.transpose(held[0, :, 512:640].astype(F32))[64:72, :]
    side = place[2]
    first = first_half((rows, 128))
    for half in range(2):

        def join(i, carry, half=half):
            at = pl.ds(pl.multiple_of(i * 96, 96), 96)
            for number, made in enumerate(join_first(held[2 * half, at, :], held[2 * half + 1, at, :])):
                weights[half, at, number * 128 : (number + 1) * 128] = made
            return carry

        lax.fori_loop(0, model // 96, join, 0)
        for x, where in ((x_own, side), (x_recv, 1 - side)):
            at = pl.ds(pl.multiple_of(where * rows, rows), rows)
            cos, sin = cosine[at, :], sine[at, :]
            made = dotf(x[...], weights[half])
            for p in range(3):
                lanes = slice(p * 128, (p + 1) * 128)
                u = tile(made, p)
                q[half][at, lanes] = ((u * cos + turn(u, first) * sin).astype(BF16) * 0.125).astype(BF16)
                u = tile(made, 3 + p)
                k[half][at, lanes] = (u * cos + turn(u, first) * sin).astype(BF16)
                v[half][at, lanes] = tile(made, 6 + p).astype(BF16)


def project(fast, place, x_own, x_recv, cosine, sine, pieces):
    rows, model = x_own.shape
    field = jax.ShapeDtypeStruct((2 * rows, 384), BF16)
    made = pl.pallas_call(
        functools.partial(qkv_kernel, fast),
        out_shape=(field,) * 6
        + (jax.ShapeDtypeStruct((8, model), F32), jax.ShapeDtypeStruct((2, model, 1152), BF16)),
        in_specs=[whole(space=pltpu.SMEM)] + [whole()] * 4 + [whole(space=pl.ANY)] * len(pieces),
        out_specs=(whole(),) * 8,
        scratch_shapes=[pltpu.VMEM((4, model, 640), BF16), pltpu.SemaphoreType.DMA((n_blocks(fast),))],
        compiler_params=params(),
        name="project_qkv",
    )(place, x_own, x_recv, cosine, sine, *pieces)
    return made[0:2], made[2:4], made[4:6], made[6], made[7]


class Layout:
    def __init__(self, rows, prompt, step):
        self.rows = rows
        self.prompt = prompt
        self.step = step
        self.pair = 2 * step
        self.cont_blocks = (rows - prompt) // (4 * step)
        self.width = 8 * step


def pair_rows(ref, lay, start):
    return (ref[pl.ds(start, lay.pair), :], ref[pl.ds(lay.rows + start, lay.pair), :])


def pair_start(lay, block, pair):
    return lay.prompt + (2 * block + pair) * lay.pair


def cont_query(ref, lay, block):
    parts = []
    for pair in range(2):
        parts += pair_rows(ref, lay, pair_start(lay, block, pair))
    return jnp.concatenate(parts, 0)


def cont_keys(own, other, lay, block, pair):
    start = pair_start(lay, block, pair)
    return jnp.concatenate(pair_rows(own, lay, start) + pair_rows(other, lay, start), 0)


def causal(count, key_axis):
    key = lax.broadcasted_iota(jnp.int32, (count, count), key_axis)
    row = lax.broadcasted_iota(jnp.int32, (count, count), 1 - key_axis)
    return jnp.where(key <= row, 0.0, NEGATIVE)


def shared_segments(lay):
    return [(0, 0), (0, lay.rows), (1, 0), (1, lay.rows)]


def attend_kernel(lay, place, q_ref, ko, vo, kp, vp, own_mask, mixed, lse, lse_s):
    inner = place[2] != place[3]
    q, keys, values, out = q_ref, (ko, kp), (vo, vp), mixed
    count, width = lay.prompt, lay.width
    half = width // 2
    lane = lax.broadcasted_iota(jnp.int32, (1, 128), 1) // HDIM
    spot = lax.broadcasted_iota(jnp.int32, (1, 128), 1)
    low, high = pl.ds(0, count), pl.ds(lay.rows, count)
    extra = pl.ds(pl.multiple_of(jnp.where(inner, 0, lay.rows), lay.rows), count)
    out[...] = jnp.zeros_like(out)
    lse_s[...] = jnp.zeros_like(lse_s)

    def top(scores):
        return jnp.max(functools.reduce(jnp.maximum, scores), 1, keepdims=True)

    def sums(raised):
        return jnp.sum(functools.reduce(jnp.add, raised), 1, keepdims=True)

    def head(j, carry):
        chosen = lane == j

        def pick(block):
            return jnp.where(chosen, block, jnp.zeros_like(block))

        def finish(at, made, total, highest, number):
            out[at, :] = out[at, :] + pick(made / total).astype(BF16)
            here = pl.ds(number, made.shape[0])
            lse_s[here, :] = jnp.where(spot == j, highest + jnp.log(total), lse_s[here, :])

        q_low, q_high = pick(q[low, :]), pick(q[high, :])
        q_extra = jnp.where(inner, q_low, q_high)
        mask = causal(count, 1)
        s_low = dotf(q_low, keys[0][low, :], LAST) + mask
        s_high = [
            dotf(q_high, keys[0][high, :], LAST) + mask,
            dotf(q_high, keys[0][low, :], LAST),
            dotf(q_high, keys[1][low, :], LAST),
        ]
        s_extra = dotf(q_extra, keys[1][extra, :], LAST)
        s_cont = []
        for block in range(lay.cont_blocks):
            query = pick(cont_query(q, lay, block))
            scores = [dotf(query, keys[o][pl.ds(start, count), :], LAST) for o, start in shared_segments(lay)]
            own = []
            for pair in range(2):
                rows = query[pair * half : (pair + 1) * half, :]
                own.append(dotf(rows, cont_keys(keys[0], keys[1], lay, block, pair), LAST) + own_mask[...])
            s_cont.append(scores + [jnp.concatenate(own, 0)])

        m_low, m_high, m_extra = top([s_low]), top(s_high), top([s_extra])
        m_low = jnp.maximum(m_low, jnp.where(inner, m_extra, NEGATIVE))
        m_high = jnp.maximum(m_high, jnp.where(inner, NEGATIVE, m_extra))
        p_low = jnp.exp(s_low - m_low)
        p_high = [jnp.exp(s - m_high) for s in s_high]
        p_extra = jnp.exp(s_extra - jnp.where(inner, m_low, m_high))
        l_extra = sums([p_extra])
        l_low = sums([p_low]) + jnp.where(inner, l_extra, 0.0)
        l_high = sums(p_high) + jnp.where(inner, 0.0, l_extra)
        o_extra = dotf(p_extra.astype(BF16), values[1][extra, :])
        o_low = dotf(p_low.astype(BF16), values[0][low, :]) + jnp.where(inner, o_extra, 0.0)
        o_high = (
            dotf(p_high[0].astype(BF16), values[0][high, :])
            + dotf(p_high[1].astype(BF16), values[0][low, :])
            + dotf(p_high[2].astype(BF16), values[1][low, :])
            + jnp.where(inner, 0.0, o_extra)
        )
        finish(low, o_low, l_low, m_low, 0)
        finish(high, o_high, l_high, m_high, count)

        for block, scores in enumerate(s_cont):
            highest = top(scores)
            raised = [jnp.exp(s - highest) for s in scores]
            total = sums(raised)
            raised = [r.astype(BF16) for r in raised]
            made = functools.reduce(
                jnp.add, [dotf(r, values[o][pl.ds(start, count), :]) for r, (o, start) in zip(raised, shared_segments(lay))]
            )
            for pair in range(2):
                cut = slice(pair * half, (pair + 1) * half)
                part = made[cut, :] + dotf(raised[-1][cut, :], cont_keys(values[0], values[1], lay, block, pair))
                part = pick(part / total[cut, :]).astype(BF16)
                start = pair_start(lay, block, pair)
                for side in range(2):
                    at = pl.ds(side * lay.rows + start, lay.pair)
                    out[at, :] = out[at, :] + part[side * lay.pair : (side + 1) * lay.pair, :]
            here = pl.ds(2 * count + block * width, width)
            lse_s[here, :] = jnp.where(spot == j, highest + jnp.log(total), lse_s[here, :])
        return carry

    lax.fori_loop(0, 2, head, 0)
    lse[0] = jnp.transpose(lse_s[...])[0:8, :]


def attend(lay, place, q, ko, vo, kp, vp, own_mask):
    total = q.shape[0]
    field = pl.BlockSpec((total, 128), lambda p, place: (0, p))
    return pl.pallas_call(
        functools.partial(attend_kernel, lay),
        out_shape=(jax.ShapeDtypeStruct(q.shape, BF16), jax.ShapeDtypeStruct((3, 8, total), F32)),
        grid_spec=pltpu.PrefetchScalarGridSpec(
            num_scalar_prefetch=1,
            grid=(3,),
            in_specs=[field] * 5 + [pl.BlockSpec(own_mask.shape, lambda p, place: (0, 0))],
            out_specs=(field, pl.BlockSpec((1, 8, total), lambda p, place: (p, 0, 0))),
            scratch_shapes=[pltpu.VMEM((total, 128), F32)],
        ),
        compiler_params=params(),
        name="attend",
    )(place, q, ko, vo, kp, vp, own_mask)


def attend_back_kernel(
    lay, place, q_ref, ko, vo, kp, vp, mixed, up_ref, lse, own_mask, dq, dko, dvo, dkp, dvp, kacc, vacc, qacc, delta_s
):
    inner = place[2] != place[3]
    q, keys, values, upstream, result = q_ref, (ko, kp), (vo, vp), up_ref, mixed
    count, width = lay.prompt, lay.width
    half = width // 2
    lane = lax.broadcasted_iota(jnp.int32, (1, 128), 1) // HDIM
    kacc[...] = jnp.zeros_like(kacc)
    vacc[...] = jnp.zeros_like(vacc)
    qacc[...] = jnp.zeros_like(qacc)
    low, high = pl.ds(0, count), pl.ds(lay.rows, count)
    shift = jnp.where(inner, 0, 1)
    extra = pl.ds(pl.multiple_of(shift * lay.rows, lay.rows), count)
    either = pl.ds(pl.multiple_of(shift * count, count), count)

    def cont_rows(ref):
        return jnp.concatenate([cont_query(ref, lay, block) for block in range(lay.cont_blocks)], 0)

    def product(rows):
        return rows(upstream).astype(F32) * rows(result).astype(F32)

    heads = jnp.where(
        lax.broadcasted_iota(jnp.int32, (8, 128), 1) // HDIM == lax.broadcasted_iota(jnp.int32, (8, 128), 0), 1.0, 0.0
    ).astype(BF16)
    for at, rows in (
        (slice(0, count), lambda ref: ref[low, :]),
        (slice(count, 2 * count), lambda ref: ref[high, :]),
        (slice(2 * count, 2 * count + lay.cont_blocks * width), cont_rows),
    ):
        made = product(rows)
        coarse = made.astype(BF16)
        fine = (made - coarse.astype(F32)).astype(BF16)
        delta_s[:, at] = dotf(heads, coarse, LAST) + dotf(heads, fine, LAST)

    def head(j, carry):
        chosen = lane == j
        me = pl.ds(j, 1)

        def pick(block):
            return jnp.where(chosen, block, jnp.zeros_like(block))

        def back(key, value, query, grads, mask, log_total, delta):
            s = dotf(key, query, LAST)
            if mask is not None:
                s = s + mask
            share = jnp.exp(s - log_total)
            d = (share * (dotf(value, grads, LAST) - delta)).astype(BF16)
            return dotf(share.astype(BF16), grads), dotf(d, query), dotf(d, key, FIRST)

        def put(other, at, dv, dk):
            vacc[other, at, :] += dv
            kacc[other, at, :] += dk

        query, grads = pick(cont_rows(q)), pick(cont_rows(upstream))
        at = pl.ds(2 * count, lay.cont_blocks * width)
        log_total, delta = lse[0, me, at], delta_s[me, at]
        shared = shared_segments(lay)
        key = jnp.concatenate([keys[o][pl.ds(start, count), :] for o, start in shared], 0)
        value = jnp.concatenate([values[o][pl.ds(start, count), :] for o, start in shared], 0)
        dv, dk, total = back(key, value, query, grads, None, log_total, delta)
        for number, (other, start) in enumerate(shared):
            piece = slice(number * count, (number + 1) * count)
            put(other, pl.ds(start, count), dv[piece, :], dk[piece, :])
        for number in range(2 * lay.cont_blocks):
            block, pair = number // 2, number % 2
            cut = slice(number * half, (number + 1) * half)
            dv, dk, made = back(
                cont_keys(keys[0], keys[1], lay, block, pair),
                cont_keys(values[0], values[1], lay, block, pair),
                query[cut, :],
                grads[cut, :],
                own_mask[...],
                log_total[:, cut],
                delta[:, cut],
            )
            start = pair_start(lay, block, pair)
            for part in range(4):
                piece = slice(part * lay.pair, (part + 1) * lay.pair)
                put(part // 2, pl.ds((part % 2) * lay.rows + start, lay.pair), dv[piece, :], dk[piece, :])
            made = pick(total[cut, :] + made)
            for part in range(2):
                spot = pl.ds(part * lay.rows + start, lay.pair)
                qacc[spot, :] += made[part * lay.pair : (part + 1) * lay.pair, :]
        mask = causal(count, 0)
        at = pl.ds(count, count)
        query, grads, log_total, delta = pick(q[high, :]), pick(upstream[high, :]), lse[0, me, at], delta_s[me, at]
        seen = ((0, high), (0, low), (1, low))
        key = jnp.concatenate([keys[o][spot, :] for o, spot in seen], 0)
        value = jnp.concatenate([values[o][spot, :] for o, spot in seen], 0)
        tall = jnp.concatenate([mask, jnp.zeros((2 * count, count), F32)], 0)
        dv, dk, made = back(key, value, query, grads, tall, log_total, delta)
        for number, (other, spot) in enumerate(seen):
            piece = slice(number * count, (number + 1) * count)
            put(other, spot, dv[piece, :], dk[piece, :])
        qacc[high, :] += pick(made)
        at = pl.ds(0, count)
        dv, dk, made = back(
            keys[0][low, :],
            values[0][low, :],
            pick(q[low, :]),
            pick(upstream[low, :]),
            mask,
            lse[0, me, at],
            delta_s[me, at],
        )
        put(0, low, dv, dk)
        qacc[low, :] += pick(made)
        dv, dk, made = back(
            keys[1][extra, :],
            values[1][extra, :],
            pick(q[extra, :]),
            pick(upstream[extra, :]),
            None,
            lse[0, me, either],
            delta_s[me, either],
        )
        put(1, extra, dv, dk)
        qacc[extra, :] += pick(made)
        return carry

    lax.fori_loop(0, 2, head, 0)
    dq[...] = (qacc[...] * 0.125).astype(BF16)
    dko[...] = kacc[0].astype(BF16)
    dkp[...] = kacc[1].astype(BF16)
    dvo[...] = vacc[0].astype(BF16)
    dvp[...] = vacc[1].astype(BF16)


def attend_back(lay, place, q, ko, vo, kp, vp, mixed, upstream, lse, own_mask):
    total = q.shape[0]
    field = pl.BlockSpec((total, 128), lambda p, place: (0, p))
    return pl.pallas_call(
        functools.partial(attend_back_kernel, lay),
        out_shape=(jax.ShapeDtypeStruct(q.shape, BF16),) * 5,
        grid_spec=pltpu.PrefetchScalarGridSpec(
            num_scalar_prefetch=1,
            grid=(3,),
            in_specs=[field] * 7
            + [
                pl.BlockSpec((1, 8, total), lambda p, place: (p, 0, 0)),
                pl.BlockSpec(own_mask.shape, lambda p, place: (0, 0)),
            ],
            out_specs=(field,) * 5,
            scratch_shapes=[
                pltpu.VMEM((2, total, 128), F32),
                pltpu.VMEM((2, total, 128), F32),
                pltpu.VMEM((total, 128), F32),
                pltpu.VMEM((8, total), F32),
            ],
        ),
        compiler_params=params(),
        name="attend_back",
    )(place, q, ko, vo, kp, vp, mixed, upstream, lse, own_mask)


def middle_kernel(fast, hid, place, mixed_a, mixed_b, xo, xr, dyo, dyr, gains, *refs):
    count = n_pieces(fast)
    pieces, refs = refs[:count], refs[count:]
    (out_own, out_send, dhp), dmixed, refs = refs[:3], refs[3:5], refs[5:]
    count = n_grads(fast)
    grads, refs = refs[:count], refs[count:]
    held, wide_o, gate_s, up_s, hid_s, dgate_s, dup_s, low_t, fed_t, att_t, gain_acc, sems = refs
    mixed = (mixed_a, mixed_b)
    step = pl.program_id(0)
    model = held.shape[1]
    rows = xo.shape[0]
    per = model // 8 if fast else model
    G, U, D, O = slice(0, hid), slice(hid, 2 * hid), slice(2 * hid, 3 * hid), 3 * hid
    side = jnp.where(step == 0, place[2], 1 - place[2])
    here = pl.ds(pl.multiple_of(side * rows, rows), rows)
    left = left_lanes(model)

    @pl.when(step == 0)
    def _():
        copies = load_weights(fast, place, pieces, held, sems, per, model)
        gain_acc[...] = jnp.zeros_like(gain_acc)
        for copy in copies:
            copy.wait()
        for half in range(2):
            even, odd = held.at[2 * half], held.at[2 * half + 1]
            wide_o[half, :, 0:128] = even[:, O : O + 128]
            wide_o[half, :, 128:256] = jnp.where(left, even[:, O + 128 : O + 256], odd[:, O : O + 128])
            wide_o[half, :, 256:384] = odd[:, O + 128 : O + 256]

    own = step == 0
    gain_a = gains[0:1, :]
    gain_f = gains[1:2, :]
    pre = jnp.where(own, xo[...], xr[...]).astype(F32)
    for half in range(2):
        pre = pre + dotf(mixed[half][here, :], wide_o[half], LAST)
    scale1 = lax.rsqrt(jnp.mean(pre * pre, -1, keepdims=True) + EPSILON)
    norm1 = pre * scale1
    normed = norm1 * gain_a
    low = normed.astype(BF16)
    low_t[step] = jnp.transpose(low)
    spot = pl.ds(pl.multiple_of(step * rows, rows), rows)

    def forward(t, fed):
        gate = dotf(low, held[t, :, G])
        up = dotf(low, held[t, :, U])
        hidden = (gate * jax.nn.sigmoid(gate) * up).astype(BF16)
        gate_s[t] = gate
        up_s[t] = up
        hid_s[t, spot, :] = hidden
        return fed + dotf(hidden, held[t, :, D], LAST)

    resid = lax.fori_loop(0, 4, forward, normed)
    scale2 = lax.rsqrt(jnp.mean(resid * resid, -1, keepdims=True) + EPSILON)
    norm2 = resid * scale2
    result = (norm2 * gain_f).astype(BF16)

    @pl.when(own)
    def _():
        out_own[...] = result

    @pl.when(jnp.logical_not(own))
    def _():
        out_send[...] = result

    dy = jnp.where(own, dyo[...], dyr[...]).astype(F32)
    gain_acc[1:2, :] += jnp.sum(dy * norm2, 0, keepdims=True)
    e2 = dy * gain_f
    d_resid = scale2 * (e2 - norm2 * jnp.mean(e2 * norm2, -1, keepdims=True))
    d_fed = d_resid.astype(BF16)
    fed_t[step] = jnp.transpose(d_fed)

    def backward(t, d_normed):
        gate, up = gate_s[t], up_s[t]
        d_hidden = dotf(d_fed, held[t, :, D])
        sig = jax.nn.sigmoid(gate)
        d_gate = (d_hidden * up * sig * (1.0 + gate * (1.0 - sig))).astype(BF16)
        d_up = (d_hidden * gate * sig).astype(BF16)
        dgate_s[t, spot, :] = d_gate
        dup_s[t, spot, :] = d_up
        return d_normed + dotf(d_gate, held[t, :, G], LAST) + dotf(d_up, held[t, :, U], LAST)

    d_normed = lax.fori_loop(0, 4, backward, d_resid)
    gain_acc[0:1, :] += jnp.sum(d_normed * norm1, 0, keepdims=True)
    e1 = d_normed * gain_a
    d_pre = scale1 * (e1 - norm1 * jnp.mean(e1 * norm1, -1, keepdims=True))
    dhp[...] = d_pre
    d_att = d_pre.astype(BF16)
    att_t[step] = jnp.transpose(d_att)
    for half in range(2):
        dmixed[half][...] = dotf(d_att, wide_o[half]).astype(BF16)

    @pl.when(step == 1)
    def _():
        columns = jnp.transpose(jnp.broadcast_to(gain_acc[0:8, :], (8, model)))
        lane = lax.broadcasted_iota(jnp.int32, (model, 128), 1) % HDIM
        extra = jnp.where(lane == 0, columns[:, 0:1], jnp.where(lane == 1, columns[:, 1:2], 0.0))
        halves = (place[2], 1 - place[2])
        for half in range(2):
            made = None
            for part in range(2):
                at = pl.ds(pl.multiple_of(halves[part] * rows, rows), rows)
                more = dotf(att_t[part], mixed[half][at, :])
                made = more if made is None else made + more
            even, odd = held.at[2 * half], held.at[2 * half + 1]
            even[:, O : O + 128] = tile(made, 0).astype(BF16)
            even[:, O + 128 : O + 256] = jnp.where(left, tile(made, 1), extra).astype(BF16)
            odd[:, O : O + 128] = jnp.where(left, extra, tile(made, 1)).astype(BF16)
            odd[:, O + 128 : O + 256] = tile(made, 2).astype(BF16)

        def weight(r, carry):
            t = 2 * (place[2] ^ (r // 2)) + (place[3] ^ (r % 2)) if fast else r
            for columns, first, second in ((D, fed_t, hid_s), (G, low_t, dgate_s), (U, low_t, dup_s)):
                made = dotf(first[0], second[t, 0:rows, :]) + dotf(first[1], second[t, rows : 2 * rows, :])
                held[t, :, columns] = made.astype(BF16)
            if fast:
                for dc in range(2):

                    @pl.when(r % 2 == dc)
                    def _(dc=dc):
                        send_block(place, r // 2, dc, held, grads, sems, per, True)

            return carry

        lax.fori_loop(0, 4, weight, 0)
        if fast:
            for r in range(4):
                send_block(place, r // 2, r % 2, held, grads, sems, per, False)
        else:
            for copy in store_grads(fast, place, held, grads, sems, per, model):
                copy.wait()


def send_block(place, ky, dc, held, targets, sems, rows, start):
    z, x, y, c = place[0], place[1], place[2], place[3]
    t = 2 * (y ^ ky) + (c ^ dc)
    for kz in range(4):
        for kx in range(2):
            half, k = kz // 2, kz % 2
            far, near = (ky, kx) if half == 0 else (kx, ky)
            row = pl.multiple_of(((z ^ kz) * 2 + (x ^ kx)) * rows, rows)
            number = 16 * dc + 8 * ky + 2 * kz + kx
            copy = pltpu.make_async_copy(
                held.at[t, pl.ds(row, rows), :], targets[2 * half + dc].at[far, near, k], sems.at[number]
            )
            if start:
                copy.start()
            else:
                copy.wait()


def once(shape, index=None):
    return pl.BlockSpec(shape, index or (lambda i, place: (0,) * len(shape)), pipeline_mode=pl.Buffered(1))


def middle(fast, place, mixed, xo, xr, dyo, dyr, gains, pieces, hid):
    rows, model = xo.shape
    columns = 3 * hid + 256
    grads = grad_shapes(fast, model // 8 if fast else model, model, columns)

    def side_at(i, place):
        return (jnp.where(i == 0, place[2], 1 - place[2]), 0)

    half_rows = once((rows, model))
    field = once((2 * rows, 384))
    return pl.pallas_call(
        functools.partial(middle_kernel, fast, hid),
        out_shape=(
            jax.ShapeDtypeStruct((rows, model), BF16),
            jax.ShapeDtypeStruct((rows, model), BF16),
            jax.ShapeDtypeStruct((2 * rows, model), F32),
            jax.ShapeDtypeStruct(mixed[0].shape, BF16),
            jax.ShapeDtypeStruct(mixed[0].shape, BF16),
        )
        + grads,
        grid_spec=pltpu.PrefetchScalarGridSpec(
            num_scalar_prefetch=1,
            grid=(2,),
            in_specs=[field, field] + [half_rows] * 4 + [once((8, model))] + [whole(space=pl.ANY)] * len(pieces),
            out_specs=(
                pl.BlockSpec((rows, model), lambda i, place: (0, 0)),
                pl.BlockSpec((rows, model), lambda i, place: (0, 0)),
                pl.BlockSpec((rows, model), lambda i, place: (i, 0)),
                pl.BlockSpec((rows, 384), side_at),
                pl.BlockSpec((rows, 384), side_at),
            )
            + (whole(space=pl.ANY),) * len(grads),
            scratch_shapes=[
                pltpu.VMEM((4, model, columns), BF16),
                pltpu.VMEM((2, model, 384), BF16),
                pltpu.VMEM((4, rows, hid), F32),
                pltpu.VMEM((4, rows, hid), F32),
                pltpu.VMEM((4, 2 * rows, hid), BF16),
                pltpu.VMEM((4, 2 * rows, hid), BF16),
                pltpu.VMEM((4, 2 * rows, hid), BF16),
                pltpu.VMEM((2, model, rows), BF16),
                pltpu.VMEM((2, model, rows), BF16),
                pltpu.VMEM((2, model, rows), BF16),
                pltpu.VMEM((8, model), F32),
                pltpu.SemaphoreType.DMA((n_blocks(fast),)),
            ],
        ),
        compiler_params=params(),
        name="middle",
    )(place, *mixed, xo, xr, dyo, dyr, gains, *pieces)


def qkv_back_kernel(fast, place, x_own, x_recv, cosine, sine, dhp, weights, *refs):
    dq, dko, dvo, dkr, dvr = [refs[2 * i : 2 * i + 2] for i in range(5)]
    dx_own, dx_send = refs[10:12]
    grads, refs = refs[12 : 12 + n_grads(fast)], refs[12 + n_grads(fast) :]
    held, joined, sems = refs
    rows, model = x_own.shape
    per = model // 8 if fast else model
    side = place[2]
    first = first_half((rows, 128))
    x_t = [jnp.transpose(x[...]) for x in (x_own, x_recv)]
    dx = [dhp[0:rows, :], dhp[rows : 2 * rows, :]]
    for half in range(2):
        for number, where in enumerate((side, 1 - side)):
            at = pl.ds(pl.multiple_of(where * rows, rows), rows)
            cos, sin = cosine[at, :], sine[at, :]
            for p in range(3):
                lanes = slice(p * 128, (p + 1) * 128)
                u = dq[half][at, lanes].astype(F32)
                joined[number, :, p * 128 : (p + 1) * 128] = (u * cos - turn(u, first) * sin).astype(BF16)
                u = dko[half][at, lanes].astype(F32) + dkr[half][at, lanes].astype(F32)
                joined[number, :, 384 + p * 128 : 512 + p * 128] = (u * cos - turn(u, first) * sin).astype(BF16)
                u = dvo[half][at, lanes].astype(F32) + dvr[half][at, lanes].astype(F32)
                joined[number, :, 768 + p * 128 : 896 + p * 128] = u.astype(BF16)
            dx[number] = dx[number] + dotf(joined[number], weights[half], LAST)
        fields = []
        for kind in range(3):
            lanes = slice(kind * 384, (kind + 1) * 384)
            made = (dotf(x_t[0], joined[0, :, lanes]) + dotf(x_t[1], joined[1, :, lanes])).astype(BF16)
            fields.append([tile(made, p) for p in range(3)])
        even, odd = split_first(*fields)
        for p in range(5):
            held[2 * half, :, p * 128 : (p + 1) * 128] = even[p]
            held[2 * half + 1, :, p * 128 : (p + 1) * 128] = odd[p]
    dx_own[...] = dx[0]
    dx_send[...] = dx[1].astype(BF16)
    for copy in store_grads(fast, place, held, grads, sems, per, model):
        copy.wait()


def project_back(fast, place, x_own, x_recv, cosine, sine, dhp, weights, fields):
    rows, model = x_own.shape
    grads = grad_shapes(fast, model // 8 if fast else model, model, 640)
    return pl.pallas_call(
        functools.partial(qkv_back_kernel, fast),
        out_shape=(jax.ShapeDtypeStruct((rows, model), F32), jax.ShapeDtypeStruct((rows, model), BF16)) + grads,
        in_specs=[whole(space=pltpu.SMEM)] + [whole()] * 16,
        out_specs=(whole(), whole()) + (whole(space=pl.ANY),) * len(grads),
        scratch_shapes=[
            pltpu.VMEM((4, model, 640), BF16),
            pltpu.VMEM((2, rows, 1152), BF16),
            pltpu.SemaphoreType.DMA((n_blocks(fast),)),
        ],
        compiler_params=params(),
        name="project_back",
    )(place, x_own, x_recv, cosine, sine, dhp, weights, *fields)


def tables(quarters, prompt, step, groups, plen):
    half = HDIM // 2
    places = []
    for quarter in quarters:
        places.append((quarter * prompt + jnp.arange(prompt)).astype(F32))
        places.append(jnp.tile((plen + quarter * step + jnp.arange(step)).astype(F32), groups))
    lanes = jnp.arange(2 * HDIM)
    frequency = 10000.0 ** (-(lanes % half).astype(F32) / half)
    angle = jnp.concatenate(places)[:, None] * frequency[None, :]
    return jnp.cos(angle), jnp.sin(angle) * jnp.where(lanes % HDIM < half, -1.0, 1.0)[None, :]


def own_continuation_mask(quarters, step):
    offset = jnp.arange(2 * step) % step
    cont = jnp.arange(2 * step) // step
    places = jnp.concatenate([quarter * step + offset for quarter in quarters])
    number = jnp.tile(cont, 4)
    rows = 4 * step
    allowed = (places[:, None] <= places[None, :rows]) & (number[:, None] == number[None, :rows])
    mask = jnp.where(allowed, 0.0, NEGATIVE).astype(F32)
    return mask, mask.T


def on_device(
    fast,
    prompt_tokens,
    continuation_tokens,
    prompt_index,
    attention_gain,
    query_weight,
    key_weight,
    value_weight,
    output_weight,
    feedforward_gain,
    gate_weight,
    up_weight,
    down_weight,
    prompt_cotangent,
    continuation_cotangent,
):
    z, x, y, c = [lax.axis_index(name).astype(jnp.int32) for name in ("z", "x", "y", "c")]
    place = jnp.stack([z, x, y, c])
    prompts, prompt_rows, model = prompt_tokens.shape
    conts, step, _ = continuation_tokens.shape
    groups = conts // prompts
    plen = 4 * prompt_rows
    rows = prompt_rows + groups * step
    lay = Layout(rows, prompt_rows, step)
    shard_rows, columns = query_weight.shape
    hid = gate_weight.shape[1]
    local = 2 * y + c
    other = 2 * y + (1 - c)
    quarters = [jnp.minimum(t, 3 - t) if low else jnp.maximum(t, 3 - t) for t in (local, other) for low in (1, 0)]

    gains = [attention_gain[:, None], feedforward_gain[:, None], jnp.zeros((shard_rows, 62), BF16)]
    first = [query_weight, value_weight, key_weight]
    first = jnp.where(c == 0, jnp.concatenate(first + gains, 1), jnp.concatenate(gains + first, 1))
    wide = [gate_weight, up_weight]
    down, out, gap = down_weight.T, output_weight.T, jnp.zeros((shard_rows, 64), BF16)
    rest = jnp.where(c == 0, jnp.concatenate(wide + [down, out, gap], 1), jnp.concatenate(wide + [down, gap, out], 1))

    def swap(data):
        return lax.ppermute(data, ("y", "c"), [(0, 3), (3, 0), (1, 2), (2, 1)])

    def across(fields):
        return tuple(over("c", field) for field in fields)

    if fast:
        x_own, x_send = pack(place, prompt_index, prompt_tokens, continuation_tokens)
        x_recv = swap(x_send)
        dy_own, dy_send = pack(after(place, x_send), prompt_index, prompt_cotangent, continuation_cotangent)
        first = after(first, dy_send)
        got = gather_line(first)
        line = stack_line(first, after(got, rest))
        got = gather_near(line)
        rest = after(rest, *line)
        rest_got = gather_line(rest)
        dy_recv = swap(after(dy_send, *line))
        cosine, sine = tables(after(tuple(quarters[:2]), *line), prompt_rows, step, groups, plen)
        own_mask, row_mask = own_continuation_mask(after(tuple(quarters), *line), step)
        plane = stack_near(line, after(got, cosine, sine, own_mask, row_mask, x_recv, dy_recv, rest_got[0], rest_got[1]))
        far = gather_far(plane)
        first_pieces = gather_core(plane, far)
        rest_line = stack_line(rest, after(rest_got, *far))
        rest_got = gather_near(rest_line)
        q, k, v, gains, weights = project(
            fast, place, x_own, x_recv, cosine, sine, after(first_pieces, *rest_line)
        )
        k_other, v_other = across(k), across(v)
        rest_plane = stack_near(rest_line, after(rest_got, q[0]))
        rest_far = gather_far(rest_plane)
        mixed, lse = [None, None], [None, None]
        mixed[0], lse[0] = attend(
            lay, place, q[0], k[0], v[0], k_other[0], v_other[0], after(row_mask, *rest_plane)
        )
        mixed[1], lse[1] = attend(
            lay, place, q[1], k[1], v[1], k_other[1], v_other[1], after(row_mask, mixed[0])
        )
        rest_pieces = gather_core(after(rest_plane, mixed[1]), after(rest_far, mixed[1]))
    else:
        x_own, x_send = pack(place, prompt_index, prompt_tokens, continuation_tokens)
        dy_own, dy_send = pack(place, prompt_index, prompt_cotangent, continuation_cotangent)
        x_recv, dy_recv = swap(x_send), swap(dy_send)
        first_pieces, rest_pieces = gather_any(first), gather_any(rest)
        cosine, sine = tables(quarters[:2], prompt_rows, step, groups, plen)
        own_mask, row_mask = own_continuation_mask(quarters, step)
        q, k, v, gains, weights = project(fast, place, x_own, x_recv, cosine, sine, first_pieces)
        k_other, v_other = across(k), across(v)
        made = [
            attend(lay, place, q[i], k[i], v[i], k_other[i], v_other[i], row_mask) for i in range(2)
        ]
        mixed, lse = [m[0] for m in made], [m[1] for m in made]
    made = middle(fast, place, mixed, x_own, x_recv, dy_own, dy_recv, gains, rest_pieces, hid)
    out_own, out_send, dhp = made[:3]
    dmixed, grads = made[3:5], made[5:]

    def back(half, mask):
        return attend_back(
            lay,
            place,
            q[half],
            k[half],
            v[half],
            k_other[half],
            v_other[half],
            mixed[half],
            dmixed[half],
            lse[half],
            mask,
        )

    def collect(made):
        return [[m[i] for m in made] for i in range(3)] + [[over("c", m[i]) for m in made] for i in (3, 4)]

    if fast:
        rest_sum = Reduction(grads)
        sums = [rest_sum.far_sum(0), rest_sum.far_sum(1)]
        rest_sum.far(sums)
        done = [back(0, after(own_mask, *sums))]
        rest_sum.gate(done[0][0])
        sums = rest_sum.near_sums()
        rest_sum.near(sums)
        out_recv = swap(after(out_send, *sums))
        done.append(back(1, after(own_mask, *sums)))
        rest_sum.gate(done[1][0])
        sums = rest_sum.line_sums()
        rest_sum.line(sums)
        fields = sum(collect(done), [])
        made = project_back(fast, place, x_own, x_recv, cosine, sine, after(dhp, *sums), weights, fields)
        dx_own, dx_send = made[:2]
        first_sum = Reduction(made[2:])
        sums = [first_sum.far_sum(0), first_sum.far_sum(1)]
        first_sum.far(sums)
        out_prompt, out_cont = unpack(place, prompt_index, out_own, after(out_recv, *sums), prompt_rows, step, BF16)
        first_sum.gate(out_prompt)
        sums = first_sum.near_sums()
        first_sum.near(sums)
        dx_recv = swap(after(dx_send, *sums))
        rest_sum.gate(*sums)
        rest_grad = rest_sum.result()
        first_sum.gate(rest_grad)
        first_sum.line(first_sum.line_sums())
        first_grad = first_sum.result()
    else:
        out_recv = swap(out_send)
        rest_grad = reduce_any(grads[0])
        fields = sum(collect([back(half, own_mask) for half in range(2)]), [])
        made = project_back(fast, place, x_own, x_recv, cosine, sine, dhp, weights, fields)
        dx_own, dx_send = made[:2]
        dx_recv = swap(dx_send)
        first_grad = reduce_any(made[2])
        out_prompt, out_cont = unpack(place, prompt_index, out_own, out_recv, prompt_rows, step, BF16)
    dx_prompt, dx_cont = unpack(place, prompt_index, dx_own, dx_recv, prompt_rows, step, F32)
    first_grad = jnp.where(c == 0, first_grad[:, : 3 * columns], first_grad[:, 64:])
    start = 3 * hid
    gain_grads = jnp.where(c == 0, rest_grad[:, start + columns : start + columns + 2], rest_grad[:, start : start + 2])
    out_grad = jnp.where(c == 0, rest_grad[:, start : start + columns], rest_grad[:, start + 64 :])
    return (
        out_prompt,
        out_cont,
        dx_prompt,
        dx_cont,
        gain_grads[:, 0],
        first_grad[:, :columns],
        first_grad[:, 2 * columns :],
        first_grad[:, columns : 2 * columns],
        out_grad.T,
        gain_grads[:, 1],
        rest_grad[:, :hid],
        rest_grad[:, hid : 2 * hid],
        rest_grad[:, 2 * hid : start].T,
    )


def solution(mesh):
    parts = mesh.shape["dp"]
    grid = Mesh(mesh.devices.reshape(parts // 2, 2, 2, 2), ("z", "x", "y", "c"))
    dp, tensor = ("z", "x"), ("y", "c")
    fast = parts == 8
    tokens, columns, rows, vector = P(dp, tensor, None), P(dp, tensor), P(tensor, dp), P(dp)
    in_specs = (
        tokens,
        tokens,
        vector,
        vector,
        columns,
        columns,
        columns,
        rows,
        vector,
        columns,
        columns,
        rows,
        tokens,
        tokens,
    )
    out_specs = (
        tokens,
        tokens,
        tokens,
        tokens,
        vector,
        columns,
        columns,
        columns,
        rows,
        vector,
        columns,
        columns,
        rows,
    )
    return jax.shard_map(
        functools.partial(on_device, fast), mesh=grid, in_specs=in_specs, out_specs=out_specs, check_vma=False
    )
```

```python
import functools
import math

import jax
import jax.numpy as jnp
from jax import lax
from jax.experimental import pallas as pl
from jax.experimental.pallas import tpu as pltpu
from jax.sharding import Mesh
from jax.sharding import PartitionSpec as P

HDIM = 64
NEGATIVE = -1e30
EPSILON = 1e-06
BF16 = jnp.bfloat16
F32 = jnp.float32
LAST = ((1,), (1,))
FIRST = ((0,), (0,))
LIMIT = 64000 * 1024


def dotf(left, right, contract=((1,), (0,))):
    return lax.dot_general(left, right, (contract, ((), ())), preferred_element_type=F32)


def whole(shape=None, space=pltpu.VMEM):
    return pl.BlockSpec(memory_space=space)


def params(limit=LIMIT, **more):
    return pltpu.CompilerParams(vmem_limit_bytes=limit, **more)


def fill_order(index_ref, order_ref, count_ref, groups, total):
    count_ref[0] = 0
    count_ref[1] = 0

    def place(number, carry):
        prompt = index_ref[number]
        seen = count_ref[prompt]
        order_ref[prompt * groups + seen] = number
        count_ref[prompt] = seen + 1
        return carry

    lax.fori_loop(0, total, place, 0)


def pack_kernel(groups, place, index, prompt_x, cont_x, x_own, x_send, order, count):
    rows = prompt_x.shape[1]
    step = cont_x.shape[1]
    fill_order(index, order, count, groups, cont_x.shape[0])
    mine = place[2]
    for which, out in ((1 - mine, x_send), (mine, x_own)):
        out[0:rows, :] = prompt_x[which]
        for slot in range(groups):
            out[rows + slot * step : rows + (slot + 1) * step, :] = cont_x[order[which * groups + slot]]


def pack(place, index, prompt_x, cont_x):
    groups = cont_x.shape[0] // prompt_x.shape[0]
    count = prompt_x.shape[1] + groups * cont_x.shape[1]
    rows = jax.ShapeDtypeStruct((count, prompt_x.shape[2]), BF16)
    return pl.pallas_call(
        functools.partial(pack_kernel, groups),
        out_shape=(rows,) * 2,
        in_specs=[whole(space=pltpu.SMEM)] * 2 + [whole()] * 2,
        out_specs=(whole(),) * 2,
        scratch_shapes=[pltpu.SMEM((2 * groups,), jnp.int32), pltpu.SMEM((2,), jnp.int32)],
        compiler_params=params(),
        name="pack_rows",
    )(place, index, prompt_x, cont_x)


def unpack_kernel(groups, place, index, own, back, prompt_out, cont_out, order, count):
    rows = prompt_out.shape[1]
    step = cont_out.shape[1]
    fill_order(index, order, count, groups, cont_out.shape[0])
    mine = place[2]
    for which, source in ((mine, own), (1 - mine, back)):
        prompt_out[which] = source[0:rows, :].astype(prompt_out.dtype)
        for slot in range(groups):
            piece = source[rows + slot * step : rows + (slot + 1) * step, :]
            cont_out[order[which * groups + slot]] = piece.astype(cont_out.dtype)


def unpack(place, index, own, back, rows, step, dtype):
    conts = index.shape[0]
    groups = conts // 2
    width = own.shape[1]
    return pl.pallas_call(
        functools.partial(unpack_kernel, groups),
        out_shape=(
            jax.ShapeDtypeStruct((2, rows, width), dtype),
            jax.ShapeDtypeStruct((conts, step, width), dtype),
        ),
        in_specs=[whole(space=pltpu.SMEM)] * 2 + [whole()] * 2,
        out_specs=(whole(),) * 2,
        scratch_shapes=[pltpu.SMEM((2 * groups,), jnp.int32), pltpu.SMEM((2,), jnp.int32)],
        compiler_params=params(),
        name="unpack_rows",
    )(place, index, own, back)


def scatter_kernel(groups, parts, own, aliased, place, index, *refs):
    sources, refs = refs[:parts], refs[parts + aliased :]
    prompt_out, cont_out, rows_s, order, count, sems = refs
    rows = prompt_out.shape[1]
    step = cont_out.shape[1]
    fill_order(index, order, count, groups, cont_out.shape[0])
    which = place[2] if own else 1 - place[2]
    size = sources[0].shape[0]
    copies = []
    for number, source in enumerate(sources):
        rows_s[number * size : (number + 1) * size, :] = source[...].astype(F32)
    copies.append(pltpu.make_async_copy(rows_s.at[pl.ds(0, rows), :], prompt_out.at[which], sems.at[0]))
    for slot in range(groups):
        piece = rows_s.at[pl.ds(rows + slot * step, step), :]
        copies.append(pltpu.make_async_copy(piece, cont_out.at[order[which * groups + slot]], sems.at[1 + slot]))
    for copy in copies:
        copy.start()
    for copy in copies:
        copy.wait()


def scatter(place, index, own, sources, rows, step, placed=()):
    conts = index.shape[0]
    groups = conts // 2
    width = sources[0].shape[1]
    aliases = {2 + len(sources) + i: i for i in range(len(placed))}
    return pl.pallas_call(
        functools.partial(scatter_kernel, groups, len(sources), own, len(placed)),
        out_shape=(jax.ShapeDtypeStruct((2, rows, width), F32), jax.ShapeDtypeStruct((conts, step, width), F32)),
        in_specs=[whole(space=pltpu.SMEM)] * 2 + [whole()] * len(sources) + [whole(space=pl.ANY)] * len(placed),
        out_specs=(whole(space=pl.ANY),) * 2,
        scratch_shapes=[
            pltpu.VMEM((rows + groups * step, width), F32),
            pltpu.SMEM((2 * groups,), jnp.int32),
            pltpu.SMEM((2,), jnp.int32),
            pltpu.SemaphoreType.DMA((1 + groups,)),
        ],
        input_output_aliases=aliases,
        compiler_params=params(),
        name="scatter_rows",
    )(place, index, *sources, *placed)


def blocks(fast, place, rows, model):
    if not fast:
        return [(0, (t,), t, 0, model) for t in range(4)]
    z, x, y, c = place[0], place[1], place[2], place[3]
    found = []
    for dc in range(2):
        for half in range(2):
            for near in range(2):
                for far in range(2):
                    kx, ky = (near, far) if half == 0 else (far, near)
                    for k in range(2):
                        t = 2 * (y ^ ky) + (c ^ dc)
                        row = ((z ^ (2 * half + k)) * 2 + (x ^ kx)) * rows
                        found.append((4 * dc + 2 * half + far, (near, k), t, row, rows))
    return found


def weight_copies(fast, place, pieces, held, sems, rows, model, columns=slice(None), base=0):
    copies = []
    for number, (piece, at, t, row, count) in enumerate(blocks(fast, place, rows, model)):
        if fast:
            row = pl.multiple_of(row, rows)
        source = pieces[piece].at[at + (slice(None), columns)]
        copies.append(
            pltpu.make_async_copy(source, held.at[t, pl.ds(row, count), columns], sems.at[base + number])
        )
    return copies


def store_grads(fast, place, held, outs, sems, rows, model):
    copies = []
    for number, (piece, at, t, row, count) in enumerate(blocks(fast, place, rows, model)):
        if fast:
            row = pl.multiple_of(row, rows)
            target = outs[2 * ((piece % 4) // 2) + piece // 4].at[(piece % 2,) + at]
        else:
            target = outs[0].at[at]
        copy = pltpu.make_async_copy(held.at[t, pl.ds(row, count), :], target, sems.at[number])
        copy.start()
        copies.append(copy)
    return copies


def n_blocks(fast):
    return 32 if fast else 4


def n_pieces(fast):
    return 8 if fast else 1


def n_grads(fast):
    return 4 if fast else 1


def grad_shapes(fast, rows, model, columns):
    if fast:
        return (jax.ShapeDtypeStruct((2, 2, 2, rows, columns), BF16),) * 4
    return (jax.ShapeDtypeStruct((4, model, columns), BF16),)


SWAP = [(0, 1), (1, 0)]


def over(axis, data):
    return lax.ppermute(data, axis, SWAP)


def over_z(data, k):
    return lax.ppermute(data, "z", [(i, i ^ k) for i in range(4)])


def after(data, *others):
    return lax.optimization_barrier((data,) + others)[0]


def gather_line(shard):
    return [over_z(shard, k) for k in (1, 2, 3)]


def stack_line(shard, got):
    return (jnp.stack([shard, got[0]]), jnp.stack([got[1], got[2]]))


def gather_near(line):
    return (over("x", line[0]), over("y", line[1]))


def stack_near(line, got):
    return tuple(jnp.stack([a, b]) for a, b in zip(line, got))


def gather_far(plane):
    return (over("y", plane[0]), over("x", plane[1]))


def gather_core(plane, far):
    mine = (plane[0], far[0], plane[1], far[1])
    return mine + tuple(over("c", piece) for piece in mine)


def gather_any(shard):
    flat = lax.all_gather(shard, ("z", "x"), axis=0, tiled=True)
    return (lax.all_gather(flat, ("y", "c"), axis=0, tiled=False),)


def total(items):
    return functools.reduce(jnp.add, [item.astype(F32) for item in items])


class Reduction:
    def __init__(self, grads):
        self.parts = [[grads[2 * half], over("c", grads[2 * half + 1])] for half in range(2)]

    def gate(self, *others):
        self.got = after(self.got, *others)

    def far_sum(self, half):
        return total([p[1] for p in self.parts[half]]).astype(BF16)

    def far(self, sums):
        self.got = [over(axis, s) for axis, s in zip(("y", "x"), sums)]

    def near_sums(self):
        self.from_far = self.got
        return [total([p[0, 1] for p in self.parts[h]] + [self.from_far[h][1]]).astype(BF16) for h in range(2)]

    def near(self, sums):
        self.got = [over(axis, s) for axis, s in zip(("x", "y"), sums)]

    def block(self, half, k):
        return [p[0, 0, k] for p in self.parts[half]] + [self.from_far[half][0, k], self.from_near[half][k]]

    def line_sums(self):
        self.from_near = self.got
        return [total(self.block(half, k)).astype(BF16) for half, k in ((0, 1), (1, 0), (1, 1))]

    def line(self, sums):
        self.got = [over_z(s, k) for k, s in zip((1, 2, 3), sums)]

    def result(self):
        return total(self.block(0, 0) + self.got)


def reduce_any(out):
    mine = lax.psum_scatter(out, ("y", "c"), scatter_dimension=0, tiled=False)
    return lax.psum_scatter(mine, ("z", "x"), scatter_dimension=0, tiled=True).astype(F32)


def left_lanes(rows):
    return lax.broadcasted_iota(jnp.int32, (rows, 128), 1) < HDIM


def flip(tile):
    return pltpu.roll(tile, HDIM, 1)


def tile(data, number):
    return data[:, number * 128 : (number + 1) * 128]


def join_first(even, odd):
    left = left_lanes(even.shape[0])
    e = [tile(even, i) for i in range(5)]
    o = [tile(odd, i) for i in range(5)]
    query = [e[0], jnp.where(left, e[1], o[0]), o[1]]
    key = [e[3], jnp.where(left, e[4], o[3]), o[4]]
    e1, e2, o2, o3 = flip(e[1]), flip(e[2]), flip(o[2]), flip(o[3])
    value = [jnp.where(left, e1, e2), jnp.where(left, e2, o2), jnp.where(left, o2, o3)]
    return query + key + value


def split_first(query, key, value):
    left = left_lanes(query[0].shape[0])
    none = jnp.zeros_like(query[0])
    v = [flip(t) for t in value]
    even = [
        query[0],
        jnp.where(left, query[1], v[0]),
        jnp.where(left, v[0], v[1]),
        key[0],
        jnp.where(left, key[1], none),
    ]
    odd = [
        jnp.where(left, none, query[1]),
        query[2],
        jnp.where(left, v[1], v[2]),
        jnp.where(left, v[2], key[1]),
        key[2],
    ]
    return even, odd


def turn(field, first):
    width = field.shape[-1]
    return jnp.where(first, pltpu.roll(field, width - HDIM // 2, 1), pltpu.roll(field, HDIM // 2, 1))


def first_half(shape):
    return lax.broadcasted_iota(jnp.int32, shape, 1) % HDIM < HDIM // 2


def qkv_kernel(fast, place, x_own, x_recv, cosine, sine, *refs):
    pieces = refs[: n_pieces(fast)]
    *results, gains, weights_out, q, k, v, weights, held, sems, out_sems = refs[n_pieces(fast) :]
    rows, model = x_own.shape
    per = model // 8 if fast else model

    def leave(half):
        return [
            pltpu.make_async_copy(made.at[half], result.at[half], out_sems.at[half, i])
            for i, (made, result) in enumerate(zip((q, k, v, weights), results + [weights_out]))
        ]

    copies = weight_copies(fast, place, pieces, held, sems, per, model)
    for copy in copies:
        copy.start()
    for copy in copies:
        copy.wait()
    gains[...] = jnp.transpose(held[0, :, 512:640].astype(F32))[64:72, :]
    side = place[2]
    first = first_half((rows, 128))

    def one(half, carry):
        def join(i, carry):
            at = pl.ds(pl.multiple_of(i * 96, 96), 96)
            for number, made in enumerate(join_first(held[2 * half, at, :], held[2 * half + 1, at, :])):
                weights[half, at, number * 128 : (number + 1) * 128] = made
            return carry

        lax.fori_loop(0, model // 96, join, 0)
        for x, where in ((x_own, side), (x_recv, 1 - side)):
            at = pl.ds(pl.multiple_of(where * rows, rows), rows)
            cos, sin = cosine[at, :], sine[at, :]
            made = dotf(x[...], weights[half])
            for p in range(3):
                lanes = slice(p * 128, (p + 1) * 128)
                u = tile(made, p)
                q[half, at, lanes] = ((u * cos + turn(u, first) * sin).astype(BF16) * 0.125).astype(BF16)
                u = tile(made, 3 + p)
                k[half, at, lanes] = (u * cos + turn(u, first) * sin).astype(BF16)
                v[half, at, lanes] = tile(made, 6 + p).astype(BF16)
        for copy in leave(half):
            copy.start()
        return carry

    lax.fori_loop(0, 2, one, 0)
    for half in range(2):
        for copy in leave(half):
            copy.wait()


def project(fast, place, x_own, x_recv, cosine, sine, pieces):
    rows, model = x_own.shape
    field = jax.ShapeDtypeStruct((2, 2 * rows, 384), BF16)
    return pl.pallas_call(
        functools.partial(qkv_kernel, fast),
        out_shape=(field,) * 3
        + (jax.ShapeDtypeStruct((8, model), F32), jax.ShapeDtypeStruct((2, model, 1152), BF16)),
        in_specs=[whole(space=pltpu.SMEM)] + [whole()] * 4 + [whole(space=pl.ANY)] * len(pieces),
        out_specs=(whole(space=pl.ANY),) * 3 + (whole(), whole(space=pl.ANY)),
        scratch_shapes=[pltpu.VMEM((2, 2 * rows, 384), BF16)] * 3
        + [
            pltpu.VMEM((2, model, 1152), BF16),
            pltpu.VMEM((4, model, 640), BF16),
            pltpu.SemaphoreType.DMA((n_blocks(fast),)),
            pltpu.SemaphoreType.DMA((2, 4)),
        ],
        compiler_params=params(),
        name="project_qkv",
    )(place, x_own, x_recv, cosine, sine, *pieces)


class Layout:
    def __init__(self, rows, prompt, step):
        self.rows = rows
        self.prompt = prompt
        self.step = step
        self.pair = 2 * step
        self.cont_blocks = (rows - prompt) // (4 * step)
        self.width = 8 * step


def pair_rows(ref, lay, start):
    return (ref[pl.ds(start, lay.pair), :], ref[pl.ds(lay.rows + start, lay.pair), :])


def pair_start(lay, block, pair):
    return lay.prompt + (2 * block + pair) * lay.pair


def cont_query(ref, lay, block):
    parts = []
    for pair in range(2):
        parts += pair_rows(ref, lay, pair_start(lay, block, pair))
    return jnp.concatenate(parts, 0)


def cont_keys(own, other, lay, block, pair):
    start = pair_start(lay, block, pair)
    return jnp.concatenate(pair_rows(own, lay, start) + pair_rows(other, lay, start), 0)


def causal(count, key_axis):
    key = lax.broadcasted_iota(jnp.int32, (count, count), key_axis)
    row = lax.broadcasted_iota(jnp.int32, (count, count), 1 - key_axis)
    return jnp.where(key <= row, 0.0, NEGATIVE)


def shared_segments(lay):
    return [(0, 0), (0, lay.rows), (1, 0), (1, lay.rows)]


def attend_kernel(lay, place, q_ref, ko, vo, kp, vp, own_mask, mixed, lse, lse_s):
    inner = place[2] != place[3]
    q, keys, values, out = q_ref.at[0], (ko.at[0], kp.at[0]), (vo.at[0], vp.at[0]), mixed.at[0]
    count, width = lay.prompt, lay.width
    half = width // 2
    lane = lax.broadcasted_iota(jnp.int32, (1, 128), 1) // HDIM
    spot = lax.broadcasted_iota(jnp.int32, (1, 128), 1)
    low, high = pl.ds(0, count), pl.ds(lay.rows, count)
    extra = pl.ds(pl.multiple_of(jnp.where(inner, 0, lay.rows), lay.rows), count)
    out[...] = jnp.zeros_like(out)
    lse_s[...] = jnp.zeros_like(lse_s)

    def top(scores):
        return jnp.max(functools.reduce(jnp.maximum, scores), 1, keepdims=True)

    def sums(raised):
        return jnp.sum(functools.reduce(jnp.add, raised), 1, keepdims=True)

    def head(j, carry):
        chosen = lane == j

        def pick(block):
            return jnp.where(chosen, block, jnp.zeros_like(block))

        def finish(at, made, total, highest, number):
            out[at, :] = out[at, :] + pick(made / total).astype(BF16)
            here = pl.ds(number, made.shape[0])
            lse_s[here, :] = jnp.where(spot == j, highest + jnp.log(total), lse_s[here, :])

        q_low, q_high = pick(q[low, :]), pick(q[high, :])
        q_extra = jnp.where(inner, q_low, q_high)
        mask = causal(count, 1)
        s_low = dotf(q_low, keys[0][low, :], LAST) + mask
        s_high = [
            dotf(q_high, keys[0][high, :], LAST) + mask,
            dotf(q_high, keys[0][low, :], LAST),
            dotf(q_high, keys[1][low, :], LAST),
        ]
        s_extra = dotf(q_extra, keys[1][extra, :], LAST)
        s_cont = []
        for block in range(lay.cont_blocks):
            query = pick(cont_query(q, lay, block))
            scores = [dotf(query, keys[o][pl.ds(start, count), :], LAST) for o, start in shared_segments(lay)]
            own = []
            for pair in range(2):
                rows = query[pair * half : (pair + 1) * half, :]
                own.append(dotf(rows, cont_keys(keys[0], keys[1], lay, block, pair), LAST) + own_mask[...])
            s_cont.append(scores + [jnp.concatenate(own, 0)])

        m_low, m_high, m_extra = top([s_low]), top(s_high), top([s_extra])
        m_low = jnp.maximum(m_low, jnp.where(inner, m_extra, NEGATIVE))
        m_high = jnp.maximum(m_high, jnp.where(inner, NEGATIVE, m_extra))
        p_low = jnp.exp(s_low - m_low)
        p_high = [jnp.exp(s - m_high) for s in s_high]
        p_extra = jnp.exp(s_extra - jnp.where(inner, m_low, m_high))
        l_extra = sums([p_extra])
        l_low = sums([p_low]) + jnp.where(inner, l_extra, 0.0)
        l_high = sums(p_high) + jnp.where(inner, 0.0, l_extra)
        o_extra = dotf(p_extra.astype(BF16), values[1][extra, :])
        o_low = dotf(p_low.astype(BF16), values[0][low, :]) + jnp.where(inner, o_extra, 0.0)
        o_high = (
            dotf(p_high[0].astype(BF16), values[0][high, :])
            + dotf(p_high[1].astype(BF16), values[0][low, :])
            + dotf(p_high[2].astype(BF16), values[1][low, :])
            + jnp.where(inner, 0.0, o_extra)
        )
        finish(low, o_low, l_low, m_low, 0)
        finish(high, o_high, l_high, m_high, count)

        for block, scores in enumerate(s_cont):
            highest = top(scores)
            raised = [jnp.exp(s - highest) for s in scores]
            total = sums(raised)
            raised = [r.astype(BF16) for r in raised]
            made = functools.reduce(
                jnp.add, [dotf(r, values[o][pl.ds(start, count), :]) for r, (o, start) in zip(raised, shared_segments(lay))]
            )
            for pair in range(2):
                cut = slice(pair * half, (pair + 1) * half)
                part = made[cut, :] + dotf(raised[-1][cut, :], cont_keys(values[0], values[1], lay, block, pair))
                part = pick(part / total[cut, :]).astype(BF16)
                start = pair_start(lay, block, pair)
                for side in range(2):
                    at = pl.ds(side * lay.rows + start, lay.pair)
                    out[at, :] = out[at, :] + part[side * lay.pair : (side + 1) * lay.pair, :]
            here = pl.ds(2 * count + block * width, width)
            lse_s[here, :] = jnp.where(spot == j, highest + jnp.log(total), lse_s[here, :])
        return carry

    lax.fori_loop(0, 2, head, 0)
    lse[0, 0] = jnp.transpose(lse_s[...])[0:8, :]


def attend(lay, place, q, ko, vo, kp, vp, own_mask):
    total = q.shape[1]
    field = pl.BlockSpec((1, total, 128), lambda h, p, place: (h, 0, p))
    return pl.pallas_call(
        functools.partial(attend_kernel, lay),
        out_shape=(jax.ShapeDtypeStruct(q.shape, BF16), jax.ShapeDtypeStruct((2, 3, 8, total), F32)),
        grid_spec=pltpu.PrefetchScalarGridSpec(
            num_scalar_prefetch=1,
            grid=(2, 3),
            in_specs=[field] * 5 + [pl.BlockSpec(own_mask.shape, lambda h, p, place: (0, 0))],
            out_specs=(field, pl.BlockSpec((1, 1, 8, total), lambda h, p, place: (h, p, 0, 0))),
            scratch_shapes=[pltpu.VMEM((total, 128), F32)],
        ),
        compiler_params=params(),
        name="attend",
    )(place, q, ko, vo, kp, vp, own_mask)


def attend_back_kernel(
    lay, place, q_ref, ko, vo, kp, vp, mixed, up_ref, lse_ref, own_mask, dq, dko, dvo, dkp, dvp, kacc, vacc, qacc, delta_s
):
    inner = place[2] != place[3]
    q, keys, values = q_ref.at[0], (ko.at[0], kp.at[0]), (vo.at[0], vp.at[0])
    upstream, result, lse = up_ref.at[0], mixed.at[0], lse_ref.at[0]
    count, width = lay.prompt, lay.width
    half = width // 2
    lane = lax.broadcasted_iota(jnp.int32, (1, 128), 1) // HDIM
    kacc[...] = jnp.zeros_like(kacc)
    vacc[...] = jnp.zeros_like(vacc)
    qacc[...] = jnp.zeros_like(qacc)
    low, high = pl.ds(0, count), pl.ds(lay.rows, count)
    shift = jnp.where(inner, 0, 1)
    extra = pl.ds(pl.multiple_of(shift * lay.rows, lay.rows), count)
    either = pl.ds(pl.multiple_of(shift * count, count), count)

    def cont_rows(ref):
        return jnp.concatenate([cont_query(ref, lay, block) for block in range(lay.cont_blocks)], 0)

    def product(rows):
        return rows(upstream).astype(F32) * rows(result).astype(F32)

    heads = jnp.where(
        lax.broadcasted_iota(jnp.int32, (8, 128), 1) // HDIM == lax.broadcasted_iota(jnp.int32, (8, 128), 0), 1.0, 0.0
    ).astype(BF16)
    for at, rows in (
        (slice(0, count), lambda ref: ref[low, :]),
        (slice(count, 2 * count), lambda ref: ref[high, :]),
        (slice(2 * count, 2 * count + lay.cont_blocks * width), cont_rows),
    ):
        made = product(rows)
        coarse = made.astype(BF16)
        fine = (made - coarse.astype(F32)).astype(BF16)
        delta_s[:, at] = dotf(heads, coarse, LAST) + dotf(heads, fine, LAST)

    def head(j, carry):
        chosen = lane == j
        me = pl.ds(j, 1)

        def pick(block):
            return jnp.where(chosen, block, jnp.zeros_like(block))

        def back(key, value, query, grads, mask, log_total, delta):
            s = dotf(key, query, LAST)
            if mask is not None:
                s = s + mask
            share = jnp.exp(s - log_total)
            d = (share * (dotf(value, grads, LAST) - delta)).astype(BF16)
            return dotf(share.astype(BF16), grads), dotf(d, query), dotf(d, key, FIRST)

        def put(other, at, dv, dk):
            vacc[other, at, :] += dv
            kacc[other, at, :] += dk

        query, grads = pick(cont_rows(q)), pick(cont_rows(upstream))
        at = pl.ds(2 * count, lay.cont_blocks * width)
        log_total, delta = lse[0, me, at], delta_s[me, at]
        shared = shared_segments(lay)
        key = jnp.concatenate([keys[o][pl.ds(start, count), :] for o, start in shared], 0)
        value = jnp.concatenate([values[o][pl.ds(start, count), :] for o, start in shared], 0)
        dv, dk, total = back(key, value, query, grads, None, log_total, delta)
        for number, (other, start) in enumerate(shared):
            piece = slice(number * count, (number + 1) * count)
            put(other, pl.ds(start, count), dv[piece, :], dk[piece, :])
        for number in range(2 * lay.cont_blocks):
            block, pair = number // 2, number % 2
            cut = slice(number * half, (number + 1) * half)
            dv, dk, made = back(
                cont_keys(keys[0], keys[1], lay, block, pair),
                cont_keys(values[0], values[1], lay, block, pair),
                query[cut, :],
                grads[cut, :],
                own_mask[...],
                log_total[:, cut],
                delta[:, cut],
            )
            start = pair_start(lay, block, pair)
            for part in range(4):
                piece = slice(part * lay.pair, (part + 1) * lay.pair)
                put(part // 2, pl.ds((part % 2) * lay.rows + start, lay.pair), dv[piece, :], dk[piece, :])
            made = pick(total[cut, :] + made)
            for part in range(2):
                spot = pl.ds(part * lay.rows + start, lay.pair)
                qacc[spot, :] += made[part * lay.pair : (part + 1) * lay.pair, :]
        mask = causal(count, 0)
        at = pl.ds(count, count)
        query, grads, log_total, delta = pick(q[high, :]), pick(upstream[high, :]), lse[0, me, at], delta_s[me, at]
        seen = ((0, high), (0, low), (1, low))
        key = jnp.concatenate([keys[o][spot, :] for o, spot in seen], 0)
        value = jnp.concatenate([values[o][spot, :] for o, spot in seen], 0)
        tall = jnp.concatenate([mask, jnp.zeros((2 * count, count), F32)], 0)
        dv, dk, made = back(key, value, query, grads, tall, log_total, delta)
        for number, (other, spot) in enumerate(seen):
            piece = slice(number * count, (number + 1) * count)
            put(other, spot, dv[piece, :], dk[piece, :])
        qacc[high, :] += pick(made)
        at = pl.ds(0, count)
        dv, dk, made = back(
            keys[0][low, :],
            values[0][low, :],
            pick(q[low, :]),
            pick(upstream[low, :]),
            mask,
            lse[0, me, at],
            delta_s[me, at],
        )
        put(0, low, dv, dk)
        qacc[low, :] += pick(made)
        dv, dk, made = back(
            keys[1][extra, :],
            values[1][extra, :],
            pick(q[extra, :]),
            pick(upstream[extra, :]),
            None,
            lse[0, me, either],
            delta_s[me, either],
        )
        put(1, extra, dv, dk)
        qacc[extra, :] += pick(made)
        return carry

    lax.fori_loop(0, 2, head, 0)
    dq[...] = (qacc[...] * 0.125).astype(BF16)
    dko[...] = kacc[0].astype(BF16)
    dkp[...] = kacc[1].astype(BF16)
    dvo[...] = vacc[0].astype(BF16)
    dvp[...] = vacc[1].astype(BF16)


def attend_back(lay, place, half, q, ko, vo, kp, vp, mixed, upstream, lse, own_mask):
    total = q.shape[1]
    field = pl.BlockSpec((1, total, 128), lambda p, place: (half, 0, p))
    made = pl.BlockSpec((total, 128), lambda p, place: (0, p))
    return pl.pallas_call(
        functools.partial(attend_back_kernel, lay),
        out_shape=(jax.ShapeDtypeStruct((total, 384), BF16),) * 5,
        grid_spec=pltpu.PrefetchScalarGridSpec(
            num_scalar_prefetch=1,
            grid=(3,),
            in_specs=[field] * 7
            + [
                pl.BlockSpec((1, 1, 8, total), lambda p, place: (half, p, 0, 0)),
                pl.BlockSpec(own_mask.shape, lambda p, place: (0, 0)),
            ],
            out_specs=(made,) * 5,
            scratch_shapes=[
                pltpu.VMEM((2, total, 128), F32),
                pltpu.VMEM((2, total, 128), F32),
                pltpu.VMEM((total, 128), F32),
                pltpu.VMEM((8, total), F32),
            ],
        ),
        compiler_params=params(),
        name="attend_back",
    )(place, q, ko, vo, kp, vp, mixed, upstream, lse, own_mask)


def middle_kernel(fast, hid, place, mixed, xo, xr, dyo, dyr, gains, *refs):
    count = n_pieces(fast)
    pieces, refs = refs[:count], refs[count:]
    (out_own, out_send, dhp, dmixed), refs = refs[:4], refs[4:]
    count = n_grads(fast)
    grads, refs = refs[:count], refs[count:]
    held, wide_o, gate_s, up_s, hid_s, dgate_s, dup_s, low_t, fed_t, att_t, gain_acc, sum_s, sems = refs
    step = pl.program_id(0)
    model = held.shape[1]
    rows = xo.shape[0]
    per = model // 8 if fast else model
    G, U, D, O = slice(0, hid), slice(hid, 2 * hid), slice(2 * hid, 3 * hid), 3 * hid
    side = jnp.where(step == 0, place[2], 1 - place[2])
    here = pl.ds(pl.multiple_of(side * rows, rows), rows)
    left = left_lanes(model)
    out_copies = weight_copies(fast, place, pieces, held, sems, per, model, slice(O, O + 256))
    other_copies = weight_copies(fast, place, pieces, held, sems, per, model, slice(0, O), n_blocks(fast))

    @pl.when(step == 0)
    def _():
        for copy in out_copies + other_copies:
            copy.start()
        gain_acc[...] = jnp.zeros_like(gain_acc)
        for copy in out_copies:
            copy.wait()
        for half in range(2):
            even, odd = held.at[2 * half], held.at[2 * half + 1]
            wide_o[half, :, 0:128] = even[:, O : O + 128]
            wide_o[half, :, 128:256] = jnp.where(left, even[:, O + 128 : O + 256], odd[:, O : O + 128])
            wide_o[half, :, 256:384] = odd[:, O + 128 : O + 256]

    own = step == 0
    gain_a = gains[0:1, :]
    gain_f = gains[1:2, :]
    pre = jnp.where(own, xo[...], xr[...]).astype(F32)
    for half in range(2):
        pre = pre + dotf(mixed[half, here, :], wide_o[half], LAST)
    scale1 = lax.rsqrt(jnp.mean(pre * pre, -1, keepdims=True) + EPSILON)
    norm1 = pre * scale1
    normed = norm1 * gain_a
    low = normed.astype(BF16)
    low_t[step] = jnp.transpose(low)
    spot = pl.ds(pl.multiple_of(step * rows, rows), rows)

    @pl.when(step == 0)
    def _():
        for copy in other_copies:
            copy.wait()

    def forward(t, carry):
        gate = dotf(low, held[t, :, G])
        up = dotf(low, held[t, :, U])
        gate_s[t] = gate
        up_s[t] = up
        hid_s[t, spot, :] = (gate * jax.nn.sigmoid(gate) * up).astype(BF16)
        return carry

    def add_over(fields, columns):
        field = jnp.concatenate([fields[t, spot, :] for t in range(4)], 1)

        def chunk(n, carry):
            at = pl.ds(pl.multiple_of(n * 256, 256), 256)
            weight = jnp.concatenate([held[t, at, columns] for t in range(4)], 1)
            sum_s[:, at] = sum_s[:, at] + dotf(field, weight, LAST)
            return carry

        lax.fori_loop(0, model // 256, chunk, 0)

    lax.fori_loop(0, 4, forward, 0)
    sum_s[...] = normed
    add_over(hid_s, D)
    resid = sum_s[...]
    scale2 = lax.rsqrt(jnp.mean(resid * resid, -1, keepdims=True) + EPSILON)
    norm2 = resid * scale2
    result = (norm2 * gain_f).astype(BF16)

    @pl.when(own)
    def _():
        out_own[...] = result

    @pl.when(jnp.logical_not(own))
    def _():
        out_send[...] = result

    dy = jnp.where(own, dyo[...], dyr[...]).astype(F32)
    gain_acc[1:2, :] += jnp.sum(dy * norm2, 0, keepdims=True)
    e2 = dy * gain_f
    d_resid = scale2 * (e2 - norm2 * jnp.mean(e2 * norm2, -1, keepdims=True))
    d_fed = d_resid.astype(BF16)
    fed_t[step] = jnp.transpose(d_fed)

    def backward(t, carry):
        gate, up = gate_s[t], up_s[t]
        d_hidden = dotf(d_fed, held[t, :, D])
        sig = jax.nn.sigmoid(gate)
        dgate_s[t, spot, :] = (d_hidden * up * sig * (1.0 + gate * (1.0 - sig))).astype(BF16)
        dup_s[t, spot, :] = (d_hidden * gate * sig).astype(BF16)
        return carry

    lax.fori_loop(0, 4, backward, 0)
    sum_s[...] = d_resid
    add_over(dgate_s, G)
    add_over(dup_s, U)
    d_normed = sum_s[...]
    gain_acc[0:1, :] += jnp.sum(d_normed * norm1, 0, keepdims=True)
    e1 = d_normed * gain_a
    d_pre = scale1 * (e1 - norm1 * jnp.mean(e1 * norm1, -1, keepdims=True))
    dhp[...] = d_pre
    d_att = d_pre.astype(BF16)
    att_t[step] = jnp.transpose(d_att)
    for half in range(2):
        dmixed[half] = dotf(d_att, wide_o[half]).astype(BF16)

    @pl.when(step == 1)
    def _():
        columns = jnp.transpose(jnp.broadcast_to(gain_acc[0:8, :], (8, model)))
        lane = lax.broadcasted_iota(jnp.int32, (model, 128), 1) % HDIM
        extra = jnp.where(lane == 0, columns[:, 0:1], jnp.where(lane == 1, columns[:, 1:2], 0.0))
        halves = (place[2], 1 - place[2])
        for half in range(2):
            made = None
            for part in range(2):
                at = pl.ds(pl.multiple_of(halves[part] * rows, rows), rows)
                more = dotf(att_t[part], mixed[half, at, :])
                made = more if made is None else made + more
            even, odd = held.at[2 * half], held.at[2 * half + 1]
            even[:, O : O + 128] = tile(made, 0).astype(BF16)
            even[:, O + 128 : O + 256] = jnp.where(left, tile(made, 1), extra).astype(BF16)
            odd[:, O : O + 128] = jnp.where(left, extra, tile(made, 1)).astype(BF16)
            odd[:, O + 128 : O + 256] = tile(made, 2).astype(BF16)

        def weight(r, carry):
            t = 2 * (place[2] ^ (r // 2)) + (place[3] ^ (r % 2)) if fast else r
            for columns, first, second in ((D, fed_t, hid_s), (G, low_t, dgate_s), (U, low_t, dup_s)):
                made = dotf(first[0], second[t, 0:rows, :]) + dotf(first[1], second[t, rows : 2 * rows, :])
                held[t, :, columns] = made.astype(BF16)
            if fast:
                for dc in range(2):

                    @pl.when(r % 2 == dc)
                    def _(dc=dc):
                        send_block(place, r // 2, dc, held, grads, sems, per, True)

            return carry

        lax.fori_loop(0, 4, weight, 0)
        if fast:
            for r in range(4):
                send_block(place, r // 2, r % 2, held, grads, sems, per, False)
        else:
            for copy in store_grads(fast, place, held, grads, sems, per, model):
                copy.wait()


def send_block(place, ky, dc, held, targets, sems, rows, start):
    z, x, y, c = place[0], place[1], place[2], place[3]
    t = 2 * (y ^ ky) + (c ^ dc)
    for kz in range(4):
        for kx in range(2):
            half, k = kz // 2, kz % 2
            far, near = (ky, kx) if half == 0 else (kx, ky)
            row = pl.multiple_of(((z ^ kz) * 2 + (x ^ kx)) * rows, rows)
            number = 16 * dc + 8 * ky + 2 * kz + kx
            copy = pltpu.make_async_copy(
                held.at[t, pl.ds(row, rows), :], targets[2 * half + dc].at[far, near, k], sems.at[number]
            )
            if start:
                copy.start()
            else:
                copy.wait()


def once(shape, index=None):
    return pl.BlockSpec(shape, index or (lambda i, place: (0,) * len(shape)), pipeline_mode=pl.Buffered(1))


def middle(fast, place, mixed, xo, xr, dyo, dyr, gains, pieces, hid):
    rows, model = xo.shape
    columns = 3 * hid + 256
    grads = grad_shapes(fast, model // 8 if fast else model, model, columns)

    def side_at(i, place):
        return (0, jnp.where(i == 0, place[2], 1 - place[2]), 0)

    half_rows = once((rows, model))
    field = once((2, 2 * rows, 384))
    return pl.pallas_call(
        functools.partial(middle_kernel, fast, hid),
        out_shape=(
            jax.ShapeDtypeStruct((rows, model), BF16),
            jax.ShapeDtypeStruct((rows, model), BF16),
            jax.ShapeDtypeStruct((2 * rows, model), F32),
            jax.ShapeDtypeStruct(mixed.shape, BF16),
        )
        + grads,
        grid_spec=pltpu.PrefetchScalarGridSpec(
            num_scalar_prefetch=1,
            grid=(2,),
            in_specs=[field] + [half_rows] * 4 + [once((8, model))] + [whole(space=pl.ANY)] * len(pieces),
            out_specs=(
                pl.BlockSpec((rows, model), lambda i, place: (0, 0)),
                pl.BlockSpec((rows, model), lambda i, place: (0, 0)),
                pl.BlockSpec((rows, model), lambda i, place: (i, 0)),
                pl.BlockSpec((2, rows, 384), side_at),
            )
            + (whole(space=pl.ANY),) * len(grads),
            scratch_shapes=[
                pltpu.VMEM((4, model, columns), BF16),
                pltpu.VMEM((2, model, 384), BF16),
                pltpu.VMEM((4, rows, hid), F32),
                pltpu.VMEM((4, rows, hid), F32),
                pltpu.VMEM((4, 2 * rows, hid), BF16),
                pltpu.VMEM((4, 2 * rows, hid), BF16),
                pltpu.VMEM((4, 2 * rows, hid), BF16),
                pltpu.VMEM((2, model, rows), BF16),
                pltpu.VMEM((2, model, rows), BF16),
                pltpu.VMEM((2, model, rows), BF16),
                pltpu.VMEM((8, model), F32),
                pltpu.VMEM((rows, model), F32),
                pltpu.SemaphoreType.DMA((2 * n_blocks(fast),)),
            ],
        ),
        compiler_params=params(),
        name="middle",
    )(place, mixed, xo, xr, dyo, dyr, gains, *pieces)


def qkv_back_kernel(fast, place, x_own, x_recv, cosine, sine, dhp_ref, weights_ref, *refs):
    fields = [refs[2 * i : 2 * i + 2] for i in range(5)]
    dx_own, dx_sends = refs[10], refs[11:13]
    grads, refs = refs[13 : 13 + n_grads(fast)], refs[13 + n_grads(fast) :]
    held, joined, made, x_t, dx, weights, moved, sems, extra_sems = refs
    rows, model = x_own.shape
    per = model // 8 if fast else model
    side = place[2]
    first = first_half((rows, 128))
    copies = [pltpu.make_async_copy(dhp_ref, dx, extra_sems.at[0])]
    for half in range(2):
        copies.append(pltpu.make_async_copy(weights_ref.at[half], weights.at[half], extra_sems.at[1 + 6 * half]))
        for i in range(5):
            copies.append(pltpu.make_async_copy(fields[i][half], moved.at[half, i], extra_sems.at[2 + i + 6 * half]))
    for copy in copies:
        copy.start()
    for number, x in enumerate((x_own, x_recv)):
        x_t[number] = jnp.transpose(x[...])
    for copy in copies[:7]:
        copy.wait()

    def one(half, carry):
        @pl.when(half == 1)
        def _():
            for copy in copies[7:]:
                copy.wait()

        def turn_back(number, carry):
            at = pl.ds(pl.multiple_of((side ^ number) * rows, rows), rows)
            cos, sin = cosine[at, :], sine[at, :]
            for p in range(3):
                lanes = slice(p * 128, (p + 1) * 128)
                query, key, value, key_more, value_more = [moved[half, i, at, lanes].astype(F32) for i in range(5)]
                joined[number, 0, :, lanes] = (query * cos - turn(query, first) * sin).astype(BF16)
                key = key + key_more
                joined[number, 1, :, lanes] = (key * cos - turn(key, first) * sin).astype(BF16)
                joined[number, 2, :, lanes] = (value + value_more).astype(BF16)
            whole_row = jnp.concatenate([joined[number, kind] for kind in range(3)], 1)
            spot = pl.ds(pl.multiple_of(number * rows, rows), rows)
            dx[spot, :] = dx[spot, :] + dotf(whole_row, weights[half], LAST)
            return carry

        def weight(kind, carry):
            made[kind] = (dotf(x_t[0], joined[0, kind]) + dotf(x_t[1], joined[1, kind])).astype(BF16)
            return carry

        lax.fori_loop(0, 2, turn_back, 0)
        lax.fori_loop(0, 3, weight, 0)

        def split(i, carry):
            at = pl.ds(pl.multiple_of(i * 96, 96), 96)
            even, odd = split_first(*[[tile(made[kind, at, :], p) for p in range(3)] for kind in range(3)])
            for p in range(5):
                held[2 * half, at, p * 128 : (p + 1) * 128] = even[p]
                held[2 * half + 1, at, p * 128 : (p + 1) * 128] = odd[p]
            return carry

        lax.fori_loop(0, model // 96, split, 0)
        if fast:
            for dc in range(2):
                send_block(place, side ^ half, dc, held, grads, sems, per, True)
        return carry

    lax.fori_loop(0, 2, one, 0)
    dx_own[...] = dx[0:rows, :]
    for number in range(2):
        cut = slice(rows + number * (rows // 2), rows + (number + 1) * (rows // 2))
        dx_sends[number][...] = dx[cut, :].astype(BF16)
    if fast:
        for half in range(2):
            for dc in range(2):
                send_block(place, side ^ half, dc, held, grads, sems, per, False)
    else:
        for copy in store_grads(fast, place, held, grads, sems, per, model):
            copy.wait()


def project_back(fast, place, x_own, x_recv, cosine, sine, dhp, weights, fields):
    rows, model = x_own.shape
    grads = grad_shapes(fast, model // 8 if fast else model, model, 640)
    return pl.pallas_call(
        functools.partial(qkv_back_kernel, fast),
        out_shape=(jax.ShapeDtypeStruct((rows, model), F32),)
        + (jax.ShapeDtypeStruct((rows // 2, model), BF16),) * 2
        + grads,
        in_specs=[whole(space=pltpu.SMEM)]
        + [whole()] * 4
        + [whole(space=pl.ANY)] * 2
        + [whole(space=pl.ANY)] * 10,
        out_specs=(whole(),) * 3 + (whole(space=pl.ANY),) * len(grads),
        scratch_shapes=[
            pltpu.VMEM((4, model, 640), BF16),
            pltpu.VMEM((2, 3, rows, 384), BF16),
            pltpu.VMEM((3, model, 384), BF16),
            pltpu.VMEM((2, model, rows), BF16),
            pltpu.VMEM((2 * rows, model), F32),
            pltpu.VMEM((2, model, 1152), BF16),
            pltpu.VMEM((2, 5, 2 * rows, 384), BF16),
            pltpu.SemaphoreType.DMA((n_blocks(fast),)),
            pltpu.SemaphoreType.DMA((13,)),
        ],
        compiler_params=params(),
        name="project_back",
    )(place, x_own, x_recv, cosine, sine, dhp, weights, *fields)


def tables(quarters, prompt, step, groups, plen):
    half = HDIM // 2
    places = []
    for quarter in quarters:
        places.append((quarter * prompt + jnp.arange(prompt)).astype(F32))
        places.append(jnp.tile((plen + quarter * step + jnp.arange(step)).astype(F32), groups))
    lanes = jnp.arange(2 * HDIM)
    frequency = 10000.0 ** (-(lanes % half).astype(F32) / half)
    angle = jnp.concatenate(places)[:, None] * frequency[None, :]
    return jnp.cos(angle), jnp.sin(angle) * jnp.where(lanes % HDIM < half, -1.0, 1.0)[None, :]


def own_continuation_mask(quarters, step):
    offset = jnp.arange(2 * step) % step
    cont = jnp.arange(2 * step) // step
    places = jnp.concatenate([quarter * step + offset for quarter in quarters])
    number = jnp.tile(cont, 4)
    rows = 4 * step
    allowed = (places[:, None] <= places[None, :rows]) & (number[:, None] == number[None, :rows])
    mask = jnp.where(allowed, 0.0, NEGATIVE).astype(F32)
    return mask, mask.T


def on_device(
    fast,
    prompt_tokens,
    continuation_tokens,
    prompt_index,
    attention_gain,
    query_weight,
    key_weight,
    value_weight,
    output_weight,
    feedforward_gain,
    gate_weight,
    up_weight,
    down_weight,
    prompt_cotangent,
    continuation_cotangent,
):
    z, x, y, c = [lax.axis_index(name).astype(jnp.int32) for name in ("z", "x", "y", "c")]
    place = jnp.stack([z, x, y, c])
    prompts, prompt_rows, model = prompt_tokens.shape
    conts, step, _ = continuation_tokens.shape
    groups = conts // prompts
    plen = 4 * prompt_rows
    rows = prompt_rows + groups * step
    lay = Layout(rows, prompt_rows, step)
    shard_rows, columns = query_weight.shape
    hid = gate_weight.shape[1]
    local = 2 * y + c
    other = 2 * y + (1 - c)
    quarters = [jnp.minimum(t, 3 - t) if low else jnp.maximum(t, 3 - t) for t in (local, other) for low in (1, 0)]

    gains = [attention_gain[:, None], feedforward_gain[:, None], jnp.zeros((shard_rows, 62), BF16)]
    first = [query_weight, value_weight, key_weight]
    first = jnp.where(c == 0, jnp.concatenate(first + gains, 1), jnp.concatenate(gains + first, 1))
    wide = [gate_weight, up_weight]
    down, out, gap = down_weight.T, output_weight.T, jnp.zeros((shard_rows, 64), BF16)
    rest = jnp.where(c == 0, jnp.concatenate(wide + [down, out, gap], 1), jnp.concatenate(wide + [down, gap, out], 1))

    def swap(data):
        return lax.ppermute(data, ("y", "c"), [(0, 3), (3, 0), (1, 2), (2, 1)])

    if fast:
        x_own, x_send = pack(place, prompt_index, prompt_tokens, continuation_tokens)
        x_recv = swap(x_send)
        dy_own, dy_send = pack(after(place, x_send), prompt_index, prompt_cotangent, continuation_cotangent)
        first = after(first, dy_send)
        got = gather_line(first)
        line = stack_line(first, after(got, rest))
        got = gather_near(line)
        rest = after(rest, *line)
        rest_got = gather_line(rest)
        dy_recv = swap(after(dy_send, *line))
        cosine, sine = tables(after(tuple(quarters[:2]), *line), prompt_rows, step, groups, plen)
        own_mask, row_mask = own_continuation_mask(after(tuple(quarters), *line), step)
        plane = stack_near(line, after(got, cosine, sine, own_mask, row_mask, x_recv, dy_recv, rest_got[0], rest_got[1]))
        far = gather_far(plane)
        first_pieces = gather_core(plane, far)
        rest_line = stack_line(rest, after(rest_got, *far))
        rest_got = gather_near(rest_line)
        q, k, v, gains, weights = project(
            fast, place, x_own, x_recv, cosine, sine, after(first_pieces, *rest_line)
        )
        k_other, v_other = over("c", k), over("c", v)
        rest_plane = stack_near(rest_line, after(rest_got, q))
        rest_far = gather_far(rest_plane)
        mixed, lse = attend(lay, place, q, k, v, k_other, v_other, after(row_mask, *rest_plane))
        rest_pieces = gather_core(after(rest_plane, mixed), after(rest_far, mixed))
    else:
        x_own, x_send = pack(place, prompt_index, prompt_tokens, continuation_tokens)
        dy_own, dy_send = pack(place, prompt_index, prompt_cotangent, continuation_cotangent)
        x_recv, dy_recv = swap(x_send), swap(dy_send)
        first_pieces, rest_pieces = gather_any(first), gather_any(rest)
        cosine, sine = tables(quarters[:2], prompt_rows, step, groups, plen)
        own_mask, row_mask = own_continuation_mask(quarters, step)
        q, k, v, gains, weights = project(fast, place, x_own, x_recv, cosine, sine, first_pieces)
        k_other, v_other = over("c", k), over("c", v)
        mixed, lse = attend(lay, place, q, k, v, k_other, v_other, row_mask)
    made = middle(fast, place, mixed, x_own, x_recv, dy_own, dy_recv, gains, rest_pieces, hid)
    out_own, out_send, dhp, dmixed = made[:4]
    grads = made[4:]

    def back(half, mask):
        return attend_back(lay, place, half, q, k, v, k_other, v_other, mixed, dmixed, lse, mask)

    def collect(made):
        return [[m[i] for m in made] for i in range(3)] + [[over("c", m[i]) for m in made] for i in (3, 4)]

    if fast:
        rest_sum = Reduction(grads)
        sums = [rest_sum.far_sum(0), rest_sum.far_sum(1)]
        rest_sum.far(sums)
        done = [back(0, after(own_mask, *sums))]
        rest_sum.gate(done[0][0])
        sums = rest_sum.near_sums()
        rest_sum.near(sums)
        out_recv = swap(after(out_send, *sums))
        done.append(back(1, after(own_mask, *sums)))
        rest_sum.gate(done[1][0])
        sums = rest_sum.line_sums()
        rest_sum.line(sums)
        fields = sum(collect(done), [])
        made = project_back(fast, place, x_own, x_recv, cosine, sine, after(dhp, out_recv, *sums), weights, fields)
        dx_own, dx_sends = made[0], made[1:3]
        first_sum = Reduction(after(made[3:], rest_sum.got[0], rest_sum.got[1]))
        out_prompt, out_cont = unpack(place, prompt_index, out_own, after(out_recv, dx_own), prompt_rows, step, BF16)
        sums = [first_sum.far_sum(0), first_sum.far_sum(1)]
        first_sum.far(sums)
        dx_first = swap(dx_sends[0])
        rest_sum.gate(out_prompt, dx_first, *sums)
        rest_grad = rest_sum.result()
        placed = scatter(after(place, rest_grad), prompt_index, True, (dx_own,), prompt_rows, step)
        first_sum.gate(rest_grad, *placed)
        sums = first_sum.near_sums()
        first_sum.near(sums)
        sums = first_sum.line_sums()
        first_sum.line(sums)
        dx_recv = (dx_first, swap(after(dx_sends[1], placed[0], *sums)))
        first_grad = first_sum.result()
    else:
        out_recv = swap(out_send)
        rest_grad = reduce_any(grads[0])
        fields = sum(collect([back(half, own_mask) for half in range(2)]), [])
        made = project_back(fast, place, x_own, x_recv, cosine, sine, dhp, weights, fields)
        dx_own, dx_recv = made[0], (swap(made[1]), swap(made[2]))
        placed = scatter(place, prompt_index, True, (dx_own,), prompt_rows, step)
        first_grad = reduce_any(made[3])
        out_prompt, out_cont = unpack(place, prompt_index, out_own, out_recv, prompt_rows, step, BF16)
    dx_prompt, dx_cont = scatter(place, prompt_index, False, dx_recv, prompt_rows, step, placed)
    first_grad = jnp.where(c == 0, first_grad[:, : 3 * columns], first_grad[:, 64:])
    start = 3 * hid
    gain_grads = jnp.where(c == 0, rest_grad[:, start + columns : start + columns + 2], rest_grad[:, start : start + 2])
    out_grad = jnp.where(c == 0, rest_grad[:, start : start + columns], rest_grad[:, start + 64 :])
    return (
        out_prompt,
        out_cont,
        dx_prompt,
        dx_cont,
        gain_grads[:, 0],
        first_grad[:, :columns],
        first_grad[:, 2 * columns :],
        first_grad[:, columns : 2 * columns],
        out_grad.T,
        gain_grads[:, 1],
        rest_grad[:, :hid],
        rest_grad[:, hid : 2 * hid],
        rest_grad[:, 2 * hid : start].T,
    )


def solution(mesh):
    parts = mesh.shape["dp"]
    grid = Mesh(mesh.devices.reshape(parts // 2, 2, 2, 2), ("z", "x", "y", "c"))
    dp, tensor = ("z", "x"), ("y", "c")
    fast = parts == 8
    tokens, columns, rows, vector = P(dp, tensor, None), P(dp, tensor), P(tensor, dp), P(dp)
    in_specs = (
        tokens,
        tokens,
        vector,
        vector,
        columns,
        columns,
        columns,
        rows,
        vector,
        columns,
        columns,
        rows,
        tokens,
        tokens,
    )
    out_specs = (
        tokens,
        tokens,
        tokens,
        tokens,
        vector,
        columns,
        columns,
        columns,
        rows,
        vector,
        columns,
        columns,
        rows,
    )
    return jax.shard_map(
        functools.partial(on_device, fast), mesh=grid, in_specs=in_specs, out_specs=out_specs, check_vma=False
    )
```

```python
import functools
import math

import jax
import jax.numpy as jnp
from jax import lax
from jax.experimental import pallas as pl
from jax.experimental.pallas import tpu as pltpu
from jax.sharding import Mesh
from jax.sharding import PartitionSpec as P

HDIM = 64
NEGATIVE = -1e30
EPSILON = 1e-06
BF16 = jnp.bfloat16
F32 = jnp.float32
LAST = ((1,), (1,))
FIRST = ((0,), (0,))
LIMIT = 64000 * 1024


def dotf(left, right, contract=((1,), (0,))):
    return lax.dot_general(left, right, (contract, ((), ())), preferred_element_type=F32)


def whole(shape=None, space=pltpu.VMEM):
    return pl.BlockSpec(memory_space=space)


def params(limit=LIMIT, **more):
    return pltpu.CompilerParams(vmem_limit_bytes=limit, **more)


def fill_order(index_ref, order_ref, count_ref, groups, total):
    count_ref[0] = 0
    count_ref[1] = 0

    def place(number, carry):
        prompt = index_ref[number]
        seen = count_ref[prompt]
        order_ref[prompt * groups + seen] = number
        count_ref[prompt] = seen + 1
        return carry

    lax.fori_loop(0, total, place, 0)


def pack_kernel(groups, place, index, prompt_x, cont_x, x_own, *refs):
    sends, (order, count) = refs[:-2], refs[-2:]
    rows = prompt_x.shape[1]
    step = cont_x.shape[1]
    fill_order(index, order, count, groups, cont_x.shape[0])
    mine = place[2]
    for which, outs in ((1 - mine, sends), (mine, (x_own,))):
        size = outs[0].shape[0]
        outs[0][0:rows, :] = prompt_x[which]
        for slot in range(groups):
            start = rows + slot * step
            at = slice(start % size, start % size + step)
            outs[start // size][at, :] = cont_x[order[which * groups + slot]]


def pack(place, index, prompt_x, cont_x, pieces):
    groups = cont_x.shape[0] // prompt_x.shape[0]
    count = prompt_x.shape[1] + groups * cont_x.shape[1]
    width = prompt_x.shape[2]
    return pl.pallas_call(
        functools.partial(pack_kernel, groups),
        out_shape=(jax.ShapeDtypeStruct((count, width), BF16),)
        + (jax.ShapeDtypeStruct((count // pieces, width), BF16),) * pieces,
        in_specs=[whole(space=pltpu.SMEM)] * 2 + [whole()] * 2,
        out_specs=(whole(),) * (1 + pieces),
        scratch_shapes=[pltpu.SMEM((2 * groups,), jnp.int32), pltpu.SMEM((2,), jnp.int32)],
        compiler_params=params(),
        name="pack_rows",
    )(place, index, prompt_x, cont_x)


def unpack_kernel(groups, place, index, own, back, prompt_out, cont_out, order, count):
    rows = prompt_out.shape[1]
    step = cont_out.shape[1]
    fill_order(index, order, count, groups, cont_out.shape[0])
    mine = place[2]
    for which, source in ((mine, own), (1 - mine, back)):
        prompt_out[which] = source[0:rows, :].astype(prompt_out.dtype)
        for slot in range(groups):
            piece = source[rows + slot * step : rows + (slot + 1) * step, :]
            cont_out[order[which * groups + slot]] = piece.astype(cont_out.dtype)


def unpack(place, index, own, back, rows, step, dtype):
    conts = index.shape[0]
    groups = conts // 2
    width = own.shape[1]
    return pl.pallas_call(
        functools.partial(unpack_kernel, groups),
        out_shape=(
            jax.ShapeDtypeStruct((2, rows, width), dtype),
            jax.ShapeDtypeStruct((conts, step, width), dtype),
        ),
        in_specs=[whole(space=pltpu.SMEM)] * 2 + [whole()] * 2,
        out_specs=(whole(),) * 2,
        scratch_shapes=[pltpu.SMEM((2 * groups,), jnp.int32), pltpu.SMEM((2,), jnp.int32)],
        compiler_params=params(),
        name="unpack_rows",
    )(place, index, own, back)


def scatter_kernel(groups, parts, own, aliased, place, index, *refs):
    sources, refs = refs[:parts], refs[parts + aliased :]
    prompt_out, cont_out, rows_s, order, count, sems = refs
    rows = prompt_out.shape[1]
    step = cont_out.shape[1]
    fill_order(index, order, count, groups, cont_out.shape[0])
    which = place[2] if own else 1 - place[2]
    size = sources[0].shape[0]
    copies = []
    for number, source in enumerate(sources):
        rows_s[number * size : (number + 1) * size, :] = source[...].astype(F32)
    copies.append(pltpu.make_async_copy(rows_s.at[pl.ds(0, rows), :], prompt_out.at[which], sems.at[0]))
    for slot in range(groups):
        piece = rows_s.at[pl.ds(rows + slot * step, step), :]
        copies.append(pltpu.make_async_copy(piece, cont_out.at[order[which * groups + slot]], sems.at[1 + slot]))
    for copy in copies:
        copy.start()
    for copy in copies:
        copy.wait()


def scatter(place, index, own, sources, rows, step, placed=()):
    conts = index.shape[0]
    groups = conts // 2
    width = sources[0].shape[1]
    aliases = {2 + len(sources) + i: i for i in range(len(placed))}
    return pl.pallas_call(
        functools.partial(scatter_kernel, groups, len(sources), own, len(placed)),
        out_shape=(jax.ShapeDtypeStruct((2, rows, width), F32), jax.ShapeDtypeStruct((conts, step, width), F32)),
        in_specs=[whole(space=pltpu.SMEM)] * 2 + [whole()] * len(sources) + [whole(space=pl.ANY)] * len(placed),
        out_specs=(whole(space=pl.ANY),) * 2,
        scratch_shapes=[
            pltpu.VMEM((rows + groups * step, width), F32),
            pltpu.SMEM((2 * groups,), jnp.int32),
            pltpu.SMEM((2,), jnp.int32),
            pltpu.SemaphoreType.DMA((1 + groups,)),
        ],
        input_output_aliases=aliases,
        compiler_params=params(),
        name="scatter_rows",
    )(place, index, *sources, *placed)


def blocks(fast, place, rows, model):
    if not fast:
        return [(0, (t,), t, 0, model) for t in range(4)]
    z, x, y, c = place[0], place[1], place[2], place[3]
    found = []
    for dc in range(2):
        for half in range(2):
            for near in range(2):
                for far in range(2):
                    kx, ky = (near, far) if half == 0 else (far, near)
                    for k in range(2):
                        t = 2 * (y ^ ky) + (c ^ dc)
                        row = ((z ^ (2 * half + k)) * 2 + (x ^ kx)) * rows
                        found.append((4 * dc + 2 * half + far, (near, k), t, row, rows))
    return found


def weight_copies(fast, place, pieces, held, sems, rows, model, columns=slice(None), base=0):
    copies = []
    for number, (piece, at, t, row, count) in enumerate(blocks(fast, place, rows, model)):
        if fast:
            row = pl.multiple_of(row, rows)
        source = pieces[piece].at[at + (slice(None), columns)]
        copies.append(
            pltpu.make_async_copy(source, held.at[t, pl.ds(row, count), columns], sems.at[base + number])
        )
    return copies


def store_grads(held, out, sems):
    copies = [pltpu.make_async_copy(held.at[t], out.at[t], sems.at[t]) for t in range(4)]
    for copy in copies:
        copy.start()
    for copy in copies:
        copy.wait()


def n_blocks(fast):
    return 32 if fast else 4


def n_pieces(fast):
    return 8 if fast else 1


def n_grads(fast):
    return 6 if fast else 1


def grad_shapes(fast, rows, model, columns):
    if fast:
        part = jax.ShapeDtypeStruct((2, 2, rows, columns), BF16)
        return (jax.ShapeDtypeStruct((2, 2, 2, rows, columns), BF16), part, part) * 2
    return (jax.ShapeDtypeStruct((4, model, columns), BF16),)


SWAP = [(0, 1), (1, 0)]


def over(axis, data):
    return lax.ppermute(data, axis, SWAP)


def over_z(data, k):
    return lax.ppermute(data, "z", [(i, i ^ k) for i in range(4)])


def after(data, *others):
    return lax.optimization_barrier((data,) + others)[0]


def gather_line(shard):
    return [over_z(shard, k) for k in (1, 2, 3)]


def stack_line(shard, got):
    return (jnp.stack([shard, got[0]]), jnp.stack([got[1], got[2]]))


def gather_near(line):
    return (over("x", line[0]), over("y", line[1]))


def stack_near(line, got):
    return tuple(jnp.stack([a, b]) for a, b in zip(line, got))


def gather_far(plane):
    return (over("y", plane[0]), over("x", plane[1]))


def gather_core(plane, far):
    mine = (plane[0], far[0], plane[1], far[1])
    return mine + tuple(over("c", piece) for piece in mine)


def gather_any(shard):
    flat = lax.all_gather(shard, ("z", "x"), axis=0, tiled=True)
    return (lax.all_gather(flat, ("y", "c"), axis=0, tiled=False),)


def total(items):
    return functools.reduce(jnp.add, [item.astype(F32) for item in items])


def add_kernel(terms, *refs):
    inputs = 1 + max(number for blocks in terms for number, _ in blocks)
    ins, refs = refs[:inputs], refs[inputs:]
    outs, refs = refs[: len(terms)], refs[len(terms) :]
    held, made, (in_sems, out_sems) = refs[: len(terms)], refs[len(terms) : 2 * len(terms)], refs[2 * len(terms) :]
    copies = []
    for s, blocks in enumerate(terms):
        row = []
        for i, (number, at) in enumerate(blocks):
            source = ins[number].at[at] if at else ins[number]
            row.append(pltpu.make_async_copy(source, held[s].at[i], in_sems.at[s, i]))
            row[-1].start()
        copies.append(row)
    leaving = []
    for s, blocks in enumerate(terms):
        for copy in copies[s]:
            copy.wait()
        *lead, rows, _ = made[s].shape

        def one(step, carry, s=s, blocks=blocks, lead=lead, rows=rows):
            place, chunk = step // (rows // 32), step % (rows // 32)
            at = (pl.ds(pl.multiple_of(chunk * 32, 32), 32), slice(None))
            if len(lead) == 1:
                at = (place,) + at
            if len(lead) == 2:
                at = (place // lead[1], place % lead[1]) + at
            if len(blocks) == 2:
                made[s][at] = held[s][(0,) + at] + held[s][(1,) + at]
            else:
                made[s][at] = total([held[s][(i,) + at] for i in range(len(blocks))]).astype(BF16)
            return carry

        lax.fori_loop(0, math.prod(lead) * (rows // 32), one, 0)
        leaving.append(pltpu.make_async_copy(made[s], outs[s], out_sems.at[s]))
        leaving[-1].start()
    for copy in leaving:
        copy.wait()


def add_blocks(sums):
    arrays, terms = [], []
    for blocks in sums:
        row = []
        for data, at in blocks:
            found = [i for i, other in enumerate(arrays) if other is data]
            if not found:
                arrays.append(data)
                found = [len(arrays) - 1]
            row.append((found[0], at))
        terms.append(tuple(row))
    shapes = [blocks[0][0].shape[len(blocks[0][1]) :] for blocks in sums]
    most = max(len(blocks) for blocks in sums)
    return pl.pallas_call(
        functools.partial(add_kernel, tuple(terms)),
        out_shape=tuple(jax.ShapeDtypeStruct(shape, BF16) for shape in shapes),
        in_specs=[whole(space=pl.ANY)] * len(arrays),
        out_specs=(whole(space=pl.ANY),) * len(sums),
        scratch_shapes=[pltpu.VMEM((len(blocks),) + shape, BF16) for blocks, shape in zip(sums, shapes)]
        + [pltpu.VMEM(shape, BF16) for shape in shapes]
        + [pltpu.SemaphoreType.DMA((len(sums), most)), pltpu.SemaphoreType.DMA((len(sums),))],
        compiler_params=params(),
        name="add_blocks",
    )(*arrays)


def add_here(sums):
    return [total([data[at] for data, at in blocks]).astype(BF16) for blocks in sums]


class Reduction:
    def __init__(self, grads, large):
        self.add = add_blocks if large else add_here
        self.keep = (grads[0], grads[3])
        self.away = (grads[2], grads[5])
        self.from_core = [over("c", grads[1]), over("c", grads[4])]

    def gate(self, *others):
        self.got = after(self.got, *others)

    def far_sums(self):
        sums = self.add([[(self.keep[half], (1,)), (self.from_core[half], ())] for half in range(2)])
        self.from_core = [over("c", part) for part in after(self.away, *sums)]
        return sums

    def far(self, sums):
        self.got = [over(axis, s) for axis, s in zip(("y", "x"), sums)]

    def near_sums(self):
        self.from_far = self.got
        return self.add(
            [
                [(self.keep[half], (0, 1)), (self.from_core[half], (1,)), (self.from_far[half], (1,))]
                for half in range(2)
            ]
        )

    def near(self, sums):
        self.got = [over(axis, s) for axis, s in zip(("x", "y"), sums)]

    def block(self, half, k):
        return [
            (self.keep[half], (0, 0, k)),
            (self.from_core[half], (0, k)),
            (self.from_far[half], (0, k)),
            (self.from_near[half], (k,)),
        ]

    def line_sums(self):
        self.from_near = self.got
        return self.add([self.block(half, k) for half, k in ((0, 1), (1, 0), (1, 1))])

    def line(self, sums):
        self.got = [over_z(s, k) for k, s in zip((1, 2, 3), sums)]

    def result(self):
        return total([data[at] for data, at in self.block(0, 0)] + list(self.got))


def reduce_any(out):
    mine = lax.psum_scatter(out, ("y", "c"), scatter_dimension=0, tiled=False)
    return lax.psum_scatter(mine, ("z", "x"), scatter_dimension=0, tiled=True).astype(F32)


def left_lanes(rows):
    return lax.broadcasted_iota(jnp.int32, (rows, 128), 1) < HDIM


def flip(tile):
    return pltpu.roll(tile, HDIM, 1)


def tile(data, number):
    return data[:, number * 128 : (number + 1) * 128]


def join_first(even, odd):
    left = left_lanes(even.shape[0])
    e = [tile(even, i) for i in range(5)]
    o = [tile(odd, i) for i in range(5)]
    query = [e[0], jnp.where(left, e[1], o[0]), o[1]]
    key = [e[3], jnp.where(left, e[4], o[3]), o[4]]
    e1, e2, o2, o3 = flip(e[1]), flip(e[2]), flip(o[2]), flip(o[3])
    value = [jnp.where(left, e1, e2), jnp.where(left, e2, o2), jnp.where(left, o2, o3)]
    return query + key + value


def split_first(query, key, value):
    left = left_lanes(query[0].shape[0])
    none = jnp.zeros_like(query[0])
    v = [flip(t) for t in value]
    even = [
        query[0],
        jnp.where(left, query[1], v[0]),
        jnp.where(left, v[0], v[1]),
        key[0],
        jnp.where(left, key[1], none),
    ]
    odd = [
        jnp.where(left, none, query[1]),
        query[2],
        jnp.where(left, v[1], v[2]),
        jnp.where(left, v[2], key[1]),
        key[2],
    ]
    return even, odd


def turn(field, first):
    width = field.shape[-1]
    return jnp.where(first, pltpu.roll(field, width - HDIM // 2, 1), pltpu.roll(field, HDIM // 2, 1))


def first_half(shape):
    return lax.broadcasted_iota(jnp.int32, shape, 1) % HDIM < HDIM // 2


def qkv_kernel(fast, place, x_own, x_recv, cosine, sine, *refs):
    pieces = refs[: n_pieces(fast)]
    *results, gains, weights_out, q, k, v, weights, held, sems, out_sems = refs[n_pieces(fast) :]
    rows, model = x_own.shape
    per = model // 8 if fast else model

    def leave(half):
        return [
            pltpu.make_async_copy(made.at[half], result.at[half], out_sems.at[half, i])
            for i, (made, result) in enumerate(zip((q, k, v, weights), results + [weights_out]))
        ]

    copies = weight_copies(fast, place, pieces, held, sems, per, model)
    for copy in copies:
        copy.start()
    for copy in copies:
        copy.wait()
    gains[...] = jnp.transpose(held[0, :, 512:640].astype(F32))[64:72, :]
    side = place[2]
    first = first_half((rows, 128))

    def one(half, carry):
        def join(i, carry):
            at = pl.ds(pl.multiple_of(i * 96, 96), 96)
            for number, made in enumerate(join_first(held[2 * half, at, :], held[2 * half + 1, at, :])):
                weights[half, at, number * 128 : (number + 1) * 128] = made
            return carry

        lax.fori_loop(0, model // 96, join, 0)
        for x, where in ((x_own, side), (x_recv, 1 - side)):
            at = pl.ds(pl.multiple_of(where * rows, rows), rows)
            cos, sin = cosine[at, :], sine[at, :]
            made = dotf(x[...], weights[half])
            for p in range(3):
                lanes = slice(p * 128, (p + 1) * 128)
                u = tile(made, p)
                q[half, at, lanes] = ((u * cos + turn(u, first) * sin).astype(BF16) * 0.125).astype(BF16)
                u = tile(made, 3 + p)
                k[half, at, lanes] = (u * cos + turn(u, first) * sin).astype(BF16)
                v[half, at, lanes] = tile(made, 6 + p).astype(BF16)
        for copy in leave(half):
            copy.start()
        return carry

    lax.fori_loop(0, 2, one, 0)
    for half in range(2):
        for copy in leave(half):
            copy.wait()


def project(fast, place, x_own, x_recv, cosine, sine, pieces):
    rows, model = x_own.shape
    field = jax.ShapeDtypeStruct((2, 2 * rows, 384), BF16)
    return pl.pallas_call(
        functools.partial(qkv_kernel, fast),
        out_shape=(field,) * 3
        + (jax.ShapeDtypeStruct((8, model), F32), jax.ShapeDtypeStruct((2, model, 1152), BF16)),
        in_specs=[whole(space=pltpu.SMEM)] + [whole()] * 4 + [whole(space=pl.ANY)] * len(pieces),
        out_specs=(whole(space=pl.ANY),) * 3 + (whole(), whole(space=pl.ANY)),
        scratch_shapes=[pltpu.VMEM((2, 2 * rows, 384), BF16)] * 3
        + [
            pltpu.VMEM((2, model, 1152), BF16),
            pltpu.VMEM((4, model, 640), BF16),
            pltpu.SemaphoreType.DMA((n_blocks(fast),)),
            pltpu.SemaphoreType.DMA((2, 4)),
        ],
        compiler_params=params(),
        name="project_qkv",
    )(place, x_own, x_recv, cosine, sine, *pieces)


class Layout:
    def __init__(self, rows, prompt, step):
        self.rows = rows
        self.prompt = prompt
        self.step = step
        self.pair = 2 * step
        self.cont_blocks = (rows - prompt) // (4 * step)
        self.width = 8 * step


def pair_rows(ref, lay, start):
    return (ref[pl.ds(start, lay.pair), :], ref[pl.ds(lay.rows + start, lay.pair), :])


def pair_start(lay, block, pair):
    return lay.prompt + (2 * block + pair) * lay.pair


def cont_query(ref, lay, block):
    parts = []
    for pair in range(2):
        parts += pair_rows(ref, lay, pair_start(lay, block, pair))
    return jnp.concatenate(parts, 0)


def cont_keys(own, other, lay, block, pair):
    start = pair_start(lay, block, pair)
    return jnp.concatenate(pair_rows(own, lay, start) + pair_rows(other, lay, start), 0)


def causal(count, key_axis):
    key = lax.broadcasted_iota(jnp.int32, (count, count), key_axis)
    row = lax.broadcasted_iota(jnp.int32, (count, count), 1 - key_axis)
    return jnp.where(key <= row, 0.0, NEGATIVE)


def shared_segments(lay):
    return [(0, 0), (0, lay.rows), (1, 0), (1, lay.rows)]


def attend_kernel(lay, place, q_ref, ko, vo, kp, vp, own_mask, mixed, lse, lse_s):
    inner = place[2] != place[3]
    q, keys, values, out = q_ref.at[0], (ko.at[0], kp.at[0]), (vo.at[0], vp.at[0]), mixed.at[0]
    count, width = lay.prompt, lay.width
    half = width // 2
    lane = lax.broadcasted_iota(jnp.int32, (1, 128), 1) // HDIM
    spot = lax.broadcasted_iota(jnp.int32, (1, 128), 1)
    low, high = pl.ds(0, count), pl.ds(lay.rows, count)
    extra = pl.ds(pl.multiple_of(jnp.where(inner, 0, lay.rows), lay.rows), count)
    out[...] = jnp.zeros_like(out)
    lse_s[...] = jnp.zeros_like(lse_s)

    def top(scores):
        return jnp.max(functools.reduce(jnp.maximum, scores), 1, keepdims=True)

    def sums(raised):
        return jnp.sum(functools.reduce(jnp.add, raised), 1, keepdims=True)

    def head(j, carry):
        chosen = lane == j

        def pick(block):
            return jnp.where(chosen, block, jnp.zeros_like(block))

        def finish(at, made, total, highest, number):
            out[at, :] = out[at, :] + pick(made / total).astype(BF16)
            here = pl.ds(number, made.shape[0])
            lse_s[here, :] = jnp.where(spot == j, highest + jnp.log(total), lse_s[here, :])

        q_low, q_high = pick(q[low, :]), pick(q[high, :])
        q_extra = jnp.where(inner, q_low, q_high)
        mask = causal(count, 1)
        s_low = dotf(q_low, keys[0][low, :], LAST) + mask
        s_high = [
            dotf(q_high, keys[0][high, :], LAST) + mask,
            dotf(q_high, keys[0][low, :], LAST),
            dotf(q_high, keys[1][low, :], LAST),
        ]
        s_extra = dotf(q_extra, keys[1][extra, :], LAST)
        s_cont = []
        for block in range(lay.cont_blocks):
            query = pick(cont_query(q, lay, block))
            scores = [dotf(query, keys[o][pl.ds(start, count), :], LAST) for o, start in shared_segments(lay)]
            own = []
            for pair in range(2):
                rows = query[pair * half : (pair + 1) * half, :]
                own.append(dotf(rows, cont_keys(keys[0], keys[1], lay, block, pair), LAST) + own_mask[...])
            s_cont.append(scores + [jnp.concatenate(own, 0)])

        m_low, m_high, m_extra = top([s_low]), top(s_high), top([s_extra])
        m_low = jnp.maximum(m_low, jnp.where(inner, m_extra, NEGATIVE))
        m_high = jnp.maximum(m_high, jnp.where(inner, NEGATIVE, m_extra))
        p_low = jnp.exp(s_low - m_low)
        p_high = [jnp.exp(s - m_high) for s in s_high]
        p_extra = jnp.exp(s_extra - jnp.where(inner, m_low, m_high))
        l_extra = sums([p_extra])
        l_low = sums([p_low]) + jnp.where(inner, l_extra, 0.0)
        l_high = sums(p_high) + jnp.where(inner, 0.0, l_extra)
        o_extra = dotf(p_extra.astype(BF16), values[1][extra, :])
        o_low = dotf(p_low.astype(BF16), values[0][low, :]) + jnp.where(inner, o_extra, 0.0)
        o_high = (
            dotf(p_high[0].astype(BF16), values[0][high, :])
            + dotf(p_high[1].astype(BF16), values[0][low, :])
            + dotf(p_high[2].astype(BF16), values[1][low, :])
            + jnp.where(inner, 0.0, o_extra)
        )
        finish(low, o_low, l_low, m_low, 0)
        finish(high, o_high, l_high, m_high, count)

        for block, scores in enumerate(s_cont):
            highest = top(scores)
            raised = [jnp.exp(s - highest) for s in scores]
            total = sums(raised)
            raised = [r.astype(BF16) for r in raised]
            made = functools.reduce(
                jnp.add, [dotf(r, values[o][pl.ds(start, count), :]) for r, (o, start) in zip(raised, shared_segments(lay))]
            )
            for pair in range(2):
                cut = slice(pair * half, (pair + 1) * half)
                part = made[cut, :] + dotf(raised[-1][cut, :], cont_keys(values[0], values[1], lay, block, pair))
                part = pick(part / total[cut, :]).astype(BF16)
                start = pair_start(lay, block, pair)
                for side in range(2):
                    at = pl.ds(side * lay.rows + start, lay.pair)
                    out[at, :] = out[at, :] + part[side * lay.pair : (side + 1) * lay.pair, :]
            here = pl.ds(2 * count + block * width, width)
            lse_s[here, :] = jnp.where(spot == j, highest + jnp.log(total), lse_s[here, :])
        return carry

    lax.fori_loop(0, 2, head, 0)
    lse[0, 0] = jnp.transpose(lse_s[...])[0:8, :]


def attend(lay, place, q, ko, vo, kp, vp, own_mask):
    total = q.shape[1]
    field = pl.BlockSpec((1, total, 128), lambda h, p, place: (h, 0, p))
    return pl.pallas_call(
        functools.partial(attend_kernel, lay),
        out_shape=(jax.ShapeDtypeStruct(q.shape, BF16), jax.ShapeDtypeStruct((2, 3, 8, total), F32)),
        grid_spec=pltpu.PrefetchScalarGridSpec(
            num_scalar_prefetch=1,
            grid=(2, 3),
            in_specs=[field] * 5 + [pl.BlockSpec(own_mask.shape, lambda h, p, place: (0, 0))],
            out_specs=(field, pl.BlockSpec((1, 1, 8, total), lambda h, p, place: (h, p, 0, 0))),
            scratch_shapes=[pltpu.VMEM((total, 128), F32)],
        ),
        compiler_params=params(),
        name="attend",
    )(place, q, ko, vo, kp, vp, own_mask)


def attend_back_kernel(
    lay, place, q_ref, ko, vo, kp, vp, mixed, up_ref, lse_ref, own_mask, dq, dko, dvo, dkp, dvp, kacc, vacc, qacc, delta_s
):
    inner = place[2] != place[3]
    q, keys, values = q_ref.at[0], (ko.at[0], kp.at[0]), (vo.at[0], vp.at[0])
    upstream, result, lse = up_ref.at[0], mixed.at[0], lse_ref.at[0]
    count, width = lay.prompt, lay.width
    half = width // 2
    lane = lax.broadcasted_iota(jnp.int32, (1, 128), 1) // HDIM
    kacc[...] = jnp.zeros_like(kacc)
    vacc[...] = jnp.zeros_like(vacc)
    qacc[...] = jnp.zeros_like(qacc)
    low, high = pl.ds(0, count), pl.ds(lay.rows, count)
    shift = jnp.where(inner, 0, 1)
    extra = pl.ds(pl.multiple_of(shift * lay.rows, lay.rows), count)
    either = pl.ds(pl.multiple_of(shift * count, count), count)

    def cont_rows(ref):
        return jnp.concatenate([cont_query(ref, lay, block) for block in range(lay.cont_blocks)], 0)

    def product(rows):
        return rows(upstream).astype(F32) * rows(result).astype(F32)

    heads = jnp.where(
        lax.broadcasted_iota(jnp.int32, (8, 128), 1) // HDIM == lax.broadcasted_iota(jnp.int32, (8, 128), 0), 1.0, 0.0
    ).astype(BF16)
    for at, rows in (
        (slice(0, count), lambda ref: ref[low, :]),
        (slice(count, 2 * count), lambda ref: ref[high, :]),
        (slice(2 * count, 2 * count + lay.cont_blocks * width), cont_rows),
    ):
        made = product(rows)
        coarse = made.astype(BF16)
        fine = (made - coarse.astype(F32)).astype(BF16)
        delta_s[:, at] = dotf(heads, coarse, LAST) + dotf(heads, fine, LAST)

    def head(j, carry):
        chosen = lane == j
        me = pl.ds(j, 1)

        def pick(block):
            return jnp.where(chosen, block, jnp.zeros_like(block))

        def back(key, value, query, grads, mask, log_total, delta):
            s = dotf(key, query, LAST)
            if mask is not None:
                s = s + mask
            share = jnp.exp(s - log_total)
            d = (share * (dotf(value, grads, LAST) - delta)).astype(BF16)
            return dotf(share.astype(BF16), grads), dotf(d, query), dotf(d, key, FIRST)

        def put(other, at, dv, dk):
            vacc[other, at, :] += dv
            kacc[other, at, :] += dk

        query, grads = pick(cont_rows(q)), pick(cont_rows(upstream))
        at = pl.ds(2 * count, lay.cont_blocks * width)
        log_total, delta = lse[0, me, at], delta_s[me, at]
        shared = shared_segments(lay)
        key = jnp.concatenate([keys[o][pl.ds(start, count), :] for o, start in shared], 0)
        value = jnp.concatenate([values[o][pl.ds(start, count), :] for o, start in shared], 0)
        dv, dk, total = back(key, value, query, grads, None, log_total, delta)
        for number, (other, start) in enumerate(shared):
            piece = slice(number * count, (number + 1) * count)
            put(other, pl.ds(start, count), dv[piece, :], dk[piece, :])
        for number in range(2 * lay.cont_blocks):
            block, pair = number // 2, number % 2
            cut = slice(number * half, (number + 1) * half)
            dv, dk, made = back(
                cont_keys(keys[0], keys[1], lay, block, pair),
                cont_keys(values[0], values[1], lay, block, pair),
                query[cut, :],
                grads[cut, :],
                own_mask[...],
                log_total[:, cut],
                delta[:, cut],
            )
            start = pair_start(lay, block, pair)
            for part in range(4):
                piece = slice(part * lay.pair, (part + 1) * lay.pair)
                put(part // 2, pl.ds((part % 2) * lay.rows + start, lay.pair), dv[piece, :], dk[piece, :])
            made = pick(total[cut, :] + made)
            for part in range(2):
                spot = pl.ds(part * lay.rows + start, lay.pair)
                qacc[spot, :] += made[part * lay.pair : (part + 1) * lay.pair, :]
        mask = causal(count, 0)
        at = pl.ds(count, count)
        query, grads, log_total, delta = pick(q[high, :]), pick(upstream[high, :]), lse[0, me, at], delta_s[me, at]
        seen = ((0, high), (0, low), (1, low))
        key = jnp.concatenate([keys[o][spot, :] for o, spot in seen], 0)
        value = jnp.concatenate([values[o][spot, :] for o, spot in seen], 0)
        tall = jnp.concatenate([mask, jnp.zeros((2 * count, count), F32)], 0)
        dv, dk, made = back(key, value, query, grads, tall, log_total, delta)
        for number, (other, spot) in enumerate(seen):
            piece = slice(number * count, (number + 1) * count)
            put(other, spot, dv[piece, :], dk[piece, :])
        qacc[high, :] += pick(made)
        at = pl.ds(0, count)
        dv, dk, made = back(
            keys[0][low, :],
            values[0][low, :],
            pick(q[low, :]),
            pick(upstream[low, :]),
            mask,
            lse[0, me, at],
            delta_s[me, at],
        )
        put(0, low, dv, dk)
        qacc[low, :] += pick(made)
        dv, dk, made = back(
            keys[1][extra, :],
            values[1][extra, :],
            pick(q[extra, :]),
            pick(upstream[extra, :]),
            None,
            lse[0, me, either],
            delta_s[me, either],
        )
        put(1, extra, dv, dk)
        qacc[extra, :] += pick(made)
        return carry

    lax.fori_loop(0, 2, head, 0)
    dq[...] = (qacc[...] * 0.125).astype(BF16)
    dko[...] = kacc[0].astype(BF16)
    dkp[...] = kacc[1].astype(BF16)
    dvo[...] = vacc[0].astype(BF16)
    dvp[...] = vacc[1].astype(BF16)


def attend_back(lay, place, half, q, ko, vo, kp, vp, mixed, upstream, lse, own_mask):
    total = q.shape[1]
    field = pl.BlockSpec((1, total, 128), lambda p, place: (half, 0, p))
    made = pl.BlockSpec((total, 128), lambda p, place: (0, p))
    return pl.pallas_call(
        functools.partial(attend_back_kernel, lay),
        out_shape=(jax.ShapeDtypeStruct((total, 384), BF16),) * 5,
        grid_spec=pltpu.PrefetchScalarGridSpec(
            num_scalar_prefetch=1,
            grid=(3,),
            in_specs=[field] * 7
            + [
                pl.BlockSpec((1, 1, 8, total), lambda p, place: (half, p, 0, 0)),
                pl.BlockSpec(own_mask.shape, lambda p, place: (0, 0)),
            ],
            out_specs=(made,) * 5,
            scratch_shapes=[
                pltpu.VMEM((2, total, 128), F32),
                pltpu.VMEM((2, total, 128), F32),
                pltpu.VMEM((total, 128), F32),
                pltpu.VMEM((8, total), F32),
            ],
        ),
        compiler_params=params(),
        name="attend_back",
    )(place, q, ko, vo, kp, vp, mixed, upstream, lse, own_mask)


def middle_kernel(fast, hid, place, mixed, xo, xr, dyo, dyr_a, dyr_b, gains, *refs):
    count = n_pieces(fast)
    pieces, refs = refs[:count], refs[count:]
    (out_own, out_send, dhp, dmixed), refs = refs[:4], refs[4:]
    count = n_grads(fast)
    grads, refs = refs[:count], refs[count:]
    held, wide_o, gate_s, up_s, hid_s, dgate_s, dup_s, low_t, fed_t, att_t, gain_acc, sum_s, sems = refs
    step = pl.program_id(0)
    model = held.shape[1]
    rows = xo.shape[0]
    per = model // 8 if fast else model
    G, U, D, O = slice(0, hid), slice(hid, 2 * hid), slice(2 * hid, 3 * hid), 3 * hid
    side = jnp.where(step == 0, place[2], 1 - place[2])
    here = pl.ds(pl.multiple_of(side * rows, rows), rows)
    left = left_lanes(model)
    out_copies = weight_copies(fast, place, pieces, held, sems, per, model, slice(O, O + 256))
    other_copies = weight_copies(fast, place, pieces, held, sems, per, model, slice(0, O), n_blocks(fast))

    @pl.when(step == 0)
    def _():
        for copy in out_copies + other_copies:
            copy.start()
        gain_acc[...] = jnp.zeros_like(gain_acc)
        for copy in out_copies:
            copy.wait()
        for half in range(2):
            even, odd = held.at[2 * half], held.at[2 * half + 1]
            wide_o[half, :, 0:128] = even[:, O : O + 128]
            wide_o[half, :, 128:256] = jnp.where(left, even[:, O + 128 : O + 256], odd[:, O : O + 128])
            wide_o[half, :, 256:384] = odd[:, O + 128 : O + 256]

    own = step == 0
    gain_a = gains[0:1, :]
    gain_f = gains[1:2, :]
    pre = jnp.where(own, xo[...], xr[...]).astype(F32)
    for half in range(2):
        pre = pre + dotf(mixed[half, here, :], wide_o[half], LAST)
    scale1 = lax.rsqrt(jnp.mean(pre * pre, -1, keepdims=True) + EPSILON)
    norm1 = pre * scale1
    normed = norm1 * gain_a
    low = normed.astype(BF16)
    low_t[step] = jnp.transpose(low)
    spot = pl.ds(pl.multiple_of(step * rows, rows), rows)

    @pl.when(step == 0)
    def _():
        for copy in other_copies:
            copy.wait()

    def forward(t, carry):
        gate = dotf(low, held[t, :, G])
        up = dotf(low, held[t, :, U])
        gate_s[t] = gate
        up_s[t] = up
        hid_s[t, spot, :] = (gate * jax.nn.sigmoid(gate) * up).astype(BF16)
        return carry

    def add_over(fields, columns):
        field = jnp.concatenate([fields[t, spot, :] for t in range(4)], 1)

        def chunk(n, carry):
            at = pl.ds(pl.multiple_of(n * 256, 256), 256)
            weight = jnp.concatenate([held[t, at, columns] for t in range(4)], 1)
            sum_s[:, at] = sum_s[:, at] + dotf(field, weight, LAST)
            return carry

        lax.fori_loop(0, model // 256, chunk, 0)

    lax.fori_loop(0, 4, forward, 0)
    sum_s[...] = normed
    add_over(hid_s, D)
    resid = sum_s[...]
    scale2 = lax.rsqrt(jnp.mean(resid * resid, -1, keepdims=True) + EPSILON)
    norm2 = resid * scale2
    result = (norm2 * gain_f).astype(BF16)

    @pl.when(own)
    def _():
        out_own[...] = result

    @pl.when(jnp.logical_not(own))
    def _():
        out_send[...] = result

    dy = jnp.where(own, dyo[...], jnp.concatenate([dyr_a[...], dyr_b[...]], 0)).astype(F32)
    gain_acc[1:2, :] += jnp.sum(dy * norm2, 0, keepdims=True)
    e2 = dy * gain_f
    d_resid = scale2 * (e2 - norm2 * jnp.mean(e2 * norm2, -1, keepdims=True))
    d_fed = d_resid.astype(BF16)
    fed_t[step] = jnp.transpose(d_fed)

    def backward(t, carry):
        gate, up = gate_s[t], up_s[t]
        d_hidden = dotf(d_fed, held[t, :, D])
        sig = jax.nn.sigmoid(gate)
        dgate_s[t, spot, :] = (d_hidden * up * sig * (1.0 + gate * (1.0 - sig))).astype(BF16)
        dup_s[t, spot, :] = (d_hidden * gate * sig).astype(BF16)
        return carry

    lax.fori_loop(0, 4, backward, 0)
    sum_s[...] = d_resid
    add_over(dgate_s, G)
    add_over(dup_s, U)
    d_normed = sum_s[...]
    gain_acc[0:1, :] += jnp.sum(d_normed * norm1, 0, keepdims=True)
    e1 = d_normed * gain_a
    d_pre = scale1 * (e1 - norm1 * jnp.mean(e1 * norm1, -1, keepdims=True))
    dhp[...] = d_pre
    d_att = d_pre.astype(BF16)
    att_t[step] = jnp.transpose(d_att)
    for half in range(2):
        dmixed[half] = dotf(d_att, wide_o[half]).astype(BF16)

    @pl.when(step == 1)
    def _():
        columns = jnp.transpose(jnp.broadcast_to(gain_acc[0:8, :], (8, model)))
        lane = lax.broadcasted_iota(jnp.int32, (model, 128), 1) % HDIM
        extra = jnp.where(lane == 0, columns[:, 0:1], jnp.where(lane == 1, columns[:, 1:2], 0.0))
        halves = (place[2], 1 - place[2])
        for half in range(2):
            made = None
            for part in range(2):
                at = pl.ds(pl.multiple_of(halves[part] * rows, rows), rows)
                more = dotf(att_t[part], mixed[half, at, :])
                made = more if made is None else made + more
            even, odd = held.at[2 * half], held.at[2 * half + 1]
            even[:, O : O + 128] = tile(made, 0).astype(BF16)
            even[:, O + 128 : O + 256] = jnp.where(left, tile(made, 1), extra).astype(BF16)
            odd[:, O : O + 128] = jnp.where(left, extra, tile(made, 1)).astype(BF16)
            odd[:, O + 128 : O + 256] = tile(made, 2).astype(BF16)

        def weight(r, carry):
            t = 2 * (place[2] ^ (r // 2)) + (place[3] ^ (r % 2)) if fast else r
            for columns, first, second in ((D, fed_t, hid_s), (G, low_t, dgate_s), (U, low_t, dup_s)):
                made = dotf(first[0], second[t, 0:rows, :]) + dotf(first[1], second[t, rows : 2 * rows, :])
                held[t, :, columns] = made.astype(BF16)
            if fast:
                for dc in range(2):

                    @pl.when(r % 2 == dc)
                    def _(dc=dc):
                        send_block(place, r // 2, dc, held, grads, sems, per, True)

            return carry

        lax.fori_loop(0, 4, weight, 0)
        if fast:
            for r in range(4):
                send_block(place, r // 2, r % 2, held, grads, sems, per, False)
        else:
            store_grads(held, grads[0], sems)


def send_block(place, ky, dc, held, targets, sems, rows, start):
    z, x, y, c = place[0], place[1], place[2], place[3]
    t = 2 * (y ^ ky) + (c ^ dc)

    def move(target, row, number):
        copy = pltpu.make_async_copy(held.at[t, pl.ds(row, rows), :], target, sems.at[number])
        if start:
            copy.start()
        else:
            copy.wait()

    for kz in range(4):
        for kx in range(2):
            half, k = kz // 2, kz % 2
            far, near = (ky, kx) if half == 0 else (kx, ky)
            row = pl.multiple_of(((z ^ kz) * 2 + (x ^ kx)) * rows, rows)
            number = 16 * dc + 8 * ky + 2 * kz + kx
            keep, first, second = targets[3 * half : 3 * half + 3]
            if dc == 0:
                move(keep.at[far, near, k], row, number)
            elif half == 1 or not start:
                move((second, first)[far if half == 1 else 0].at[near, k], row, number)
            else:
                for value, target in ((1, first), (0, second)):

                    @pl.when(far == value)
                    def _(target=target, row=row, number=number, near=near, k=k):
                        move(target.at[near, k], row, number)


def once(shape, index=None):
    return pl.BlockSpec(shape, index or (lambda i, place: (0,) * len(shape)), pipeline_mode=pl.Buffered(1))


def middle(fast, place, mixed, xo, xr, dyo, dyr, gains, pieces, hid):
    rows, model = xo.shape
    columns = 3 * hid + 256
    grads = grad_shapes(fast, model // 8 if fast else model, model, columns)

    def side_at(i, place):
        return (0, jnp.where(i == 0, place[2], 1 - place[2]), 0)

    half_rows = once((rows, model))
    field = once((2, 2 * rows, 384))
    return pl.pallas_call(
        functools.partial(middle_kernel, fast, hid),
        out_shape=(
            jax.ShapeDtypeStruct((rows, model), BF16),
            jax.ShapeDtypeStruct((rows, model), BF16),
            jax.ShapeDtypeStruct((2 * rows, model), F32),
            jax.ShapeDtypeStruct(mixed.shape, BF16),
        )
        + grads,
        grid_spec=pltpu.PrefetchScalarGridSpec(
            num_scalar_prefetch=1,
            grid=(2,),
            in_specs=[field]
            + [half_rows] * 3
            + [once((rows // 2, model))] * 2
            + [once((8, model))]
            + [whole(space=pl.ANY)] * len(pieces),
            out_specs=(
                pl.BlockSpec((rows, model), lambda i, place: (0, 0)),
                pl.BlockSpec((rows, model), lambda i, place: (0, 0)),
                pl.BlockSpec((rows, model), lambda i, place: (i, 0)),
                pl.BlockSpec((2, rows, 384), side_at),
            )
            + (whole(space=pl.ANY),) * len(grads),
            scratch_shapes=[
                pltpu.VMEM((4, model, columns), BF16),
                pltpu.VMEM((2, model, 384), BF16),
                pltpu.VMEM((4, rows, hid), F32),
                pltpu.VMEM((4, rows, hid), F32),
                pltpu.VMEM((4, 2 * rows, hid), BF16),
                pltpu.VMEM((4, 2 * rows, hid), BF16),
                pltpu.VMEM((4, 2 * rows, hid), BF16),
                pltpu.VMEM((2, model, rows), BF16),
                pltpu.VMEM((2, model, rows), BF16),
                pltpu.VMEM((2, model, rows), BF16),
                pltpu.VMEM((8, model), F32),
                pltpu.VMEM((rows, model), F32),
                pltpu.SemaphoreType.DMA((2 * n_blocks(fast),)),
            ],
        ),
        compiler_params=params(),
        name="middle",
    )(place, mixed, xo, xr, dyo, *dyr, gains, *pieces)


def qkv_back_kernel(fast, place, x_own, x_recv, cosine, sine, dhp_ref, weights_ref, *refs):
    fields = [refs[2 * i : 2 * i + 2] for i in range(5)]
    dx_own, dx_sends = refs[10], refs[11:13]
    grads, refs = refs[13 : 13 + n_grads(fast)], refs[13 + n_grads(fast) :]
    held, joined, made, x_t, dx, base, weights, moved, sems, extra_sems = refs
    rows, model = x_own.shape
    per = model // 8 if fast else model
    side = place[2]
    first = first_half((rows, 128))
    copies = [pltpu.make_async_copy(dhp_ref, base, extra_sems.at[0])]
    for half in range(2):
        copies.append(pltpu.make_async_copy(weights_ref.at[half], weights.at[half], extra_sems.at[1 + 6 * half]))
        for i in range(5):
            copies.append(pltpu.make_async_copy(fields[i][half], moved.at[half, i], extra_sems.at[2 + i + 6 * half]))
    for copy in copies[1:] + copies[:1]:
        copy.start()
    for number, x in enumerate((x_own, x_recv)):
        x_t[number] = jnp.transpose(x[...])
    for copy in copies[1:7]:
        copy.wait()
    dx[...] = jnp.zeros_like(dx)

    def one(half, carry):
        @pl.when(half == 1)
        def _():
            for copy in copies[7:]:
                copy.wait()

        def turn_back(number, carry):
            at = pl.ds(pl.multiple_of((side ^ number) * rows, rows), rows)
            cos, sin = cosine[at, :], sine[at, :]
            for p in range(3):
                lanes = slice(p * 128, (p + 1) * 128)
                query, key, value, key_more, value_more = [moved[half, i, at, lanes].astype(F32) for i in range(5)]
                joined[number, 0, :, lanes] = (query * cos - turn(query, first) * sin).astype(BF16)
                key = key + key_more
                joined[number, 1, :, lanes] = (key * cos - turn(key, first) * sin).astype(BF16)
                joined[number, 2, :, lanes] = (value + value_more).astype(BF16)
            whole_row = jnp.concatenate([joined[number, kind] for kind in range(3)], 1)
            spot = pl.ds(pl.multiple_of(number * rows, rows), rows)
            dx[spot, :] = dx[spot, :] + dotf(whole_row, weights[half], LAST)
            return carry

        def weight(kind, carry):
            made[kind] = (dotf(x_t[0], joined[0, kind]) + dotf(x_t[1], joined[1, kind])).astype(BF16)
            return carry

        lax.fori_loop(0, 2, turn_back, 0)
        lax.fori_loop(0, 3, weight, 0)

        def split(i, carry):
            at = pl.ds(pl.multiple_of(i * 96, 96), 96)
            even, odd = split_first(*[[tile(made[kind, at, :], p) for p in range(3)] for kind in range(3)])
            for p in range(5):
                held[2 * half, at, p * 128 : (p + 1) * 128] = even[p]
                held[2 * half + 1, at, p * 128 : (p + 1) * 128] = odd[p]
            return carry

        lax.fori_loop(0, model // 96, split, 0)
        if fast:
            for dc in range(2):
                send_block(place, side ^ half, dc, held, grads, sems, per, True)
        return carry

    lax.fori_loop(0, 2, one, 0)
    copies[0].wait()
    dx_own[...] = dx[0:rows, :] + base[0:rows, :]
    for number in range(2):
        cut = slice(rows + number * (rows // 2), rows + (number + 1) * (rows // 2))
        dx_sends[number][...] = (dx[cut, :] + base[cut, :]).astype(BF16)
    if fast:
        for half in range(2):
            for dc in range(2):
                send_block(place, side ^ half, dc, held, grads, sems, per, False)
    else:
        store_grads(held, grads[0], sems)


def project_back(fast, place, x_own, x_recv, cosine, sine, dhp, weights, fields):
    rows, model = x_own.shape
    grads = grad_shapes(fast, model // 8 if fast else model, model, 640)
    return pl.pallas_call(
        functools.partial(qkv_back_kernel, fast),
        out_shape=(jax.ShapeDtypeStruct((rows, model), F32),)
        + (jax.ShapeDtypeStruct((rows // 2, model), BF16),) * 2
        + grads,
        in_specs=[whole(space=pltpu.SMEM)]
        + [whole()] * 4
        + [whole(space=pl.ANY)] * 2
        + [whole(space=pl.ANY)] * 10,
        out_specs=(whole(),) * 3 + (whole(space=pl.ANY),) * len(grads),
        scratch_shapes=[
            pltpu.VMEM((4, model, 640), BF16),
            pltpu.VMEM((2, 3, rows, 384), BF16),
            pltpu.VMEM((3, model, 384), BF16),
            pltpu.VMEM((2, model, rows), BF16),
            pltpu.VMEM((2 * rows, model), F32),
            pltpu.VMEM((2 * rows, model), F32),
            pltpu.VMEM((2, model, 1152), BF16),
            pltpu.VMEM((2, 5, 2 * rows, 384), BF16),
            pltpu.SemaphoreType.DMA((n_blocks(fast),)),
            pltpu.SemaphoreType.DMA((13,)),
        ],
        compiler_params=params(),
        name="project_back",
    )(place, x_own, x_recv, cosine, sine, dhp, weights, *fields)


def tables(quarters, prompt, step, groups, plen):
    half = HDIM // 2
    places = []
    for quarter in quarters:
        places.append((quarter * prompt + jnp.arange(prompt)).astype(F32))
        places.append(jnp.tile((plen + quarter * step + jnp.arange(step)).astype(F32), groups))
    lanes = jnp.arange(2 * HDIM)
    frequency = 10000.0 ** (-(lanes % half).astype(F32) / half)
    angle = jnp.concatenate(places)[:, None] * frequency[None, :]
    return jnp.cos(angle), jnp.sin(angle) * jnp.where(lanes % HDIM < half, -1.0, 1.0)[None, :]


def own_continuation_mask(quarters, step):
    offset = jnp.arange(2 * step) % step
    cont = jnp.arange(2 * step) // step
    places = jnp.concatenate([quarter * step + offset for quarter in quarters])
    number = jnp.tile(cont, 4)
    rows = 4 * step
    allowed = (places[:, None] <= places[None, :rows]) & (number[:, None] == number[None, :rows])
    mask = jnp.where(allowed, 0.0, NEGATIVE).astype(F32)
    return mask, mask.T


def on_device(
    fast,
    prompt_tokens,
    continuation_tokens,
    prompt_index,
    attention_gain,
    query_weight,
    key_weight,
    value_weight,
    output_weight,
    feedforward_gain,
    gate_weight,
    up_weight,
    down_weight,
    prompt_cotangent,
    continuation_cotangent,
):
    z, x, y, c = [lax.axis_index(name).astype(jnp.int32) for name in ("z", "x", "y", "c")]
    place = jnp.stack([z, x, y, c])
    prompts, prompt_rows, model = prompt_tokens.shape
    conts, step, _ = continuation_tokens.shape
    groups = conts // prompts
    plen = 4 * prompt_rows
    rows = prompt_rows + groups * step
    lay = Layout(rows, prompt_rows, step)
    shard_rows, columns = query_weight.shape
    hid = gate_weight.shape[1]
    local = 2 * y + c
    other = 2 * y + (1 - c)
    quarters = [jnp.minimum(t, 3 - t) if low else jnp.maximum(t, 3 - t) for t in (local, other) for low in (1, 0)]

    gains = [attention_gain[:, None], feedforward_gain[:, None], jnp.zeros((shard_rows, 62), BF16)]
    first = [query_weight, value_weight, key_weight]
    first = jnp.where(c == 0, jnp.concatenate(first + gains, 1), jnp.concatenate(gains + first, 1))
    wide = [gate_weight, up_weight]
    down, out, gap = down_weight.T, output_weight.T, jnp.zeros((shard_rows, 64), BF16)
    rest = jnp.where(c == 0, jnp.concatenate(wide + [down, out, gap], 1), jnp.concatenate(wide + [down, gap, out], 1))

    def swap(data):
        return lax.ppermute(data, ("y", "c"), [(0, 3), (3, 0), (1, 2), (2, 1)])

    if fast:
        x_own, x_send = pack(place, prompt_index, prompt_tokens, continuation_tokens, 1)
        x_recv = swap(x_send)
        dy_own, *dy_sends = pack(after(place, x_send), prompt_index, prompt_cotangent, continuation_cotangent, 2)
        first = after(first, dy_sends[0])
        got = gather_line(first)
        line = stack_line(first, after(got, rest))
        got = gather_near(line)
        rest = after(rest, *line)
        rest_got = gather_line(rest)
        dy_first = swap(after(dy_sends[0], *line))
        cosine, sine = tables(after(tuple(quarters[:2]), *line), prompt_rows, step, groups, plen)
        own_mask, row_mask = own_continuation_mask(after(tuple(quarters), *line), step)
        plane = stack_near(line, after(got, cosine, sine, own_mask, row_mask, x_recv, dy_first, rest_got[0], rest_got[1]))
        far = gather_far(plane)
        dy_second = swap(after(dy_sends[1], *plane))
        dy_recv = (dy_first, dy_second)
        first_pieces = gather_core(plane, far)
        rest_line = stack_line(rest, after(rest_got, *far))
        rest_got = gather_near(rest_line)
        q, k, v, gains, weights = project(
            fast, place, x_own, x_recv, cosine, sine, after(first_pieces, dy_second, *rest_line)
        )
        k_other, v_other = over("c", k), over("c", v)
        rest_plane = stack_near(rest_line, after(rest_got, q))
        rest_far = gather_far(rest_plane)
        mixed, lse = attend(lay, place, q, k, v, k_other, v_other, after(row_mask, *rest_plane))
        rest_pieces = gather_core(after(rest_plane, mixed), after(rest_far, mixed))
    else:
        x_own, x_send = pack(place, prompt_index, prompt_tokens, continuation_tokens, 1)
        dy_own, *dy_sends = pack(place, prompt_index, prompt_cotangent, continuation_cotangent, 2)
        x_recv, dy_recv = swap(x_send), [swap(piece) for piece in dy_sends]
        first_pieces, rest_pieces = gather_any(first), gather_any(rest)
        cosine, sine = tables(quarters[:2], prompt_rows, step, groups, plen)
        own_mask, row_mask = own_continuation_mask(quarters, step)
        q, k, v, gains, weights = project(fast, place, x_own, x_recv, cosine, sine, first_pieces)
        k_other, v_other = over("c", k), over("c", v)
        mixed, lse = attend(lay, place, q, k, v, k_other, v_other, row_mask)
    made = middle(fast, place, mixed, x_own, x_recv, dy_own, dy_recv, gains, rest_pieces, hid)
    out_own, out_send, dhp, dmixed = made[:4]
    grads = made[4:]

    def back(half, mask):
        return attend_back(lay, place, half, q, k, v, k_other, v_other, mixed, dmixed, lse, mask)

    def collect(made):
        return [[m[i] for m in made] for i in range(3)] + [[over("c", m[i]) for m in made] for i in (3, 4)]

    if fast:
        rest_sum = Reduction(grads, True)
        sums = rest_sum.far_sums()
        rest_sum.far(sums)
        done = [back(0, after(own_mask, *sums))]
        rest_sum.gate(done[0][0])
        sums = rest_sum.near_sums()
        rest_sum.near(sums)
        out_recv = swap(after(out_send, *sums))
        done.append(back(1, after(own_mask, *sums)))
        rest_sum.gate(done[1][0])
        sums = rest_sum.line_sums()
        rest_sum.line(sums)
        fields = sum(collect(done), [])
        made = project_back(fast, place, x_own, x_recv, cosine, sine, after(dhp, out_recv, *sums), weights, fields)
        dx_own, dx_sends = made[0], made[1:3]
        first_sum = Reduction(after(made[3:], rest_sum.got[0], rest_sum.got[1]), False)
        out_prompt, out_cont = unpack(place, prompt_index, out_own, after(out_recv, dx_own), prompt_rows, step, BF16)
        sums = first_sum.far_sums()
        first_sum.far(sums)
        dx_first = swap(dx_sends[0])
        rest_sum.gate(out_prompt, dx_first, *sums)
        rest_grad = rest_sum.result()
        placed = scatter(after(place, rest_grad), prompt_index, True, (dx_own,), prompt_rows, step)
        first_sum.gate(rest_grad, *placed)
        sums = first_sum.near_sums()
        first_sum.near(sums)
        sums = first_sum.line_sums()
        first_sum.line(sums)
        dx_recv = (dx_first, swap(after(dx_sends[1], placed[0], *sums)))
        first_grad = first_sum.result()
    else:
        out_recv = swap(out_send)
        rest_grad = reduce_any(grads[0])
        fields = sum(collect([back(half, own_mask) for half in range(2)]), [])
        made = project_back(fast, place, x_own, x_recv, cosine, sine, dhp, weights, fields)
        dx_own, dx_recv = made[0], (swap(made[1]), swap(made[2]))
        placed = scatter(place, prompt_index, True, (dx_own,), prompt_rows, step)
        first_grad = reduce_any(made[3])
        out_prompt, out_cont = unpack(place, prompt_index, out_own, out_recv, prompt_rows, step, BF16)
    dx_prompt, dx_cont = scatter(place, prompt_index, False, dx_recv, prompt_rows, step, placed)
    first_grad = jnp.where(c == 0, first_grad[:, : 3 * columns], first_grad[:, 64:])
    start = 3 * hid
    gain_grads = jnp.where(c == 0, rest_grad[:, start + columns : start + columns + 2], rest_grad[:, start : start + 2])
    out_grad = jnp.where(c == 0, rest_grad[:, start : start + columns], rest_grad[:, start + 64 :])
    return (
        out_prompt,
        out_cont,
        dx_prompt,
        dx_cont,
        gain_grads[:, 0],
        first_grad[:, :columns],
        first_grad[:, 2 * columns :],
        first_grad[:, columns : 2 * columns],
        out_grad.T,
        gain_grads[:, 1],
        rest_grad[:, :hid],
        rest_grad[:, hid : 2 * hid],
        rest_grad[:, 2 * hid : start].T,
    )


def solution(mesh):
    parts = mesh.shape["dp"]
    grid = Mesh(mesh.devices.reshape(parts // 2, 2, 2, 2), ("z", "x", "y", "c"))
    dp, tensor = ("z", "x"), ("y", "c")
    fast = parts == 8
    tokens, columns, rows, vector = P(dp, tensor, None), P(dp, tensor), P(tensor, dp), P(dp)
    in_specs = (
        tokens,
        tokens,
        vector,
        vector,
        columns,
        columns,
        columns,
        rows,
        vector,
        columns,
        columns,
        rows,
        tokens,
        tokens,
    )
    out_specs = (
        tokens,
        tokens,
        tokens,
        tokens,
        vector,
        columns,
        columns,
        columns,
        rows,
        vector,
        columns,
        columns,
        rows,
    )
    return jax.shard_map(
        functools.partial(on_device, fast), mesh=grid, in_specs=in_specs, out_specs=out_specs, check_vma=False
    )
```

```python
import functools
import math

import jax
import jax.numpy as jnp
from jax import lax
from jax.experimental import pallas as pl
from jax.experimental.pallas import tpu as pltpu
from jax.sharding import Mesh
from jax.sharding import PartitionSpec as P

HDIM = 64
NEGATIVE = -1e30
EPSILON = 1e-06
BF16 = jnp.bfloat16
F32 = jnp.float32
LAST = ((1,), (1,))
FIRST = ((0,), (0,))
LIMIT = 64000 * 1024


def dotf(left, right, contract=((1,), (0,))):
    return lax.dot_general(left, right, (contract, ((), ())), preferred_element_type=F32)


def whole(shape=None, space=pltpu.VMEM):
    return pl.BlockSpec(memory_space=space)


def params(limit=LIMIT, **more):
    return pltpu.CompilerParams(vmem_limit_bytes=limit, **more)


def fill_order(index_ref, order_ref, count_ref, groups, total):
    count_ref[0] = 0
    count_ref[1] = 0

    def place(number, carry):
        prompt = index_ref[number]
        seen = count_ref[prompt]
        order_ref[prompt * groups + seen] = number
        count_ref[prompt] = seen + 1
        return carry

    lax.fori_loop(0, total, place, 0)


def pack_kernel(groups, place, index, prompt_x, cont_x, x_own, *refs):
    sends, (order, count) = refs[:-2], refs[-2:]
    rows = prompt_x.shape[1]
    step = cont_x.shape[1]
    fill_order(index, order, count, groups, cont_x.shape[0])
    mine = place[2]
    for which, outs in ((1 - mine, sends), (mine, (x_own,))):
        size = outs[0].shape[0]
        outs[0][0:rows, :] = prompt_x[which]
        for slot in range(groups):
            start = rows + slot * step
            at = slice(start % size, start % size + step)
            outs[start // size][at, :] = cont_x[order[which * groups + slot]]


def pack(place, index, prompt_x, cont_x, pieces):
    groups = cont_x.shape[0] // prompt_x.shape[0]
    count = prompt_x.shape[1] + groups * cont_x.shape[1]
    width = prompt_x.shape[2]
    return pl.pallas_call(
        functools.partial(pack_kernel, groups),
        out_shape=(jax.ShapeDtypeStruct((count, width), BF16),)
        + (jax.ShapeDtypeStruct((count // pieces, width), BF16),) * pieces,
        in_specs=[whole(space=pltpu.SMEM)] * 2 + [whole()] * 2,
        out_specs=(whole(),) * (1 + pieces),
        scratch_shapes=[pltpu.SMEM((2 * groups,), jnp.int32), pltpu.SMEM((2,), jnp.int32)],
        compiler_params=params(),
        name="pack_rows",
    )(place, index, prompt_x, cont_x)


def unpack_kernel(groups, place, index, own, back, prompt_out, cont_out, order, count):
    rows = prompt_out.shape[1]
    step = cont_out.shape[1]
    fill_order(index, order, count, groups, cont_out.shape[0])
    mine = place[2]
    for which, source in ((mine, own), (1 - mine, back)):
        prompt_out[which] = source[0:rows, :].astype(prompt_out.dtype)
        for slot in range(groups):
            piece = source[rows + slot * step : rows + (slot + 1) * step, :]
            cont_out[order[which * groups + slot]] = piece.astype(cont_out.dtype)


def unpack(place, index, own, back, rows, step, dtype):
    conts = index.shape[0]
    groups = conts // 2
    width = own.shape[1]
    return pl.pallas_call(
        functools.partial(unpack_kernel, groups),
        out_shape=(
            jax.ShapeDtypeStruct((2, rows, width), dtype),
            jax.ShapeDtypeStruct((conts, step, width), dtype),
        ),
        in_specs=[whole(space=pltpu.SMEM)] * 2 + [whole()] * 2,
        out_specs=(whole(),) * 2,
        scratch_shapes=[pltpu.SMEM((2 * groups,), jnp.int32), pltpu.SMEM((2,), jnp.int32)],
        compiler_params=params(),
        name="unpack_rows",
    )(place, index, own, back)


def scatter_kernel(groups, parts, own, aliased, place, index, *refs):
    sources, refs = refs[:parts], refs[parts + aliased :]
    prompt_out, cont_out, rows_s, order, count, sems = refs
    rows = prompt_out.shape[1]
    step = cont_out.shape[1]
    fill_order(index, order, count, groups, cont_out.shape[0])
    which = place[2] if own else 1 - place[2]
    size = sources[0].shape[0]
    copies = []
    for number, source in enumerate(sources):
        rows_s[number * size : (number + 1) * size, :] = source[...].astype(F32)
    copies.append(pltpu.make_async_copy(rows_s.at[pl.ds(0, rows), :], prompt_out.at[which], sems.at[0]))
    for slot in range(groups):
        piece = rows_s.at[pl.ds(rows + slot * step, step), :]
        copies.append(pltpu.make_async_copy(piece, cont_out.at[order[which * groups + slot]], sems.at[1 + slot]))
    for copy in copies:
        copy.start()
    for copy in copies:
        copy.wait()


def scatter(place, index, own, sources, rows, step, placed=()):
    conts = index.shape[0]
    groups = conts // 2
    width = sources[0].shape[1]
    aliases = {2 + len(sources) + i: i for i in range(len(placed))}
    return pl.pallas_call(
        functools.partial(scatter_kernel, groups, len(sources), own, len(placed)),
        out_shape=(jax.ShapeDtypeStruct((2, rows, width), F32), jax.ShapeDtypeStruct((conts, step, width), F32)),
        in_specs=[whole(space=pltpu.SMEM)] * 2 + [whole()] * len(sources) + [whole(space=pl.ANY)] * len(placed),
        out_specs=(whole(space=pl.ANY),) * 2,
        scratch_shapes=[
            pltpu.VMEM((rows + groups * step, width), F32),
            pltpu.SMEM((2 * groups,), jnp.int32),
            pltpu.SMEM((2,), jnp.int32),
            pltpu.SemaphoreType.DMA((1 + groups,)),
        ],
        input_output_aliases=aliases,
        compiler_params=params(),
        name="scatter_rows",
    )(place, index, *sources, *placed)


def blocks(fast, place, rows, model):
    if not fast:
        return [(0, (t,), t, 0, model) for t in range(4)]
    z, x, y, c = place[0], place[1], place[2], place[3]
    found = []
    for dc in range(2):
        for half in range(2):
            for near in range(2):
                for far in range(2):
                    kx, ky = (near, far) if half == 0 else (far, near)
                    for k in range(2):
                        t = 2 * (y ^ ky) + (c ^ dc)
                        row = ((z ^ (2 * half + k)) * 2 + (x ^ kx)) * rows
                        found.append((4 * dc + 2 * half + far, (near, k), t, row, rows))
    return found


def weight_copies(fast, place, pieces, held, sems, rows, model, columns=slice(None), base=0):
    copies = []
    for number, (piece, at, t, row, count) in enumerate(blocks(fast, place, rows, model)):
        if fast:
            row = pl.multiple_of(row, rows)
        source = pieces[piece].at[at + (slice(None), columns)]
        copies.append(
            pltpu.make_async_copy(source, held.at[t, pl.ds(row, count), columns], sems.at[base + number])
        )
    return copies


def store_grads(held, out, sems):
    copies = [pltpu.make_async_copy(held.at[t], out.at[t], sems.at[t]) for t in range(4)]
    for copy in copies:
        copy.start()
    for copy in copies:
        copy.wait()


def n_blocks(fast):
    return 32 if fast else 4


def n_pieces(fast):
    return 8 if fast else 1


def n_grads(fast):
    return 6 if fast else 1


def grad_shapes(fast, rows, model, columns):
    if fast:
        part = jax.ShapeDtypeStruct((2, 2, rows, columns), BF16)
        return (jax.ShapeDtypeStruct((2, 2, 2, rows, columns), BF16), part, part) * 2
    return (jax.ShapeDtypeStruct((4, model, columns), BF16),)


SWAP = [(0, 1), (1, 0)]


def over(axis, data):
    return lax.ppermute(data, axis, SWAP)


def over_z(data, k):
    return lax.ppermute(data, "z", [(i, i ^ k) for i in range(4)])


def after(data, *others):
    return lax.optimization_barrier((data,) + others)[0]


def gather_line(shard):
    return [over_z(shard, k) for k in (1, 2, 3)]


def stack_line(shard, got):
    return (jnp.stack([shard, got[0]]), jnp.stack([got[1], got[2]]))


def gather_near(line):
    return (over("x", line[0]), over("y", line[1]))


def stack_near(line, got):
    return tuple(jnp.stack([a, b]) for a, b in zip(line, got))


def gather_far(plane):
    return (over("y", plane[0]), over("x", plane[1]))


def gather_core(plane, far):
    mine = (plane[0], far[0], plane[1], far[1])
    return mine + tuple(over("c", piece) for piece in mine)


def gather_any(shard):
    flat = lax.all_gather(shard, ("z", "x"), axis=0, tiled=True)
    return (lax.all_gather(flat, ("y", "c"), axis=0, tiled=False),)


def total(items):
    return functools.reduce(jnp.add, [item.astype(F32) for item in items])


def add_kernel(terms, *refs):
    inputs = 1 + max(number for blocks in terms for number, _ in blocks)
    ins, refs = refs[:inputs], refs[inputs:]
    outs, refs = refs[: len(terms)], refs[len(terms) :]
    held, made, (in_sems, out_sems) = refs[: len(terms)], refs[len(terms) : 2 * len(terms)], refs[2 * len(terms) :]
    copies = []
    for s, blocks in enumerate(terms):
        row = []
        for i, (number, at) in enumerate(blocks):
            source = ins[number].at[at] if at else ins[number]
            row.append(pltpu.make_async_copy(source, held[s].at[i], in_sems.at[s, i]))
            row[-1].start()
        copies.append(row)
    leaving = []
    for s, blocks in enumerate(terms):
        for copy in copies[s]:
            copy.wait()
        *lead, rows, _ = made[s].shape

        def one(step, carry, s=s, blocks=blocks, lead=lead, rows=rows):
            place, chunk = step // (rows // 32), step % (rows // 32)
            at = (pl.ds(pl.multiple_of(chunk * 32, 32), 32), slice(None))
            if len(lead) == 1:
                at = (place,) + at
            if len(lead) == 2:
                at = (place // lead[1], place % lead[1]) + at
            if len(blocks) == 2:
                made[s][at] = held[s][(0,) + at] + held[s][(1,) + at]
            else:
                made[s][at] = total([held[s][(i,) + at] for i in range(len(blocks))]).astype(BF16)
            return carry

        lax.fori_loop(0, math.prod(lead) * (rows // 32), one, 0)
        leaving.append(pltpu.make_async_copy(made[s], outs[s], out_sems.at[s]))
        leaving[-1].start()
    for copy in leaving:
        copy.wait()


def add_blocks(sums):
    arrays, terms = [], []
    for blocks in sums:
        row = []
        for data, at in blocks:
            found = [i for i, other in enumerate(arrays) if other is data]
            if not found:
                arrays.append(data)
                found = [len(arrays) - 1]
            row.append((found[0], at))
        terms.append(tuple(row))
    shapes = [blocks[0][0].shape[len(blocks[0][1]) :] for blocks in sums]
    most = max(len(blocks) for blocks in sums)
    return pl.pallas_call(
        functools.partial(add_kernel, tuple(terms)),
        out_shape=tuple(jax.ShapeDtypeStruct(shape, BF16) for shape in shapes),
        in_specs=[whole(space=pl.ANY)] * len(arrays),
        out_specs=(whole(space=pl.ANY),) * len(sums),
        scratch_shapes=[pltpu.VMEM((len(blocks),) + shape, BF16) for blocks, shape in zip(sums, shapes)]
        + [pltpu.VMEM(shape, BF16) for shape in shapes]
        + [pltpu.SemaphoreType.DMA((len(sums), most)), pltpu.SemaphoreType.DMA((len(sums),))],
        compiler_params=params(),
        name="add_blocks",
    )(*arrays)


def add_here(sums):
    return [total([data[at] for data, at in blocks]).astype(BF16) for blocks in sums]


class Reduction:
    def __init__(self, grads, large):
        self.add = add_blocks if large else add_here
        self.keep = (grads[0], grads[3])
        self.away = (grads[2], grads[5])
        self.from_core = [over("c", grads[1]), over("c", grads[4])]

    def gate(self, *others):
        self.got = after(self.got, *others)

    def far_sums(self):
        sums = self.add([[(self.keep[half], (1,)), (self.from_core[half], ())] for half in range(2)])
        self.from_core = [over("c", part) for part in after(self.away, *sums)]
        return sums

    def far(self, sums):
        self.got = [over(axis, s) for axis, s in zip(("y", "x"), sums)]

    def near_sums(self):
        self.from_far = self.got
        return self.add(
            [
                [(self.keep[half], (0, 1)), (self.from_core[half], (1,)), (self.from_far[half], (1,))]
                for half in range(2)
            ]
        )

    def near(self, sums):
        self.got = [over(axis, s) for axis, s in zip(("x", "y"), sums)]

    def block(self, half, k):
        return [
            (self.keep[half], (0, 0, k)),
            (self.from_core[half], (0, k)),
            (self.from_far[half], (0, k)),
            (self.from_near[half], (k,)),
        ]

    def line_sums(self):
        self.from_near = self.got
        return self.add([self.block(half, k) for half, k in ((0, 1), (1, 0), (1, 1))])

    def line(self, sums):
        self.got = [over_z(s, k) for k, s in zip((1, 2, 3), sums)]

    def result(self):
        return total([data[at] for data, at in self.block(0, 0)] + list(self.got))


def reduce_any(out):
    mine = lax.psum_scatter(out, ("y", "c"), scatter_dimension=0, tiled=False)
    return lax.psum_scatter(mine, ("z", "x"), scatter_dimension=0, tiled=True).astype(F32)


def left_lanes(rows):
    return lax.broadcasted_iota(jnp.int32, (rows, 128), 1) < HDIM


def flip(tile):
    return pltpu.roll(tile, HDIM, 1)


def tile(data, number):
    return data[:, number * 128 : (number + 1) * 128]


def join_first(even, odd):
    left = left_lanes(even.shape[0])
    e = [tile(even, i) for i in range(5)]
    o = [tile(odd, i) for i in range(5)]
    query = [e[0], jnp.where(left, e[1], o[0]), o[1]]
    key = [e[3], jnp.where(left, e[4], o[3]), o[4]]
    e1, e2, o2, o3 = flip(e[1]), flip(e[2]), flip(o[2]), flip(o[3])
    value = [jnp.where(left, e1, e2), jnp.where(left, e2, o2), jnp.where(left, o2, o3)]
    return query + key + value


def split_first(query, key, value):
    left = left_lanes(query[0].shape[0])
    none = jnp.zeros_like(query[0])
    v = [flip(t) for t in value]
    even = [
        query[0],
        jnp.where(left, query[1], v[0]),
        jnp.where(left, v[0], v[1]),
        key[0],
        jnp.where(left, key[1], none),
    ]
    odd = [
        jnp.where(left, none, query[1]),
        query[2],
        jnp.where(left, v[1], v[2]),
        jnp.where(left, v[2], key[1]),
        key[2],
    ]
    return even, odd


def turn(field, first):
    width = field.shape[-1]
    return jnp.where(first, pltpu.roll(field, width - HDIM // 2, 1), pltpu.roll(field, HDIM // 2, 1))


def first_half(shape):
    return lax.broadcasted_iota(jnp.int32, shape, 1) % HDIM < HDIM // 2


def qkv_kernel(fast, place, x_own, x_recv, cosine, sine, *refs):
    pieces = refs[: n_pieces(fast)]
    *results, gains, weights_out, q, k, v, weights, held, sems, out_sems = refs[n_pieces(fast) :]
    rows, model = x_own.shape
    per = model // 8 if fast else model

    def leave(half):
        return [
            pltpu.make_async_copy(made.at[half], result.at[half], out_sems.at[half, i])
            for i, (made, result) in enumerate(zip((q, k, v, weights), results + [weights_out]))
        ]

    copies = weight_copies(fast, place, pieces, held, sems, per, model)
    for copy in copies:
        copy.start()
    for copy in copies:
        copy.wait()
    gains[...] = jnp.transpose(held[0, :, 512:640].astype(F32))[64:72, :]
    side = place[2]
    first = first_half((rows, 128))

    def one(half, carry):
        def join(i, carry):
            at = pl.ds(pl.multiple_of(i * 96, 96), 96)
            for number, made in enumerate(join_first(held[2 * half, at, :], held[2 * half + 1, at, :])):
                weights[half, at, number * 128 : (number + 1) * 128] = made
            return carry

        lax.fori_loop(0, model // 96, join, 0)
        for x, where in ((x_own, side), (x_recv, 1 - side)):
            at = pl.ds(pl.multiple_of(where * rows, rows), rows)
            cos, sin = cosine[at, :], sine[at, :]
            made = dotf(x[...], weights[half])
            for p in range(3):
                lanes = slice(p * 128, (p + 1) * 128)
                u = tile(made, p)
                q[half, at, lanes] = ((u * cos + turn(u, first) * sin).astype(BF16) * 0.125).astype(BF16)
                u = tile(made, 3 + p)
                k[half, at, lanes] = (u * cos + turn(u, first) * sin).astype(BF16)
                v[half, at, lanes] = tile(made, 6 + p).astype(BF16)
        for copy in leave(half):
            copy.start()
        return carry

    lax.fori_loop(0, 2, one, 0)
    for half in range(2):
        for copy in leave(half):
            copy.wait()


def project(fast, place, x_own, x_recv, cosine, sine, pieces):
    rows, model = x_own.shape
    field = jax.ShapeDtypeStruct((2, 2 * rows, 384), BF16)
    return pl.pallas_call(
        functools.partial(qkv_kernel, fast),
        out_shape=(field,) * 3
        + (jax.ShapeDtypeStruct((8, model), F32), jax.ShapeDtypeStruct((2, model, 1152), BF16)),
        in_specs=[whole(space=pltpu.SMEM)] + [whole()] * 4 + [whole(space=pl.ANY)] * len(pieces),
        out_specs=(whole(space=pl.ANY),) * 3 + (whole(), whole(space=pl.ANY)),
        scratch_shapes=[pltpu.VMEM((2, 2 * rows, 384), BF16)] * 3
        + [
            pltpu.VMEM((2, model, 1152), BF16),
            pltpu.VMEM((4, model, 640), BF16),
            pltpu.SemaphoreType.DMA((n_blocks(fast),)),
            pltpu.SemaphoreType.DMA((2, 4)),
        ],
        compiler_params=params(),
        name="project_qkv",
    )(place, x_own, x_recv, cosine, sine, *pieces)


class Layout:
    def __init__(self, rows, prompt, step):
        self.rows = rows
        self.prompt = prompt
        self.step = step
        self.pair = 2 * step
        self.cont_blocks = (rows - prompt) // (4 * step)
        self.width = 8 * step


def pair_rows(ref, lay, start):
    return (ref[pl.ds(start, lay.pair), :], ref[pl.ds(lay.rows + start, lay.pair), :])


def pair_start(lay, block, pair):
    return lay.prompt + (2 * block + pair) * lay.pair


def cont_query(ref, lay, block):
    parts = []
    for pair in range(2):
        parts += pair_rows(ref, lay, pair_start(lay, block, pair))
    return jnp.concatenate(parts, 0)


def cont_keys(own, other, lay, block, pair):
    start = pair_start(lay, block, pair)
    return jnp.concatenate(pair_rows(own, lay, start) + pair_rows(other, lay, start), 0)


def causal(count, key_axis):
    key = lax.broadcasted_iota(jnp.int32, (count, count), key_axis)
    row = lax.broadcasted_iota(jnp.int32, (count, count), 1 - key_axis)
    return jnp.where(key <= row, 0.0, NEGATIVE)


def shared_segments(lay):
    return [(0, 0), (0, lay.rows), (1, 0), (1, lay.rows)]


def attend_kernel(lay, place, q_ref, ko, vo, kp, vp, own_mask, mixed, lse, lse_s):
    inner = place[2] != place[3]
    q, keys, values, out = q_ref.at[0], (ko.at[0], kp.at[0]), (vo.at[0], vp.at[0]), mixed.at[0]
    count, width = lay.prompt, lay.width
    half = width // 2
    lane = lax.broadcasted_iota(jnp.int32, (1, 128), 1) // HDIM
    spot = lax.broadcasted_iota(jnp.int32, (1, 128), 1)
    low, high = pl.ds(0, count), pl.ds(lay.rows, count)
    extra = pl.ds(pl.multiple_of(jnp.where(inner, 0, lay.rows), lay.rows), count)
    out[...] = jnp.zeros_like(out)
    lse_s[...] = jnp.zeros_like(lse_s)

    def top(scores):
        return jnp.max(functools.reduce(jnp.maximum, scores), 1, keepdims=True)

    def sums(raised):
        return jnp.sum(functools.reduce(jnp.add, raised), 1, keepdims=True)

    def head(j, carry):
        chosen = lane == j

        def pick(block):
            return jnp.where(chosen, block, jnp.zeros_like(block))

        def finish(at, made, total, highest, number):
            out[at, :] = out[at, :] + pick(made / total).astype(BF16)
            here = pl.ds(number, made.shape[0])
            lse_s[here, :] = jnp.where(spot == j, highest + jnp.log(total), lse_s[here, :])

        q_low, q_high = pick(q[low, :]), pick(q[high, :])
        q_extra = jnp.where(inner, q_low, q_high)
        mask = causal(count, 1)
        s_low = dotf(q_low, keys[0][low, :], LAST) + mask
        s_high = [
            dotf(q_high, keys[0][high, :], LAST) + mask,
            dotf(q_high, keys[0][low, :], LAST),
            dotf(q_high, keys[1][low, :], LAST),
        ]
        s_extra = dotf(q_extra, keys[1][extra, :], LAST)
        s_cont = []
        for block in range(lay.cont_blocks):
            query = pick(cont_query(q, lay, block))
            scores = [dotf(query, keys[o][pl.ds(start, count), :], LAST) for o, start in shared_segments(lay)]
            own = []
            for pair in range(2):
                rows = query[pair * half : (pair + 1) * half, :]
                own.append(dotf(rows, cont_keys(keys[0], keys[1], lay, block, pair), LAST) + own_mask[...])
            s_cont.append(scores + [jnp.concatenate(own, 0)])

        m_low, m_high, m_extra = top([s_low]), top(s_high), top([s_extra])
        m_low = jnp.maximum(m_low, jnp.where(inner, m_extra, NEGATIVE))
        m_high = jnp.maximum(m_high, jnp.where(inner, NEGATIVE, m_extra))
        p_low = jnp.exp(s_low - m_low)
        p_high = [jnp.exp(s - m_high) for s in s_high]
        p_extra = jnp.exp(s_extra - jnp.where(inner, m_low, m_high))
        l_extra = sums([p_extra])
        l_low = sums([p_low]) + jnp.where(inner, l_extra, 0.0)
        l_high = sums(p_high) + jnp.where(inner, 0.0, l_extra)
        o_extra = dotf(p_extra.astype(BF16), values[1][extra, :])
        o_low = dotf(p_low.astype(BF16), values[0][low, :]) + jnp.where(inner, o_extra, 0.0)
        o_high = (
            dotf(p_high[0].astype(BF16), values[0][high, :])
            + dotf(p_high[1].astype(BF16), values[0][low, :])
            + dotf(p_high[2].astype(BF16), values[1][low, :])
            + jnp.where(inner, 0.0, o_extra)
        )
        finish(low, o_low, l_low, m_low, 0)
        finish(high, o_high, l_high, m_high, count)

        for block, scores in enumerate(s_cont):
            highest = top(scores)
            raised = [jnp.exp(s - highest) for s in scores]
            total = sums(raised)
            raised = [r.astype(BF16) for r in raised]
            made = functools.reduce(
                jnp.add, [dotf(r, values[o][pl.ds(start, count), :]) for r, (o, start) in zip(raised, shared_segments(lay))]
            )
            for pair in range(2):
                cut = slice(pair * half, (pair + 1) * half)
                part = made[cut, :] + dotf(raised[-1][cut, :], cont_keys(values[0], values[1], lay, block, pair))
                part = pick(part / total[cut, :]).astype(BF16)
                start = pair_start(lay, block, pair)
                for side in range(2):
                    at = pl.ds(side * lay.rows + start, lay.pair)
                    out[at, :] = out[at, :] + part[side * lay.pair : (side + 1) * lay.pair, :]
            here = pl.ds(2 * count + block * width, width)
            lse_s[here, :] = jnp.where(spot == j, highest + jnp.log(total), lse_s[here, :])
        return carry

    lax.fori_loop(0, 2, head, 0)
    lse[0, 0] = jnp.transpose(lse_s[...])[0:8, :]


def attend(lay, place, q, ko, vo, kp, vp, own_mask):
    total = q.shape[1]
    field = pl.BlockSpec((1, total, 128), lambda h, p, place: (h, 0, p))
    return pl.pallas_call(
        functools.partial(attend_kernel, lay),
        out_shape=(jax.ShapeDtypeStruct(q.shape, BF16), jax.ShapeDtypeStruct((2, 3, 8, total), F32)),
        grid_spec=pltpu.PrefetchScalarGridSpec(
            num_scalar_prefetch=1,
            grid=(2, 3),
            in_specs=[field] * 5 + [pl.BlockSpec(own_mask.shape, lambda h, p, place: (0, 0))],
            out_specs=(field, pl.BlockSpec((1, 1, 8, total), lambda h, p, place: (h, p, 0, 0))),
            scratch_shapes=[pltpu.VMEM((total, 128), F32)],
        ),
        compiler_params=params(),
        name="attend",
    )(place, q, ko, vo, kp, vp, own_mask)


def attend_back_kernel(
    lay, place, q_ref, ko, vo, kp, vp, mixed, up_ref, lse_ref, own_mask, dq, dko, dvo, dkp, dvp, kacc, vacc, qacc, delta_s
):
    inner = place[2] != place[3]
    q, keys, values = q_ref.at[0], (ko.at[0], kp.at[0]), (vo.at[0], vp.at[0])
    upstream, result, lse = up_ref.at[0], mixed.at[0], lse_ref.at[0]
    count, width = lay.prompt, lay.width
    half = width // 2
    lane = lax.broadcasted_iota(jnp.int32, (1, 128), 1) // HDIM
    kacc[...] = jnp.zeros_like(kacc)
    vacc[...] = jnp.zeros_like(vacc)
    qacc[...] = jnp.zeros_like(qacc)
    low, high = pl.ds(0, count), pl.ds(lay.rows, count)
    shift = jnp.where(inner, 0, 1)
    extra = pl.ds(pl.multiple_of(shift * lay.rows, lay.rows), count)
    either = pl.ds(pl.multiple_of(shift * count, count), count)

    def cont_rows(ref):
        return jnp.concatenate([cont_query(ref, lay, block) for block in range(lay.cont_blocks)], 0)

    def product(rows):
        return rows(upstream).astype(F32) * rows(result).astype(F32)

    heads = jnp.where(
        lax.broadcasted_iota(jnp.int32, (8, 128), 1) // HDIM == lax.broadcasted_iota(jnp.int32, (8, 128), 0), 1.0, 0.0
    ).astype(BF16)
    for at, rows in (
        (slice(0, count), lambda ref: ref[low, :]),
        (slice(count, 2 * count), lambda ref: ref[high, :]),
        (slice(2 * count, 2 * count + lay.cont_blocks * width), cont_rows),
    ):
        made = product(rows)
        coarse = made.astype(BF16)
        fine = (made - coarse.astype(F32)).astype(BF16)
        delta_s[:, at] = dotf(heads, coarse, LAST) + dotf(heads, fine, LAST)

    def head(j, carry):
        chosen = lane == j
        me = pl.ds(j, 1)

        def pick(block):
            return jnp.where(chosen, block, jnp.zeros_like(block))

        def back(key, value, query, grads, mask, log_total, delta):
            s = dotf(key, query, LAST)
            if mask is not None:
                s = s + mask
            share = jnp.exp(s - log_total)
            d = (share * (dotf(value, grads, LAST) - delta)).astype(BF16)
            return dotf(share.astype(BF16), grads), dotf(d, query), dotf(d, key, FIRST)

        def put(other, at, dv, dk):
            vacc[other, at, :] += dv
            kacc[other, at, :] += dk

        query, grads = pick(cont_rows(q)), pick(cont_rows(upstream))
        at = pl.ds(2 * count, lay.cont_blocks * width)
        log_total, delta = lse[0, me, at], delta_s[me, at]
        shared = shared_segments(lay)
        key = jnp.concatenate([keys[o][pl.ds(start, count), :] for o, start in shared], 0)
        value = jnp.concatenate([values[o][pl.ds(start, count), :] for o, start in shared], 0)
        dv, dk, total = back(key, value, query, grads, None, log_total, delta)
        for number, (other, start) in enumerate(shared):
            piece = slice(number * count, (number + 1) * count)
            put(other, pl.ds(start, count), dv[piece, :], dk[piece, :])
        for number in range(2 * lay.cont_blocks):
            block, pair = number // 2, number % 2
            cut = slice(number * half, (number + 1) * half)
            dv, dk, made = back(
                cont_keys(keys[0], keys[1], lay, block, pair),
                cont_keys(values[0], values[1], lay, block, pair),
                query[cut, :],
                grads[cut, :],
                own_mask[...],
                log_total[:, cut],
                delta[:, cut],
            )
            start = pair_start(lay, block, pair)
            for part in range(4):
                piece = slice(part * lay.pair, (part + 1) * lay.pair)
                put(part // 2, pl.ds((part % 2) * lay.rows + start, lay.pair), dv[piece, :], dk[piece, :])
            made = pick(total[cut, :] + made)
            for part in range(2):
                spot = pl.ds(part * lay.rows + start, lay.pair)
                qacc[spot, :] += made[part * lay.pair : (part + 1) * lay.pair, :]
        mask = causal(count, 0)
        at = pl.ds(count, count)
        query, grads, log_total, delta = pick(q[high, :]), pick(upstream[high, :]), lse[0, me, at], delta_s[me, at]
        seen = ((0, high), (0, low), (1, low))
        key = jnp.concatenate([keys[o][spot, :] for o, spot in seen], 0)
        value = jnp.concatenate([values[o][spot, :] for o, spot in seen], 0)
        tall = jnp.concatenate([mask, jnp.zeros((2 * count, count), F32)], 0)
        dv, dk, made = back(key, value, query, grads, tall, log_total, delta)
        for number, (other, spot) in enumerate(seen):
            piece = slice(number * count, (number + 1) * count)
            put(other, spot, dv[piece, :], dk[piece, :])
        qacc[high, :] += pick(made)
        at = pl.ds(0, count)
        dv, dk, made = back(
            keys[0][low, :],
            values[0][low, :],
            pick(q[low, :]),
            pick(upstream[low, :]),
            mask,
            lse[0, me, at],
            delta_s[me, at],
        )
        put(0, low, dv, dk)
        qacc[low, :] += pick(made)
        dv, dk, made = back(
            keys[1][extra, :],
            values[1][extra, :],
            pick(q[extra, :]),
            pick(upstream[extra, :]),
            None,
            lse[0, me, either],
            delta_s[me, either],
        )
        put(1, extra, dv, dk)
        qacc[extra, :] += pick(made)
        return carry

    lax.fori_loop(0, 2, head, 0)
    dq[...] = (qacc[...] * 0.125).astype(BF16)
    dko[...] = kacc[0].astype(BF16)
    dkp[...] = kacc[1].astype(BF16)
    dvo[...] = vacc[0].astype(BF16)
    dvp[...] = vacc[1].astype(BF16)


def attend_back(lay, place, half, q, ko, vo, kp, vp, mixed, upstream, lse, own_mask):
    total = q.shape[1]
    field = pl.BlockSpec((1, total, 128), lambda p, place: (half, 0, p))
    made = pl.BlockSpec((total, 128), lambda p, place: (0, p))
    return pl.pallas_call(
        functools.partial(attend_back_kernel, lay),
        out_shape=(jax.ShapeDtypeStruct((total, 384), BF16),) * 5,
        grid_spec=pltpu.PrefetchScalarGridSpec(
            num_scalar_prefetch=1,
            grid=(3,),
            in_specs=[field] * 7
            + [
                pl.BlockSpec((1, 1, 8, total), lambda p, place: (half, p, 0, 0)),
                pl.BlockSpec(own_mask.shape, lambda p, place: (0, 0)),
            ],
            out_specs=(made,) * 5,
            scratch_shapes=[
                pltpu.VMEM((2, total, 128), F32),
                pltpu.VMEM((2, total, 128), F32),
                pltpu.VMEM((total, 128), F32),
                pltpu.VMEM((8, total), F32),
            ],
        ),
        compiler_params=params(),
        name="attend_back",
    )(place, q, ko, vo, kp, vp, mixed, upstream, lse, own_mask)


def middle_kernel(fast, hid, place, mixed, xo, xr, dyo, dyr_a, dyr_b, gains, *refs):
    count = n_pieces(fast)
    pieces, refs = refs[:count], refs[count:]
    (out_own, out_send, dhp, dmixed), refs = refs[:4], refs[4:]
    count = n_grads(fast)
    grads, refs = refs[:count], refs[count:]
    held, wide_o, gate_s, up_s, hid_s, dgate_s, dup_s, low_t, fed_t, att_t, gain_acc, sum_s, sems = refs
    step = pl.program_id(0)
    model = held.shape[1]
    rows = xo.shape[0]
    per = model // 8 if fast else model
    G, U, D, O = slice(0, hid), slice(hid, 2 * hid), slice(2 * hid, 3 * hid), 3 * hid
    side = jnp.where(step == 0, place[2], 1 - place[2])
    here = pl.ds(pl.multiple_of(side * rows, rows), rows)
    left = left_lanes(model)
    out_copies = weight_copies(fast, place, pieces, held, sems, per, model, slice(O, O + 256))
    other_copies = weight_copies(fast, place, pieces, held, sems, per, model, slice(0, O), n_blocks(fast))

    @pl.when(step == 0)
    def _():
        for copy in out_copies + other_copies:
            copy.start()
        gain_acc[...] = jnp.zeros_like(gain_acc)
        for copy in out_copies:
            copy.wait()
        for half in range(2):
            even, odd = held.at[2 * half], held.at[2 * half + 1]
            wide_o[half, :, 0:128] = even[:, O : O + 128]
            wide_o[half, :, 128:256] = jnp.where(left, even[:, O + 128 : O + 256], odd[:, O : O + 128])
            wide_o[half, :, 256:384] = odd[:, O + 128 : O + 256]

    own = step == 0
    gain_a = gains[0:1, :]
    gain_f = gains[1:2, :]
    pre = jnp.where(own, xo[...], xr[...]).astype(F32)
    for half in range(2):
        pre = pre + dotf(mixed[half, here, :], wide_o[half], LAST)
    scale1 = lax.rsqrt(jnp.mean(pre * pre, -1, keepdims=True) + EPSILON)
    norm1 = pre * scale1
    normed = norm1 * gain_a
    low = normed.astype(BF16)
    low_t[step] = jnp.transpose(low)
    spot = pl.ds(pl.multiple_of(step * rows, rows), rows)

    @pl.when(step == 0)
    def _():
        for copy in other_copies:
            copy.wait()

    def forward(t, carry):
        gate = dotf(low, held[t, :, G])
        up = dotf(low, held[t, :, U])
        gate_s[t] = gate
        up_s[t] = up
        hid_s[t, spot, :] = (gate * jax.nn.sigmoid(gate) * up).astype(BF16)
        return carry

    def add_over(fields, columns):
        field = jnp.concatenate([fields[t, spot, :] for t in range(4)], 1)

        def chunk(n, carry):
            at = pl.ds(pl.multiple_of(n * 256, 256), 256)
            weight = jnp.concatenate([held[t, at, columns] for t in range(4)], 1)
            sum_s[:, at] = sum_s[:, at] + dotf(field, weight, LAST)
            return carry

        lax.fori_loop(0, model // 256, chunk, 0)

    lax.fori_loop(0, 4, forward, 0)
    sum_s[...] = normed
    add_over(hid_s, D)
    resid = sum_s[...]
    scale2 = lax.rsqrt(jnp.mean(resid * resid, -1, keepdims=True) + EPSILON)
    norm2 = resid * scale2
    result = (norm2 * gain_f).astype(BF16)

    @pl.when(own)
    def _():
        out_own[...] = result

    @pl.when(jnp.logical_not(own))
    def _():
        out_send[...] = result

    dy = jnp.where(own, dyo[...], jnp.concatenate([dyr_a[...], dyr_b[...]], 0)).astype(F32)
    gain_acc[1:2, :] += jnp.sum(dy * norm2, 0, keepdims=True)
    e2 = dy * gain_f
    d_resid = scale2 * (e2 - norm2 * jnp.mean(e2 * norm2, -1, keepdims=True))
    d_fed = d_resid.astype(BF16)
    fed_t[step] = jnp.transpose(d_fed)

    def backward(t, carry):
        gate, up = gate_s[t], up_s[t]
        d_hidden = dotf(d_fed, held[t, :, D])
        sig = jax.nn.sigmoid(gate)
        dgate_s[t, spot, :] = (d_hidden * up * sig * (1.0 + gate * (1.0 - sig))).astype(BF16)
        dup_s[t, spot, :] = (d_hidden * gate * sig).astype(BF16)
        return carry

    lax.fori_loop(0, 4, backward, 0)
    sum_s[...] = d_resid
    add_over(dgate_s, G)
    add_over(dup_s, U)
    d_normed = sum_s[...]
    gain_acc[0:1, :] += jnp.sum(d_normed * norm1, 0, keepdims=True)
    e1 = d_normed * gain_a
    d_pre = scale1 * (e1 - norm1 * jnp.mean(e1 * norm1, -1, keepdims=True))
    dhp[...] = d_pre
    d_att = d_pre.astype(BF16)
    att_t[step] = jnp.transpose(d_att)
    for half in range(2):
        dmixed[half] = dotf(d_att, wide_o[half]).astype(BF16)

    @pl.when(step == 1)
    def _():
        columns = jnp.transpose(jnp.broadcast_to(gain_acc[0:8, :], (8, model)))
        lane = lax.broadcasted_iota(jnp.int32, (model, 128), 1) % HDIM
        extra = jnp.where(lane == 0, columns[:, 0:1], jnp.where(lane == 1, columns[:, 1:2], 0.0))
        halves = (place[2], 1 - place[2])
        for half in range(2):
            made = None
            for part in range(2):
                at = pl.ds(pl.multiple_of(halves[part] * rows, rows), rows)
                more = dotf(att_t[part], mixed[half, at, :])
                made = more if made is None else made + more
            even, odd = held.at[2 * half], held.at[2 * half + 1]
            even[:, O : O + 128] = tile(made, 0).astype(BF16)
            even[:, O + 128 : O + 256] = jnp.where(left, tile(made, 1), extra).astype(BF16)
            odd[:, O : O + 128] = jnp.where(left, extra, tile(made, 1)).astype(BF16)
            odd[:, O + 128 : O + 256] = tile(made, 2).astype(BF16)

        def weight(r, carry):
            t = 2 * (place[2] ^ (r // 2)) + (place[3] ^ (r % 2)) if fast else r
            for columns, first, second in ((D, fed_t, hid_s), (G, low_t, dgate_s), (U, low_t, dup_s)):
                made = dotf(first[0], second[t, 0:rows, :]) + dotf(first[1], second[t, rows : 2 * rows, :])
                held[t, :, columns] = made.astype(BF16)
            if fast:
                for dc in range(2):

                    @pl.when(r % 2 == dc)
                    def _(dc=dc):
                        send_block(place, r // 2, dc, held, grads, sems, per, True)

            return carry

        lax.fori_loop(0, 4, weight, 0)
        if fast:
            for r in range(4):
                send_block(place, r // 2, r % 2, held, grads, sems, per, False)
        else:
            store_grads(held, grads[0], sems)


def send_block(place, ky, dc, held, targets, sems, rows, start):
    z, x, y, c = place[0], place[1], place[2], place[3]
    t = 2 * (y ^ ky) + (c ^ dc)

    def move(target, row, number):
        copy = pltpu.make_async_copy(held.at[t, pl.ds(row, rows), :], target, sems.at[number])
        if start:
            copy.start()
        else:
            copy.wait()

    for kz in range(4):
        for kx in range(2):
            half, k = kz // 2, kz % 2
            far, near = (ky, kx) if half == 0 else (kx, ky)
            row = pl.multiple_of(((z ^ kz) * 2 + (x ^ kx)) * rows, rows)
            number = 16 * dc + 8 * ky + 2 * kz + kx
            keep, first, second = targets[3 * half : 3 * half + 3]
            if dc == 0:
                move(keep.at[far, near, k], row, number)
            elif half == 1 or not start:
                move((second, first)[far if half == 1 else 0].at[near, k], row, number)
            else:
                for value, target in ((1, first), (0, second)):

                    @pl.when(far == value)
                    def _(target=target, row=row, number=number, near=near, k=k):
                        move(target.at[near, k], row, number)


def once(shape, index=None):
    return pl.BlockSpec(shape, index or (lambda i, place: (0,) * len(shape)), pipeline_mode=pl.Buffered(1))


def middle(fast, place, mixed, xo, xr, dyo, dyr, gains, pieces, hid):
    rows, model = xo.shape
    columns = 3 * hid + 256
    grads = grad_shapes(fast, model // 8 if fast else model, model, columns)

    def side_at(i, place):
        return (0, jnp.where(i == 0, place[2], 1 - place[2]), 0)

    half_rows = once((rows, model))
    field = once((2, 2 * rows, 384))
    return pl.pallas_call(
        functools.partial(middle_kernel, fast, hid),
        out_shape=(
            jax.ShapeDtypeStruct((rows, model), BF16),
            jax.ShapeDtypeStruct((rows, model), BF16),
            jax.ShapeDtypeStruct((2 * rows, model), F32),
            jax.ShapeDtypeStruct(mixed.shape, BF16),
        )
        + grads,
        grid_spec=pltpu.PrefetchScalarGridSpec(
            num_scalar_prefetch=1,
            grid=(2,),
            in_specs=[field]
            + [half_rows] * 3
            + [once((rows // 2, model))] * 2
            + [once((8, model))]
            + [whole(space=pl.ANY)] * len(pieces),
            out_specs=(
                pl.BlockSpec((rows, model), lambda i, place: (0, 0)),
                pl.BlockSpec((rows, model), lambda i, place: (0, 0)),
                pl.BlockSpec((rows, model), lambda i, place: (i, 0)),
                pl.BlockSpec((2, rows, 384), side_at),
            )
            + (whole(space=pl.ANY),) * len(grads),
            scratch_shapes=[
                pltpu.VMEM((4, model, columns), BF16),
                pltpu.VMEM((2, model, 384), BF16),
                pltpu.VMEM((4, rows, hid), F32),
                pltpu.VMEM((4, rows, hid), F32),
                pltpu.VMEM((4, 2 * rows, hid), BF16),
                pltpu.VMEM((4, 2 * rows, hid), BF16),
                pltpu.VMEM((4, 2 * rows, hid), BF16),
                pltpu.VMEM((2, model, rows), BF16),
                pltpu.VMEM((2, model, rows), BF16),
                pltpu.VMEM((2, model, rows), BF16),
                pltpu.VMEM((8, model), F32),
                pltpu.VMEM((rows, model), F32),
                pltpu.SemaphoreType.DMA((2 * n_blocks(fast),)),
            ],
        ),
        compiler_params=params(),
        name="middle",
    )(place, mixed, xo, xr, dyo, *dyr, gains, *pieces)


def qkv_back_kernel(fast, place, x_own, x_recv, cosine, sine, dhp_ref, weights_ref, *refs):
    fields = [refs[2 * i : 2 * i + 2] for i in range(5)]
    dx_own, dx_sends = refs[10], refs[11:13]
    grads, refs = refs[13 : 13 + n_grads(fast)], refs[13 + n_grads(fast) :]
    held, joined, made, x_t, dx, base, weights, moved, sems, extra_sems = refs
    rows, model = x_own.shape
    per = model // 8 if fast else model
    side = place[2]
    first = first_half((rows, 128))
    copies = [pltpu.make_async_copy(dhp_ref, base, extra_sems.at[0])]
    for half in range(2):
        copies.append(pltpu.make_async_copy(weights_ref.at[half], weights.at[half], extra_sems.at[1 + 6 * half]))
        for i in range(5):
            copies.append(pltpu.make_async_copy(fields[i][half], moved.at[half, i], extra_sems.at[2 + i + 6 * half]))
    for copy in copies[1:] + copies[:1]:
        copy.start()
    for number, x in enumerate((x_own, x_recv)):
        x_t[number] = jnp.transpose(x[...])
    for copy in copies[1:7]:
        copy.wait()
    dx[...] = jnp.zeros_like(dx)

    def one(half, carry):
        @pl.when(half == 1)
        def _():
            for copy in copies[7:]:
                copy.wait()

        def turn_back(number, carry):
            at = pl.ds(pl.multiple_of((side ^ number) * rows, rows), rows)
            cos, sin = cosine[at, :], sine[at, :]
            for p in range(3):
                lanes = slice(p * 128, (p + 1) * 128)
                query, key, value, key_more, value_more = [moved[half, i, at, lanes].astype(F32) for i in range(5)]
                joined[number, 0, :, lanes] = (query * cos - turn(query, first) * sin).astype(BF16)
                key = key + key_more
                joined[number, 1, :, lanes] = (key * cos - turn(key, first) * sin).astype(BF16)
                joined[number, 2, :, lanes] = (value + value_more).astype(BF16)
            whole_row = jnp.concatenate([joined[number, kind] for kind in range(3)], 1)
            spot = pl.ds(pl.multiple_of(number * rows, rows), rows)
            dx[spot, :] = dx[spot, :] + dotf(whole_row, weights[half], LAST)
            return carry

        def weight(kind, carry):
            made[kind] = (dotf(x_t[0], joined[0, kind]) + dotf(x_t[1], joined[1, kind])).astype(BF16)
            return carry

        lax.fori_loop(0, 2, turn_back, 0)
        lax.fori_loop(0, 3, weight, 0)

        def split(i, carry):
            at = pl.ds(pl.multiple_of(i * 96, 96), 96)
            even, odd = split_first(*[[tile(made[kind, at, :], p) for p in range(3)] for kind in range(3)])
            for p in range(5):
                held[2 * half, at, p * 128 : (p + 1) * 128] = even[p]
                held[2 * half + 1, at, p * 128 : (p + 1) * 128] = odd[p]
            return carry

        lax.fori_loop(0, model // 96, split, 0)
        if fast:
            for dc in range(2):
                send_block(place, side ^ half, dc, held, grads, sems, per, True)
        return carry

    lax.fori_loop(0, 2, one, 0)
    copies[0].wait()
    dx_own[...] = dx[0:rows, :] + base[0:rows, :]
    for number in range(2):
        cut = slice(rows + number * (rows // 2), rows + (number + 1) * (rows // 2))
        dx_sends[number][...] = (dx[cut, :] + base[cut, :]).astype(BF16)
    if fast:
        for half in range(2):
            for dc in range(2):
                send_block(place, side ^ half, dc, held, grads, sems, per, False)
    else:
        store_grads(held, grads[0], sems)


def project_back(fast, place, x_own, x_recv, cosine, sine, dhp, weights, fields):
    rows, model = x_own.shape
    grads = grad_shapes(fast, model // 8 if fast else model, model, 640)
    return pl.pallas_call(
        functools.partial(qkv_back_kernel, fast),
        out_shape=(jax.ShapeDtypeStruct((rows, model), F32),)
        + (jax.ShapeDtypeStruct((rows // 2, model), BF16),) * 2
        + grads,
        in_specs=[whole(space=pltpu.SMEM)]
        + [whole()] * 4
        + [whole(space=pl.ANY)] * 2
        + [whole(space=pl.ANY)] * 10,
        out_specs=(whole(),) * 3 + (whole(space=pl.ANY),) * len(grads),
        scratch_shapes=[
            pltpu.VMEM((4, model, 640), BF16),
            pltpu.VMEM((2, 3, rows, 384), BF16),
            pltpu.VMEM((3, model, 384), BF16),
            pltpu.VMEM((2, model, rows), BF16),
            pltpu.VMEM((2 * rows, model), F32),
            pltpu.VMEM((2 * rows, model), F32),
            pltpu.VMEM((2, model, 1152), BF16),
            pltpu.VMEM((2, 5, 2 * rows, 384), BF16),
            pltpu.SemaphoreType.DMA((n_blocks(fast),)),
            pltpu.SemaphoreType.DMA((13,)),
        ],
        compiler_params=params(),
        name="project_back",
    )(place, x_own, x_recv, cosine, sine, dhp, weights, *fields)


def tables(quarters, prompt, step, groups, plen):
    half = HDIM // 2
    places = []
    for quarter in quarters:
        places.append((quarter * prompt + jnp.arange(prompt)).astype(F32))
        places.append(jnp.tile((plen + quarter * step + jnp.arange(step)).astype(F32), groups))
    lanes = jnp.arange(2 * HDIM)
    frequency = 10000.0 ** (-(lanes % half).astype(F32) / half)
    angle = jnp.concatenate(places)[:, None] * frequency[None, :]
    return jnp.cos(angle), jnp.sin(angle) * jnp.where(lanes % HDIM < half, -1.0, 1.0)[None, :]


def own_continuation_mask(quarters, step):
    offset = jnp.arange(2 * step) % step
    cont = jnp.arange(2 * step) // step
    places = jnp.concatenate([quarter * step + offset for quarter in quarters])
    number = jnp.tile(cont, 4)
    rows = 4 * step
    allowed = (places[:, None] <= places[None, :rows]) & (number[:, None] == number[None, :rows])
    mask = jnp.where(allowed, 0.0, NEGATIVE).astype(F32)
    return mask, mask.T


def on_device(
    fast,
    prompt_tokens,
    continuation_tokens,
    prompt_index,
    attention_gain,
    query_weight,
    key_weight,
    value_weight,
    output_weight,
    feedforward_gain,
    gate_weight,
    up_weight,
    down_weight,
    prompt_cotangent,
    continuation_cotangent,
):
    z, x, y, c = [lax.axis_index(name).astype(jnp.int32) for name in ("z", "x", "y", "c")]
    place = jnp.stack([z, x, y, c])
    prompts, prompt_rows, model = prompt_tokens.shape
    conts, step, _ = continuation_tokens.shape
    groups = conts // prompts
    plen = 4 * prompt_rows
    rows = prompt_rows + groups * step
    lay = Layout(rows, prompt_rows, step)
    shard_rows, columns = query_weight.shape
    hid = gate_weight.shape[1]
    local = 2 * y + c
    other = 2 * y + (1 - c)
    quarters = [jnp.minimum(t, 3 - t) if low else jnp.maximum(t, 3 - t) for t in (local, other) for low in (1, 0)]

    gains = [attention_gain[:, None], feedforward_gain[:, None], jnp.zeros((shard_rows, 62), BF16)]
    first = [query_weight, value_weight, key_weight]
    first = jnp.where(c == 0, jnp.concatenate(first + gains, 1), jnp.concatenate(gains + first, 1))
    wide = [gate_weight, up_weight]
    down, out, gap = down_weight.T, output_weight.T, jnp.zeros((shard_rows, 64), BF16)
    rest = jnp.where(c == 0, jnp.concatenate(wide + [down, out, gap], 1), jnp.concatenate(wide + [down, gap, out], 1))

    def swap(data):
        return lax.ppermute(data, ("y", "c"), [(0, 3), (3, 0), (1, 2), (2, 1)])

    if fast:
        x_own, x_send = pack(place, prompt_index, prompt_tokens, continuation_tokens, 1)
        x_recv = swap(x_send)
        dy_own, *dy_sends = pack(after(place, x_send), prompt_index, prompt_cotangent, continuation_cotangent, 2)
        first = after(first, dy_sends[0])
        got = gather_line(first)
        line = stack_line(first, after(got, rest))
        got = gather_near(line)
        rest = after(rest, *line)
        rest_got = gather_line(rest)
        dy_first = swap(after(dy_sends[0], *line))
        cosine, sine = tables(after(tuple(quarters[:2]), *line), prompt_rows, step, groups, plen)
        own_mask, row_mask = own_continuation_mask(after(tuple(quarters), *line), step)
        plane = stack_near(line, after(got, cosine, sine, own_mask, row_mask, x_recv, dy_first, rest_got[0], rest_got[1]))
        far = gather_far(plane)
        dy_second = swap(after(dy_sends[1], *plane))
        dy_recv = (dy_first, dy_second)
        first_pieces = gather_core(plane, far)
        rest_line = stack_line(rest, after(rest_got, *far))
        rest_got = gather_near(rest_line)
        q, k, v, gains, weights = project(
            fast, place, x_own, x_recv, cosine, sine, after(first_pieces, dy_second, *rest_line)
        )
        rest_got = after(rest_got, q)
        k, v = after((k, v), *rest_got)
        k_other, v_other = over("c", k), over("c", v)
        rest_plane = stack_near(rest_line, after(rest_got, q))
        rest_far = gather_far(rest_plane)
        mixed, lse = attend(lay, place, q, k, v, k_other, v_other, after(row_mask, *rest_plane))
        rest_plane = after(rest_plane, mixed)
        core_plane = [over("c", piece) for piece in rest_plane]
        rest_far = after(rest_far, mixed, *core_plane)
        core_far = [over("c", piece) for piece in rest_far]
        rest_pieces = (rest_plane[0], rest_far[0], rest_plane[1], rest_far[1])
        rest_pieces += (core_plane[0], core_far[0], core_plane[1], core_far[1])
    else:
        x_own, x_send = pack(place, prompt_index, prompt_tokens, continuation_tokens, 1)
        dy_own, *dy_sends = pack(place, prompt_index, prompt_cotangent, continuation_cotangent, 2)
        x_recv, dy_recv = swap(x_send), [swap(piece) for piece in dy_sends]
        first_pieces, rest_pieces = gather_any(first), gather_any(rest)
        cosine, sine = tables(quarters[:2], prompt_rows, step, groups, plen)
        own_mask, row_mask = own_continuation_mask(quarters, step)
        q, k, v, gains, weights = project(fast, place, x_own, x_recv, cosine, sine, first_pieces)
        k_other, v_other = over("c", k), over("c", v)
        mixed, lse = attend(lay, place, q, k, v, k_other, v_other, row_mask)
    made = middle(fast, place, mixed, x_own, x_recv, dy_own, dy_recv, gains, rest_pieces, hid)
    out_own, out_send, dhp, dmixed = made[:4]
    grads = made[4:]

    def back(half, mask):
        return attend_back(lay, place, half, q, k, v, k_other, v_other, mixed, dmixed, lse, mask)

    def collect(made):
        return [[m[i] for m in made] for i in range(3)] + [[over("c", m[i]) for m in made] for i in (3, 4)]

    if fast:
        rest_sum = Reduction(grads, True)
        sums = rest_sum.far_sums()
        rest_sum.far(sums)
        done = [back(0, after(own_mask, *sums))]
        rest_sum.gate(done[0][0])
        sums = rest_sum.near_sums()
        rest_sum.near(sums)
        out_recv = swap(after(out_send, *sums))
        done.append(back(1, after(own_mask, *sums)))
        rest_sum.gate(done[1][0])
        sums = rest_sum.line_sums()
        rest_sum.line(sums)
        fields = sum(collect(done), [])
        made = project_back(fast, place, x_own, x_recv, cosine, sine, after(dhp, out_recv, *sums), weights, fields)
        dx_own, dx_sends = made[0], made[1:3]
        first_sum = Reduction(after(made[3:], rest_sum.got[0], rest_sum.got[1]), False)
        out_prompt, out_cont = unpack(place, prompt_index, out_own, after(out_recv, dx_own), prompt_rows, step, BF16)
        sums = first_sum.far_sums()
        first_sum.far(sums)
        dx_first = swap(dx_sends[0])
        rest_sum.gate(out_prompt, dx_first, *sums)
        rest_grad = rest_sum.result()
        placed = scatter(after(place, rest_grad), prompt_index, True, (dx_own,), prompt_rows, step)
        first_sum.gate(rest_grad, *placed)
        sums = first_sum.near_sums()
        first_sum.near(sums)
        sums = first_sum.line_sums()
        first_sum.line(sums)
        dx_recv = (dx_first, swap(after(dx_sends[1], placed[0], *sums)))
        first_grad = first_sum.result()
    else:
        out_recv = swap(out_send)
        rest_grad = reduce_any(grads[0])
        fields = sum(collect([back(half, own_mask) for half in range(2)]), [])
        made = project_back(fast, place, x_own, x_recv, cosine, sine, dhp, weights, fields)
        dx_own, dx_recv = made[0], (swap(made[1]), swap(made[2]))
        placed = scatter(place, prompt_index, True, (dx_own,), prompt_rows, step)
        first_grad = reduce_any(made[3])
        out_prompt, out_cont = unpack(place, prompt_index, out_own, out_recv, prompt_rows, step, BF16)
    dx_prompt, dx_cont = scatter(place, prompt_index, False, dx_recv, prompt_rows, step, placed)
    first_grad = jnp.where(c == 0, first_grad[:, : 3 * columns], first_grad[:, 64:])
    start = 3 * hid
    gain_grads = jnp.where(c == 0, rest_grad[:, start + columns : start + columns + 2], rest_grad[:, start : start + 2])
    out_grad = jnp.where(c == 0, rest_grad[:, start : start + columns], rest_grad[:, start + 64 :])
    return (
        out_prompt,
        out_cont,
        dx_prompt,
        dx_cont,
        gain_grads[:, 0],
        first_grad[:, :columns],
        first_grad[:, 2 * columns :],
        first_grad[:, columns : 2 * columns],
        out_grad.T,
        gain_grads[:, 1],
        rest_grad[:, :hid],
        rest_grad[:, hid : 2 * hid],
        rest_grad[:, 2 * hid : start].T,
    )


def solution(mesh):
    parts = mesh.shape["dp"]
    grid = Mesh(mesh.devices.reshape(parts // 2, 2, 2, 2), ("z", "x", "y", "c"))
    dp, tensor = ("z", "x"), ("y", "c")
    fast = parts == 8
    tokens, columns, rows, vector = P(dp, tensor, None), P(dp, tensor), P(tensor, dp), P(dp)
    in_specs = (
        tokens,
        tokens,
        vector,
        vector,
        columns,
        columns,
        columns,
        rows,
        vector,
        columns,
        columns,
        rows,
        tokens,
        tokens,
    )
    out_specs = (
        tokens,
        tokens,
        tokens,
        tokens,
        vector,
        columns,
        columns,
        columns,
        rows,
        vector,
        columns,
        columns,
        rows,
    )
    return jax.shard_map(
        functools.partial(on_device, fast), mesh=grid, in_specs=in_specs, out_specs=out_specs, check_vma=False
    )
```

```python
import functools
import math

import jax
import jax.numpy as jnp
from jax import lax
from jax.experimental import pallas as pl
from jax.experimental.pallas import tpu as pltpu
from jax.sharding import Mesh
from jax.sharding import PartitionSpec as P

HDIM = 64
NEGATIVE = -1e30
EPSILON = 1e-06
BF16 = jnp.bfloat16
F32 = jnp.float32
LAST = ((1,), (1,))
FIRST = ((0,), (0,))
LIMIT = 64000 * 1024


def dotf(left, right, contract=((1,), (0,))):
    return lax.dot_general(left, right, (contract, ((), ())), preferred_element_type=F32)


def whole(shape=None, space=pltpu.VMEM):
    return pl.BlockSpec(memory_space=space)


def params(limit=LIMIT, **more):
    return pltpu.CompilerParams(vmem_limit_bytes=limit, **more)


def fill_order(index_ref, order_ref, count_ref, groups, total):
    count_ref[0] = 0
    count_ref[1] = 0

    def place(number, carry):
        prompt = index_ref[number]
        seen = count_ref[prompt]
        order_ref[prompt * groups + seen] = number
        count_ref[prompt] = seen + 1
        return carry

    lax.fori_loop(0, total, place, 0)


def pack_kernel(groups, place, index, prompt_x, cont_x, x_own, *refs):
    sends, (order, count) = refs[:-2], refs[-2:]
    rows = prompt_x.shape[1]
    step = cont_x.shape[1]
    fill_order(index, order, count, groups, cont_x.shape[0])
    mine = place[2]
    for which, outs in ((1 - mine, sends), (mine, (x_own,))):
        size = outs[0].shape[0]
        outs[0][0:rows, :] = prompt_x[which]
        for slot in range(groups):
            start = rows + slot * step
            at = slice(start % size, start % size + step)
            outs[start // size][at, :] = cont_x[order[which * groups + slot]]


def pack(place, index, prompt_x, cont_x, pieces):
    groups = cont_x.shape[0] // prompt_x.shape[0]
    count = prompt_x.shape[1] + groups * cont_x.shape[1]
    width = prompt_x.shape[2]
    return pl.pallas_call(
        functools.partial(pack_kernel, groups),
        out_shape=(jax.ShapeDtypeStruct((count, width), BF16),)
        + (jax.ShapeDtypeStruct((count // pieces, width), BF16),) * pieces,
        in_specs=[whole(space=pltpu.SMEM)] * 2 + [whole()] * 2,
        out_specs=(whole(),) * (1 + pieces),
        scratch_shapes=[pltpu.SMEM((2 * groups,), jnp.int32), pltpu.SMEM((2,), jnp.int32)],
        compiler_params=params(),
        name="pack_rows",
    )(place, index, prompt_x, cont_x)


def unpack_kernel(groups, place, index, own, back, prompt_out, cont_out, order, count):
    rows = prompt_out.shape[1]
    step = cont_out.shape[1]
    fill_order(index, order, count, groups, cont_out.shape[0])
    mine = place[2]
    for which, source in ((mine, own), (1 - mine, back)):
        prompt_out[which] = source[0:rows, :].astype(prompt_out.dtype)
        for slot in range(groups):
            piece = source[rows + slot * step : rows + (slot + 1) * step, :]
            cont_out[order[which * groups + slot]] = piece.astype(cont_out.dtype)


def unpack(place, index, own, back, rows, step, dtype):
    conts = index.shape[0]
    groups = conts // 2
    width = own.shape[1]
    return pl.pallas_call(
        functools.partial(unpack_kernel, groups),
        out_shape=(
            jax.ShapeDtypeStruct((2, rows, width), dtype),
            jax.ShapeDtypeStruct((conts, step, width), dtype),
        ),
        in_specs=[whole(space=pltpu.SMEM)] * 2 + [whole()] * 2,
        out_specs=(whole(),) * 2,
        scratch_shapes=[pltpu.SMEM((2 * groups,), jnp.int32), pltpu.SMEM((2,), jnp.int32)],
        compiler_params=params(),
        name="unpack_rows",
    )(place, index, own, back)


def scatter_kernel(groups, parts, own, aliased, place, index, *refs):
    sources, refs = refs[:parts], refs[parts + aliased :]
    prompt_out, cont_out, rows_s, order, count, sems = refs
    rows = prompt_out.shape[1]
    step = cont_out.shape[1]
    fill_order(index, order, count, groups, cont_out.shape[0])
    which = place[2] if own else 1 - place[2]
    size = sources[0].shape[0]
    copies = []
    for number, source in enumerate(sources):
        rows_s[number * size : (number + 1) * size, :] = source[...].astype(F32)
    copies.append(pltpu.make_async_copy(rows_s.at[pl.ds(0, rows), :], prompt_out.at[which], sems.at[0]))
    for slot in range(groups):
        piece = rows_s.at[pl.ds(rows + slot * step, step), :]
        copies.append(pltpu.make_async_copy(piece, cont_out.at[order[which * groups + slot]], sems.at[1 + slot]))
    for copy in copies:
        copy.start()
    for copy in copies:
        copy.wait()


def scatter(place, index, own, sources, rows, step, placed=()):
    conts = index.shape[0]
    groups = conts // 2
    width = sources[0].shape[1]
    aliases = {2 + len(sources) + i: i for i in range(len(placed))}
    return pl.pallas_call(
        functools.partial(scatter_kernel, groups, len(sources), own, len(placed)),
        out_shape=(jax.ShapeDtypeStruct((2, rows, width), F32), jax.ShapeDtypeStruct((conts, step, width), F32)),
        in_specs=[whole(space=pltpu.SMEM)] * 2 + [whole()] * len(sources) + [whole(space=pl.ANY)] * len(placed),
        out_specs=(whole(space=pl.ANY),) * 2,
        scratch_shapes=[
            pltpu.VMEM((rows + groups * step, width), F32),
            pltpu.SMEM((2 * groups,), jnp.int32),
            pltpu.SMEM((2,), jnp.int32),
            pltpu.SemaphoreType.DMA((1 + groups,)),
        ],
        input_output_aliases=aliases,
        compiler_params=params(),
        name="scatter_rows",
    )(place, index, *sources, *placed)


def blocks(fast, place, rows, model):
    if not fast:
        return [(0, (t,), t, 0, model) for t in range(4)]
    z, x, y, c = place[0], place[1], place[2], place[3]
    found = []
    for dc in range(2):
        for half in range(2):
            for near in range(2):
                for far in range(2):
                    kx, ky = (near, far) if half == 0 else (far, near)
                    for k in range(2):
                        t = 2 * (y ^ ky) + (c ^ dc)
                        row = ((z ^ (2 * half + k)) * 2 + (x ^ kx)) * rows
                        found.append((4 * dc + 2 * half + far, (near, k), t, row, rows))
    return found


def weight_copies(fast, place, pieces, held, sems, rows, model, columns=slice(None), base=0):
    copies = []
    for number, (piece, at, t, row, count) in enumerate(blocks(fast, place, rows, model)):
        if fast:
            row = pl.multiple_of(row, rows)
        source = pieces[piece].at[at + (slice(None), columns)]
        copies.append(
            pltpu.make_async_copy(source, held.at[t, pl.ds(row, count), columns], sems.at[base + number])
        )
    return copies


def store_grads(held, out, sems):
    copies = [pltpu.make_async_copy(held.at[t], out.at[t], sems.at[t]) for t in range(4)]
    for copy in copies:
        copy.start()
    for copy in copies:
        copy.wait()


def n_blocks(fast):
    return 32 if fast else 4


def n_pieces(fast):
    return 8 if fast else 1


def n_grads(fast):
    return 6 if fast else 1


def grad_shapes(fast, rows, model, columns):
    if fast:
        part = jax.ShapeDtypeStruct((2, 2, rows, columns), BF16)
        return (jax.ShapeDtypeStruct((2, 2, 2, rows, columns), BF16), part, part) * 2
    return (jax.ShapeDtypeStruct((4, model, columns), BF16),)


SWAP = [(0, 1), (1, 0)]


def over(axis, data):
    return lax.ppermute(data, axis, SWAP)


def over_z(data, k):
    return lax.ppermute(data, "z", [(i, i ^ k) for i in range(4)])


def after(data, *others):
    return lax.optimization_barrier((data,) + others)[0]


def gather_line(shard):
    return [over_z(shard, k) for k in (1, 2, 3)]


def stack_line(shard, got):
    return (jnp.stack([shard, got[0]]), jnp.stack([got[1], got[2]]))


def gather_near(line):
    return (over("x", line[0]), over("y", line[1]))


def stack_near(line, got):
    return tuple(jnp.stack([a, b]) for a, b in zip(line, got))


def gather_far(plane):
    return (over("y", plane[0]), over("x", plane[1]))


def gather_core(plane, far):
    mine = (plane[0], far[0], plane[1], far[1])
    return mine + tuple(over("c", piece) for piece in mine)


def gather_any(shard):
    flat = lax.all_gather(shard, ("z", "x"), axis=0, tiled=True)
    return (lax.all_gather(flat, ("y", "c"), axis=0, tiled=False),)


def total(items):
    return functools.reduce(jnp.add, [item.astype(F32) for item in items])


def add_kernel(terms, *refs):
    inputs = 1 + max(number for blocks in terms for number, _ in blocks)
    ins, refs = refs[:inputs], refs[inputs:]
    outs, refs = refs[: len(terms)], refs[len(terms) :]
    held, made, (in_sems, out_sems) = refs[: len(terms)], refs[len(terms) : 2 * len(terms)], refs[2 * len(terms) :]
    copies = []
    for s, blocks in enumerate(terms):
        row = []
        for i, (number, at) in enumerate(blocks):
            source = ins[number].at[at] if at else ins[number]
            row.append(pltpu.make_async_copy(source, held[s].at[i], in_sems.at[s, i]))
            row[-1].start()
        copies.append(row)
    leaving = []
    for s, blocks in enumerate(terms):
        for copy in copies[s]:
            copy.wait()
        *lead, rows, _ = made[s].shape

        def one(step, carry, s=s, blocks=blocks, lead=lead, rows=rows):
            place, chunk = step // (rows // 32), step % (rows // 32)
            at = (pl.ds(pl.multiple_of(chunk * 32, 32), 32), slice(None))
            if len(lead) == 1:
                at = (place,) + at
            if len(lead) == 2:
                at = (place // lead[1], place % lead[1]) + at
            if len(blocks) == 2:
                made[s][at] = held[s][(0,) + at] + held[s][(1,) + at]
            else:
                made[s][at] = total([held[s][(i,) + at] for i in range(len(blocks))]).astype(BF16)
            return carry

        lax.fori_loop(0, math.prod(lead) * (rows // 32), one, 0)
        leaving.append(pltpu.make_async_copy(made[s], outs[s], out_sems.at[s]))
        leaving[-1].start()
    for copy in leaving:
        copy.wait()


def add_blocks(sums):
    arrays, terms = [], []
    for blocks in sums:
        row = []
        for data, at in blocks:
            found = [i for i, other in enumerate(arrays) if other is data]
            if not found:
                arrays.append(data)
                found = [len(arrays) - 1]
            row.append((found[0], at))
        terms.append(tuple(row))
    shapes = [blocks[0][0].shape[len(blocks[0][1]) :] for blocks in sums]
    most = max(len(blocks) for blocks in sums)
    return pl.pallas_call(
        functools.partial(add_kernel, tuple(terms)),
        out_shape=tuple(jax.ShapeDtypeStruct(shape, BF16) for shape in shapes),
        in_specs=[whole(space=pl.ANY)] * len(arrays),
        out_specs=(whole(space=pl.ANY),) * len(sums),
        scratch_shapes=[pltpu.VMEM((len(blocks),) + shape, BF16) for blocks, shape in zip(sums, shapes)]
        + [pltpu.VMEM(shape, BF16) for shape in shapes]
        + [pltpu.SemaphoreType.DMA((len(sums), most)), pltpu.SemaphoreType.DMA((len(sums),))],
        compiler_params=params(),
        name="add_blocks",
    )(*arrays)


def add_here(sums):
    return [total([data[at] for data, at in blocks]).astype(BF16) for blocks in sums]


class Reduction:
    def __init__(self, grads, large):
        self.add = add_blocks if large else add_here
        self.keep = (grads[0], grads[3])
        self.away = (grads[2], grads[5])
        self.from_core = [over("c", grads[1]), over("c", grads[4])]

    def gate(self, *others):
        self.got = after(self.got, *others)

    def far_sums(self):
        sums = self.add([[(self.keep[half], (1,)), (self.from_core[half], ())] for half in range(2)])
        self.from_core = [over("c", part) for part in after(self.away, *sums)]
        return sums

    def far(self, sums):
        self.got = [over(axis, s) for axis, s in zip(("y", "x"), sums)]

    def near_sums(self):
        self.from_far = self.got
        return self.add(
            [
                [(self.keep[half], (0, 1)), (self.from_core[half], (1,)), (self.from_far[half], (1,))]
                for half in range(2)
            ]
        )

    def near(self, sums):
        self.got = [over(axis, s) for axis, s in zip(("x", "y"), sums)]

    def block(self, half, k):
        return [
            (self.keep[half], (0, 0, k)),
            (self.from_core[half], (0, k)),
            (self.from_far[half], (0, k)),
            (self.from_near[half], (k,)),
        ]

    def line_sums(self):
        self.from_near = self.got
        return self.add([self.block(half, k) for half, k in ((0, 1), (1, 0), (1, 1))])

    def line(self, sums):
        self.got = [over_z(s, k) for k, s in zip((1, 2, 3), sums)]

    def result(self):
        return total([data[at] for data, at in self.block(0, 0)] + list(self.got))


def reduce_any(out):
    mine = lax.psum_scatter(out, ("y", "c"), scatter_dimension=0, tiled=False)
    return lax.psum_scatter(mine, ("z", "x"), scatter_dimension=0, tiled=True).astype(F32)


def left_lanes(rows):
    return lax.broadcasted_iota(jnp.int32, (rows, 128), 1) < HDIM


def flip(tile):
    return pltpu.roll(tile, HDIM, 1)


def tile(data, number):
    return data[:, number * 128 : (number + 1) * 128]


def join_first(even, odd):
    left = left_lanes(even.shape[0])
    e = [tile(even, i) for i in range(5)]
    o = [tile(odd, i) for i in range(5)]
    query = [e[0], jnp.where(left, e[1], o[0]), o[1]]
    key = [e[3], jnp.where(left, e[4], o[3]), o[4]]
    e1, e2, o2, o3 = flip(e[1]), flip(e[2]), flip(o[2]), flip(o[3])
    value = [jnp.where(left, e1, e2), jnp.where(left, e2, o2), jnp.where(left, o2, o3)]
    return query + key + value


def split_first(query, key, value):
    left = left_lanes(query[0].shape[0])
    none = jnp.zeros_like(query[0])
    v = [flip(t) for t in value]
    even = [
        query[0],
        jnp.where(left, query[1], v[0]),
        jnp.where(left, v[0], v[1]),
        key[0],
        jnp.where(left, key[1], none),
    ]
    odd = [
        jnp.where(left, none, query[1]),
        query[2],
        jnp.where(left, v[1], v[2]),
        jnp.where(left, v[2], key[1]),
        key[2],
    ]
    return even, odd


def turn(field, first):
    width = field.shape[-1]
    return jnp.where(first, pltpu.roll(field, width - HDIM // 2, 1), pltpu.roll(field, HDIM // 2, 1))


def first_half(shape):
    return lax.broadcasted_iota(jnp.int32, shape, 1) % HDIM < HDIM // 2


def qkv_kernel(fast, place, x_own, x_recv, cosine, sine, *refs):
    pieces = refs[: n_pieces(fast)]
    *results, gains, weights_out, q, k, v, weights, held, sems, out_sems = refs[n_pieces(fast) :]
    rows, model = x_own.shape
    per = model // 8 if fast else model

    def leave(half):
        return [
            pltpu.make_async_copy(made.at[half], result.at[half], out_sems.at[half, i])
            for i, (made, result) in enumerate(zip((q, k, v, weights), results + [weights_out]))
        ]

    copies = weight_copies(fast, place, pieces, held, sems, per, model)
    for copy in copies:
        copy.start()
    for copy in copies:
        copy.wait()
    gains[...] = jnp.transpose(held[0, :, 512:640].astype(F32))[64:72, :]
    side = place[2]
    first = first_half((rows, 128))

    def one(half, carry):
        def join(i, carry):
            at = pl.ds(pl.multiple_of(i * 96, 96), 96)
            for number, made in enumerate(join_first(held[2 * half, at, :], held[2 * half + 1, at, :])):
                weights[half, at, number * 128 : (number + 1) * 128] = made
            return carry

        lax.fori_loop(0, model // 96, join, 0)
        for x, where in ((x_own, side), (x_recv, 1 - side)):
            at = pl.ds(pl.multiple_of(where * rows, rows), rows)
            cos, sin = cosine[at, :], sine[at, :]
            made = dotf(x[...], weights[half])
            for p in range(3):
                lanes = slice(p * 128, (p + 1) * 128)
                u = tile(made, p)
                q[half, at, lanes] = ((u * cos + turn(u, first) * sin).astype(BF16) * 0.125).astype(BF16)
                u = tile(made, 3 + p)
                k[half, at, lanes] = (u * cos + turn(u, first) * sin).astype(BF16)
                v[half, at, lanes] = tile(made, 6 + p).astype(BF16)
        for copy in leave(half):
            copy.start()
        return carry

    lax.fori_loop(0, 2, one, 0)
    for half in range(2):
        for copy in leave(half):
            copy.wait()


def project(fast, place, x_own, x_recv, cosine, sine, pieces):
    rows, model = x_own.shape
    field = jax.ShapeDtypeStruct((2, 2 * rows, 384), BF16)
    return pl.pallas_call(
        functools.partial(qkv_kernel, fast),
        out_shape=(field,) * 3
        + (jax.ShapeDtypeStruct((8, model), F32), jax.ShapeDtypeStruct((2, model, 1152), BF16)),
        in_specs=[whole(space=pltpu.SMEM)] + [whole()] * 4 + [whole(space=pl.ANY)] * len(pieces),
        out_specs=(whole(space=pl.ANY),) * 3 + (whole(), whole(space=pl.ANY)),
        scratch_shapes=[pltpu.VMEM((2, 2 * rows, 384), BF16)] * 3
        + [
            pltpu.VMEM((2, model, 1152), BF16),
            pltpu.VMEM((4, model, 640), BF16),
            pltpu.SemaphoreType.DMA((n_blocks(fast),)),
            pltpu.SemaphoreType.DMA((2, 4)),
        ],
        compiler_params=params(),
        name="project_qkv",
    )(place, x_own, x_recv, cosine, sine, *pieces)


class Layout:
    def __init__(self, rows, prompt, step):
        self.rows = rows
        self.prompt = prompt
        self.step = step
        self.pair = 2 * step
        self.cont_blocks = (rows - prompt) // (4 * step)
        self.width = 8 * step


def pair_rows(ref, lay, start):
    return (ref[pl.ds(start, lay.pair), :], ref[pl.ds(lay.rows + start, lay.pair), :])


def pair_start(lay, block, pair):
    return lay.prompt + (2 * block + pair) * lay.pair


def cont_query(ref, lay, block):
    parts = []
    for pair in range(2):
        parts += pair_rows(ref, lay, pair_start(lay, block, pair))
    return jnp.concatenate(parts, 0)


def cont_keys(own, other, lay, block, pair):
    start = pair_start(lay, block, pair)
    return jnp.concatenate(pair_rows(own, lay, start) + pair_rows(other, lay, start), 0)


def causal(count, key_axis):
    key = lax.broadcasted_iota(jnp.int32, (count, count), key_axis)
    row = lax.broadcasted_iota(jnp.int32, (count, count), 1 - key_axis)
    return jnp.where(key <= row, 0.0, NEGATIVE)


def shared_segments(lay):
    return [(0, 0), (0, lay.rows), (1, 0), (1, lay.rows)]


def attend_kernel(lay, place, q_ref, ko, vo, kp, vp, own_mask, mixed, lse, lse_s):
    inner = place[2] != place[3]
    q, keys, values, out = q_ref.at[0], (ko.at[0], kp.at[0]), (vo.at[0], vp.at[0]), mixed.at[0]
    count, width = lay.prompt, lay.width
    half = width // 2
    lane = lax.broadcasted_iota(jnp.int32, (1, 128), 1) // HDIM
    spot = lax.broadcasted_iota(jnp.int32, (1, 128), 1)
    low, high = pl.ds(0, count), pl.ds(lay.rows, count)
    extra = pl.ds(pl.multiple_of(jnp.where(inner, 0, lay.rows), lay.rows), count)
    out[...] = jnp.zeros_like(out)
    lse_s[...] = jnp.zeros_like(lse_s)

    def top(scores):
        return jnp.max(functools.reduce(jnp.maximum, scores), 1, keepdims=True)

    def sums(raised):
        return jnp.sum(functools.reduce(jnp.add, raised), 1, keepdims=True)

    def head(j, carry):
        chosen = lane == j

        def pick(block):
            return jnp.where(chosen, block, jnp.zeros_like(block))

        def finish(at, made, total, highest, number):
            out[at, :] = out[at, :] + pick(made / total).astype(BF16)
            here = pl.ds(number, made.shape[0])
            lse_s[here, :] = jnp.where(spot == j, highest + jnp.log(total), lse_s[here, :])

        q_low, q_high = pick(q[low, :]), pick(q[high, :])
        q_extra = jnp.where(inner, q_low, q_high)
        mask = causal(count, 1)
        s_low = dotf(q_low, keys[0][low, :], LAST) + mask
        s_high = [
            dotf(q_high, keys[0][high, :], LAST) + mask,
            dotf(q_high, keys[0][low, :], LAST),
            dotf(q_high, keys[1][low, :], LAST),
        ]
        s_extra = dotf(q_extra, keys[1][extra, :], LAST)
        s_cont = []
        for block in range(lay.cont_blocks):
            query = pick(cont_query(q, lay, block))
            scores = [dotf(query, keys[o][pl.ds(start, count), :], LAST) for o, start in shared_segments(lay)]
            own = []
            for pair in range(2):
                rows = query[pair * half : (pair + 1) * half, :]
                own.append(dotf(rows, cont_keys(keys[0], keys[1], lay, block, pair), LAST) + own_mask[...])
            s_cont.append(scores + [jnp.concatenate(own, 0)])

        m_low, m_high, m_extra = top([s_low]), top(s_high), top([s_extra])
        m_low = jnp.maximum(m_low, jnp.where(inner, m_extra, NEGATIVE))
        m_high = jnp.maximum(m_high, jnp.where(inner, NEGATIVE, m_extra))
        p_low = jnp.exp(s_low - m_low)
        p_high = [jnp.exp(s - m_high) for s in s_high]
        p_extra = jnp.exp(s_extra - jnp.where(inner, m_low, m_high))
        l_extra = sums([p_extra])
        l_low = sums([p_low]) + jnp.where(inner, l_extra, 0.0)
        l_high = sums(p_high) + jnp.where(inner, 0.0, l_extra)
        o_extra = dotf(p_extra.astype(BF16), values[1][extra, :])
        o_low = dotf(p_low.astype(BF16), values[0][low, :]) + jnp.where(inner, o_extra, 0.0)
        o_high = (
            dotf(p_high[0].astype(BF16), values[0][high, :])
            + dotf(p_high[1].astype(BF16), values[0][low, :])
            + dotf(p_high[2].astype(BF16), values[1][low, :])
            + jnp.where(inner, 0.0, o_extra)
        )
        finish(low, o_low, l_low, m_low, 0)
        finish(high, o_high, l_high, m_high, count)

        for block, scores in enumerate(s_cont):
            highest = top(scores)
            raised = [jnp.exp(s - highest) for s in scores]
            total = sums(raised)
            raised = [r.astype(BF16) for r in raised]
            made = functools.reduce(
                jnp.add, [dotf(r, values[o][pl.ds(start, count), :]) for r, (o, start) in zip(raised, shared_segments(lay))]
            )
            for pair in range(2):
                cut = slice(pair * half, (pair + 1) * half)
                part = made[cut, :] + dotf(raised[-1][cut, :], cont_keys(values[0], values[1], lay, block, pair))
                part = pick(part / total[cut, :]).astype(BF16)
                start = pair_start(lay, block, pair)
                for side in range(2):
                    at = pl.ds(side * lay.rows + start, lay.pair)
                    out[at, :] = out[at, :] + part[side * lay.pair : (side + 1) * lay.pair, :]
            here = pl.ds(2 * count + block * width, width)
            lse_s[here, :] = jnp.where(spot == j, highest + jnp.log(total), lse_s[here, :])
        return carry

    lax.fori_loop(0, 2, head, 0)
    lse[0, 0] = jnp.transpose(lse_s[...])[0:8, :]


def attend(lay, place, q, ko, vo, kp, vp, own_mask):
    total = q.shape[1]
    field = pl.BlockSpec((1, total, 128), lambda h, p, place: (h, 0, p))
    return pl.pallas_call(
        functools.partial(attend_kernel, lay),
        out_shape=(jax.ShapeDtypeStruct(q.shape, BF16), jax.ShapeDtypeStruct((2, 3, 8, total), F32)),
        grid_spec=pltpu.PrefetchScalarGridSpec(
            num_scalar_prefetch=1,
            grid=(2, 3),
            in_specs=[field] * 5 + [pl.BlockSpec(own_mask.shape, lambda h, p, place: (0, 0))],
            out_specs=(field, pl.BlockSpec((1, 1, 8, total), lambda h, p, place: (h, p, 0, 0))),
            scratch_shapes=[pltpu.VMEM((total, 128), F32)],
        ),
        compiler_params=params(30000 * 1024),
        name="attend",
    )(place, q, ko, vo, kp, vp, own_mask)


def attend_back_kernel(
    lay, place, q_ref, ko, vo, kp, vp, mixed, up_ref, lse_ref, own_mask, dq, dko, dvo, dkp, dvp, kacc, vacc, qacc, delta_s
):
    inner = place[2] != place[3]
    q, keys, values = q_ref.at[0], (ko.at[0], kp.at[0]), (vo.at[0], vp.at[0])
    upstream, result, lse = up_ref.at[0], mixed.at[0], lse_ref.at[0]
    count, width = lay.prompt, lay.width
    half = width // 2
    lane = lax.broadcasted_iota(jnp.int32, (1, 128), 1) // HDIM
    kacc[...] = jnp.zeros_like(kacc)
    vacc[...] = jnp.zeros_like(vacc)
    qacc[...] = jnp.zeros_like(qacc)
    low, high = pl.ds(0, count), pl.ds(lay.rows, count)
    shift = jnp.where(inner, 0, 1)
    extra = pl.ds(pl.multiple_of(shift * lay.rows, lay.rows), count)
    either = pl.ds(pl.multiple_of(shift * count, count), count)

    def cont_rows(ref):
        return jnp.concatenate([cont_query(ref, lay, block) for block in range(lay.cont_blocks)], 0)

    def product(rows):
        return rows(upstream).astype(F32) * rows(result).astype(F32)

    heads = jnp.where(
        lax.broadcasted_iota(jnp.int32, (8, 128), 1) // HDIM == lax.broadcasted_iota(jnp.int32, (8, 128), 0), 1.0, 0.0
    ).astype(BF16)
    for at, rows in (
        (slice(0, count), lambda ref: ref[low, :]),
        (slice(count, 2 * count), lambda ref: ref[high, :]),
        (slice(2 * count, 2 * count + lay.cont_blocks * width), cont_rows),
    ):
        made = product(rows)
        coarse = made.astype(BF16)
        fine = (made - coarse.astype(F32)).astype(BF16)
        delta_s[:, at] = dotf(heads, coarse, LAST) + dotf(heads, fine, LAST)

    def head(j, carry):
        chosen = lane == j
        me = pl.ds(j, 1)

        def pick(block):
            return jnp.where(chosen, block, jnp.zeros_like(block))

        def back(key, value, query, grads, mask, log_total, delta):
            s = dotf(key, query, LAST)
            if mask is not None:
                s = s + mask
            share = jnp.exp(s - log_total)
            d = (share * (dotf(value, grads, LAST) - delta)).astype(BF16)
            return dotf(share.astype(BF16), grads), dotf(d, query), dotf(d, key, FIRST)

        def put(other, at, dv, dk):
            vacc[other, at, :] += dv
            kacc[other, at, :] += dk

        query, grads = pick(cont_rows(q)), pick(cont_rows(upstream))
        at = pl.ds(2 * count, lay.cont_blocks * width)
        log_total, delta = lse[0, me, at], delta_s[me, at]
        shared = shared_segments(lay)
        key = jnp.concatenate([keys[o][pl.ds(start, count), :] for o, start in shared], 0)
        value = jnp.concatenate([values[o][pl.ds(start, count), :] for o, start in shared], 0)
        dv, dk, total = back(key, value, query, grads, None, log_total, delta)
        for number, (other, start) in enumerate(shared):
            piece = slice(number * count, (number + 1) * count)
            put(other, pl.ds(start, count), dv[piece, :], dk[piece, :])
        for number in range(2 * lay.cont_blocks):
            block, pair = number // 2, number % 2
            cut = slice(number * half, (number + 1) * half)
            dv, dk, made = back(
                cont_keys(keys[0], keys[1], lay, block, pair),
                cont_keys(values[0], values[1], lay, block, pair),
                query[cut, :],
                grads[cut, :],
                own_mask[...],
                log_total[:, cut],
                delta[:, cut],
            )
            start = pair_start(lay, block, pair)
            for part in range(4):
                piece = slice(part * lay.pair, (part + 1) * lay.pair)
                put(part // 2, pl.ds((part % 2) * lay.rows + start, lay.pair), dv[piece, :], dk[piece, :])
            made = pick(total[cut, :] + made)
            for part in range(2):
                spot = pl.ds(part * lay.rows + start, lay.pair)
                qacc[spot, :] += made[part * lay.pair : (part + 1) * lay.pair, :]
        mask = causal(count, 0)
        at = pl.ds(count, count)
        query, grads, log_total, delta = pick(q[high, :]), pick(upstream[high, :]), lse[0, me, at], delta_s[me, at]
        seen = ((0, high), (0, low), (1, low))
        key = jnp.concatenate([keys[o][spot, :] for o, spot in seen], 0)
        value = jnp.concatenate([values[o][spot, :] for o, spot in seen], 0)
        tall = jnp.concatenate([mask, jnp.zeros((2 * count, count), F32)], 0)
        dv, dk, made = back(key, value, query, grads, tall, log_total, delta)
        for number, (other, spot) in enumerate(seen):
            piece = slice(number * count, (number + 1) * count)
            put(other, spot, dv[piece, :], dk[piece, :])
        qacc[high, :] += pick(made)
        at = pl.ds(0, count)
        dv, dk, made = back(
            keys[0][low, :],
            values[0][low, :],
            pick(q[low, :]),
            pick(upstream[low, :]),
            mask,
            lse[0, me, at],
            delta_s[me, at],
        )
        put(0, low, dv, dk)
        qacc[low, :] += pick(made)
        dv, dk, made = back(
            keys[1][extra, :],
            values[1][extra, :],
            pick(q[extra, :]),
            pick(upstream[extra, :]),
            None,
            lse[0, me, either],
            delta_s[me, either],
        )
        put(1, extra, dv, dk)
        qacc[extra, :] += pick(made)
        return carry

    lax.fori_loop(0, 2, head, 0)
    dq[...] = (qacc[...] * 0.125).astype(BF16)
    dko[...] = kacc[0].astype(BF16)
    dkp[...] = kacc[1].astype(BF16)
    dvo[...] = vacc[0].astype(BF16)
    dvp[...] = vacc[1].astype(BF16)


def attend_back(lay, place, half, q, ko, vo, kp, vp, mixed, upstream, lse, own_mask):
    total = q.shape[1]
    field = pl.BlockSpec((1, total, 128), lambda p, place: (half, 0, p))
    made = pl.BlockSpec((total, 128), lambda p, place: (0, p))
    return pl.pallas_call(
        functools.partial(attend_back_kernel, lay),
        out_shape=(jax.ShapeDtypeStruct((total, 384), BF16),) * 5,
        grid_spec=pltpu.PrefetchScalarGridSpec(
            num_scalar_prefetch=1,
            grid=(3,),
            in_specs=[field] * 7
            + [
                pl.BlockSpec((1, 1, 8, total), lambda p, place: (half, p, 0, 0)),
                pl.BlockSpec(own_mask.shape, lambda p, place: (0, 0)),
            ],
            out_specs=(made,) * 5,
            scratch_shapes=[
                pltpu.VMEM((2, total, 128), F32),
                pltpu.VMEM((2, total, 128), F32),
                pltpu.VMEM((total, 128), F32),
                pltpu.VMEM((8, total), F32),
            ],
        ),
        compiler_params=params(),
        name="attend_back",
    )(place, q, ko, vo, kp, vp, mixed, upstream, lse, own_mask)


def middle_kernel(fast, hid, place, mixed, xo, xr, dyo, dyr_a, dyr_b, gains, *refs):
    count = n_pieces(fast)
    pieces, refs = refs[:count], refs[count:]
    (out_own, out_send, dhp, dmixed), refs = refs[:4], refs[4:]
    count = n_grads(fast)
    grads, refs = refs[:count], refs[count:]
    held, wide_o, gate_s, up_s, hid_s, dgate_s, dup_s, low_t, fed_t, att_t, gain_acc, sum_s, sems = refs
    step = pl.program_id(0)
    model = held.shape[1]
    rows = xo.shape[0]
    per = model // 8 if fast else model
    G, U, D, O = slice(0, hid), slice(hid, 2 * hid), slice(2 * hid, 3 * hid), 3 * hid
    side = jnp.where(step == 0, place[2], 1 - place[2])
    here = pl.ds(pl.multiple_of(side * rows, rows), rows)
    left = left_lanes(model)
    out_copies = weight_copies(fast, place, pieces, held, sems, per, model, slice(O, O + 256))
    other_copies = weight_copies(fast, place, pieces, held, sems, per, model, slice(0, O), n_blocks(fast))

    @pl.when(step == 0)
    def _():
        for copy in out_copies + other_copies:
            copy.start()
        gain_acc[...] = jnp.zeros_like(gain_acc)
        for copy in out_copies:
            copy.wait()
        for half in range(2):
            even, odd = held.at[2 * half], held.at[2 * half + 1]
            wide_o[half, :, 0:128] = even[:, O : O + 128]
            wide_o[half, :, 128:256] = jnp.where(left, even[:, O + 128 : O + 256], odd[:, O : O + 128])
            wide_o[half, :, 256:384] = odd[:, O + 128 : O + 256]

    own = step == 0
    gain_a = gains[0:1, :]
    gain_f = gains[1:2, :]
    pre = jnp.where(own, xo[...], xr[...]).astype(F32)
    for half in range(2):
        pre = pre + dotf(mixed[half, here, :], wide_o[half], LAST)
    scale1 = lax.rsqrt(jnp.mean(pre * pre, -1, keepdims=True) + EPSILON)
    norm1 = pre * scale1
    normed = norm1 * gain_a
    low = normed.astype(BF16)
    low_t[step] = jnp.transpose(low)
    spot = pl.ds(pl.multiple_of(step * rows, rows), rows)

    @pl.when(step == 0)
    def _():
        for copy in other_copies:
            copy.wait()

    def forward(t, carry):
        gate = dotf(low, held[t, :, G])
        up = dotf(low, held[t, :, U])
        gate_s[t] = gate
        up_s[t] = up
        hid_s[t, spot, :] = (gate * jax.nn.sigmoid(gate) * up).astype(BF16)
        return carry

    def add_over(fields, columns):
        field = jnp.concatenate([fields[t, spot, :] for t in range(4)], 1)

        def chunk(n, carry):
            at = pl.ds(pl.multiple_of(n * 256, 256), 256)
            weight = jnp.concatenate([held[t, at, columns] for t in range(4)], 1)
            sum_s[:, at] = sum_s[:, at] + dotf(field, weight, LAST)
            return carry

        lax.fori_loop(0, model // 256, chunk, 0)

    lax.fori_loop(0, 4, forward, 0)
    sum_s[...] = normed
    add_over(hid_s, D)
    resid = sum_s[...]
    scale2 = lax.rsqrt(jnp.mean(resid * resid, -1, keepdims=True) + EPSILON)
    norm2 = resid * scale2
    result = (norm2 * gain_f).astype(BF16)

    @pl.when(own)
    def _():
        out_own[...] = result

    @pl.when(jnp.logical_not(own))
    def _():
        out_send[...] = result

    dy = jnp.where(own, dyo[...], jnp.concatenate([dyr_a[...], dyr_b[...]], 0)).astype(F32)
    gain_acc[1:2, :] += jnp.sum(dy * norm2, 0, keepdims=True)
    e2 = dy * gain_f
    d_resid = scale2 * (e2 - norm2 * jnp.mean(e2 * norm2, -1, keepdims=True))
    d_fed = d_resid.astype(BF16)
    fed_t[step] = jnp.transpose(d_fed)

    def backward(t, carry):
        gate, up = gate_s[t], up_s[t]
        d_hidden = dotf(d_fed, held[t, :, D])
        sig = jax.nn.sigmoid(gate)
        dgate_s[t, spot, :] = (d_hidden * up * sig * (1.0 + gate * (1.0 - sig))).astype(BF16)
        dup_s[t, spot, :] = (d_hidden * gate * sig).astype(BF16)
        return carry

    lax.fori_loop(0, 4, backward, 0)
    sum_s[...] = d_resid
    add_over(dgate_s, G)
    add_over(dup_s, U)
    d_normed = sum_s[...]
    gain_acc[0:1, :] += jnp.sum(d_normed * norm1, 0, keepdims=True)
    e1 = d_normed * gain_a
    d_pre = scale1 * (e1 - norm1 * jnp.mean(e1 * norm1, -1, keepdims=True))
    dhp[...] = d_pre
    d_att = d_pre.astype(BF16)
    att_t[step] = jnp.transpose(d_att)
    for half in range(2):
        dmixed[half] = dotf(d_att, wide_o[half]).astype(BF16)

    @pl.when(step == 1)
    def _():
        columns = jnp.transpose(jnp.broadcast_to(gain_acc[0:8, :], (8, model)))
        lane = lax.broadcasted_iota(jnp.int32, (model, 128), 1) % HDIM
        extra = jnp.where(lane == 0, columns[:, 0:1], jnp.where(lane == 1, columns[:, 1:2], 0.0))
        halves = (place[2], 1 - place[2])
        for half in range(2):
            made = None
            for part in range(2):
                at = pl.ds(pl.multiple_of(halves[part] * rows, rows), rows)
                more = dotf(att_t[part], mixed[half, at, :])
                made = more if made is None else made + more
            even, odd = held.at[2 * half], held.at[2 * half + 1]
            even[:, O : O + 128] = tile(made, 0).astype(BF16)
            even[:, O + 128 : O + 256] = jnp.where(left, tile(made, 1), extra).astype(BF16)
            odd[:, O : O + 128] = jnp.where(left, extra, tile(made, 1)).astype(BF16)
            odd[:, O + 128 : O + 256] = tile(made, 2).astype(BF16)

        def weight(r, carry):
            t = 2 * (place[2] ^ (r // 2)) + (place[3] ^ (r % 2)) if fast else r
            for columns, first, second in ((D, fed_t, hid_s), (G, low_t, dgate_s), (U, low_t, dup_s)):
                made = dotf(first[0], second[t, 0:rows, :]) + dotf(first[1], second[t, rows : 2 * rows, :])
                held[t, :, columns] = made.astype(BF16)
            if fast:
                for dc in range(2):

                    @pl.when(r % 2 == dc)
                    def _(dc=dc):
                        send_block(place, r // 2, dc, held, grads, sems, per, True)

            return carry

        lax.fori_loop(0, 4, weight, 0)
        if fast:
            for r in range(4):
                send_block(place, r // 2, r % 2, held, grads, sems, per, False)
        else:
            store_grads(held, grads[0], sems)


def send_block(place, ky, dc, held, targets, sems, rows, start):
    z, x, y, c = place[0], place[1], place[2], place[3]
    t = 2 * (y ^ ky) + (c ^ dc)

    def move(target, row, number):
        copy = pltpu.make_async_copy(held.at[t, pl.ds(row, rows), :], target, sems.at[number])
        if start:
            copy.start()
        else:
            copy.wait()

    for kz in range(4):
        for kx in range(2):
            half, k = kz // 2, kz % 2
            far, near = (ky, kx) if half == 0 else (kx, ky)
            row = pl.multiple_of(((z ^ kz) * 2 + (x ^ kx)) * rows, rows)
            number = 16 * dc + 8 * ky + 2 * kz + kx
            keep, first, second = targets[3 * half : 3 * half + 3]
            if dc == 0:
                move(keep.at[far, near, k], row, number)
            elif half == 1 or not start:
                move((second, first)[far if half == 1 else 0].at[near, k], row, number)
            else:
                for value, target in ((1, first), (0, second)):

                    @pl.when(far == value)
                    def _(target=target, row=row, number=number, near=near, k=k):
                        move(target.at[near, k], row, number)


def once(shape, index=None):
    return pl.BlockSpec(shape, index or (lambda i, place: (0,) * len(shape)), pipeline_mode=pl.Buffered(1))


def middle(fast, place, mixed, xo, xr, dyo, dyr, gains, pieces, hid):
    rows, model = xo.shape
    columns = 3 * hid + 256
    grads = grad_shapes(fast, model // 8 if fast else model, model, columns)

    def side_at(i, place):
        return (0, jnp.where(i == 0, place[2], 1 - place[2]), 0)

    half_rows = once((rows, model))
    field = once((2, 2 * rows, 384))
    return pl.pallas_call(
        functools.partial(middle_kernel, fast, hid),
        out_shape=(
            jax.ShapeDtypeStruct((rows, model), BF16),
            jax.ShapeDtypeStruct((rows, model), BF16),
            jax.ShapeDtypeStruct((2 * rows, model), F32),
            jax.ShapeDtypeStruct(mixed.shape, BF16),
        )
        + grads,
        grid_spec=pltpu.PrefetchScalarGridSpec(
            num_scalar_prefetch=1,
            grid=(2,),
            in_specs=[field]
            + [half_rows] * 3
            + [once((rows // 2, model))] * 2
            + [once((8, model))]
            + [whole(space=pl.ANY)] * len(pieces),
            out_specs=(
                pl.BlockSpec((rows, model), lambda i, place: (0, 0)),
                pl.BlockSpec((rows, model), lambda i, place: (0, 0)),
                pl.BlockSpec((rows, model), lambda i, place: (i, 0)),
                pl.BlockSpec((2, rows, 384), side_at),
            )
            + (whole(space=pl.ANY),) * len(grads),
            scratch_shapes=[
                pltpu.VMEM((4, model, columns), BF16),
                pltpu.VMEM((2, model, 384), BF16),
                pltpu.VMEM((4, rows, hid), F32),
                pltpu.VMEM((4, rows, hid), F32),
                pltpu.VMEM((4, 2 * rows, hid), BF16),
                pltpu.VMEM((4, 2 * rows, hid), BF16),
                pltpu.VMEM((4, 2 * rows, hid), BF16),
                pltpu.VMEM((2, model, rows), BF16),
                pltpu.VMEM((2, model, rows), BF16),
                pltpu.VMEM((2, model, rows), BF16),
                pltpu.VMEM((8, model), F32),
                pltpu.VMEM((rows, model), F32),
                pltpu.SemaphoreType.DMA((2 * n_blocks(fast),)),
            ],
        ),
        compiler_params=params(),
        name="middle",
    )(place, mixed, xo, xr, dyo, *dyr, gains, *pieces)


def qkv_back_kernel(fast, place, x_own, x_recv, cosine, sine, dhp_ref, weights_ref, *refs):
    fields = [refs[2 * i : 2 * i + 2] for i in range(5)]
    dx_own, dx_sends = refs[10], refs[11:13]
    grads, refs = refs[13 : 13 + n_grads(fast)], refs[13 + n_grads(fast) :]
    held, joined, made, x_t, dx, base, weights, moved, sems, extra_sems = refs
    rows, model = x_own.shape
    per = model // 8 if fast else model
    side = place[2]
    first = first_half((rows, 128))
    copies = [pltpu.make_async_copy(dhp_ref, base, extra_sems.at[0])]
    for half in range(2):
        copies.append(pltpu.make_async_copy(weights_ref.at[half], weights.at[half], extra_sems.at[1 + 6 * half]))
        for i in range(5):
            copies.append(pltpu.make_async_copy(fields[i][half], moved.at[half, i], extra_sems.at[2 + i + 6 * half]))
    for copy in copies[1:] + copies[:1]:
        copy.start()
    for number, x in enumerate((x_own, x_recv)):
        x_t[number] = jnp.transpose(x[...])
    for copy in copies[1:7]:
        copy.wait()
    dx[...] = jnp.zeros_like(dx)

    def one(half, carry):
        @pl.when(half == 1)
        def _():
            for copy in copies[7:]:
                copy.wait()

        def turn_back(number, carry):
            at = pl.ds(pl.multiple_of((side ^ number) * rows, rows), rows)
            cos, sin = cosine[at, :], sine[at, :]
            for p in range(3):
                lanes = slice(p * 128, (p + 1) * 128)
                query, key, value, key_more, value_more = [moved[half, i, at, lanes].astype(F32) for i in range(5)]
                joined[number, 0, :, lanes] = (query * cos - turn(query, first) * sin).astype(BF16)
                key = key + key_more
                joined[number, 1, :, lanes] = (key * cos - turn(key, first) * sin).astype(BF16)
                joined[number, 2, :, lanes] = (value + value_more).astype(BF16)
            whole_row = jnp.concatenate([joined[number, kind] for kind in range(3)], 1)
            spot = pl.ds(pl.multiple_of(number * rows, rows), rows)
            dx[spot, :] = dx[spot, :] + dotf(whole_row, weights[half], LAST)
            return carry

        def weight(kind, carry):
            made[kind] = (dotf(x_t[0], joined[0, kind]) + dotf(x_t[1], joined[1, kind])).astype(BF16)
            return carry

        lax.fori_loop(0, 2, turn_back, 0)
        lax.fori_loop(0, 3, weight, 0)

        def split(i, carry):
            at = pl.ds(pl.multiple_of(i * 96, 96), 96)
            even, odd = split_first(*[[tile(made[kind, at, :], p) for p in range(3)] for kind in range(3)])
            for p in range(5):
                held[2 * half, at, p * 128 : (p + 1) * 128] = even[p]
                held[2 * half + 1, at, p * 128 : (p + 1) * 128] = odd[p]
            return carry

        lax.fori_loop(0, model // 96, split, 0)
        if fast:
            for dc in range(2):
                send_block(place, side ^ half, dc, held, grads, sems, per, True)
        return carry

    lax.fori_loop(0, 2, one, 0)
    copies[0].wait()
    dx_own[...] = dx[0:rows, :] + base[0:rows, :]
    for number in range(2):
        cut = slice(rows + number * (rows // 2), rows + (number + 1) * (rows // 2))
        dx_sends[number][...] = (dx[cut, :] + base[cut, :]).astype(BF16)
    if fast:
        for half in range(2):
            for dc in range(2):
                send_block(place, side ^ half, dc, held, grads, sems, per, False)
    else:
        store_grads(held, grads[0], sems)


def project_back(fast, place, x_own, x_recv, cosine, sine, dhp, weights, fields):
    rows, model = x_own.shape
    grads = grad_shapes(fast, model // 8 if fast else model, model, 640)
    return pl.pallas_call(
        functools.partial(qkv_back_kernel, fast),
        out_shape=(jax.ShapeDtypeStruct((rows, model), F32),)
        + (jax.ShapeDtypeStruct((rows // 2, model), BF16),) * 2
        + grads,
        in_specs=[whole(space=pltpu.SMEM)]
        + [whole()] * 4
        + [whole(space=pl.ANY)] * 2
        + [whole(space=pl.ANY)] * 10,
        out_specs=(whole(),) * 3 + (whole(space=pl.ANY),) * len(grads),
        scratch_shapes=[
            pltpu.VMEM((4, model, 640), BF16),
            pltpu.VMEM((2, 3, rows, 384), BF16),
            pltpu.VMEM((3, model, 384), BF16),
            pltpu.VMEM((2, model, rows), BF16),
            pltpu.VMEM((2 * rows, model), F32),
            pltpu.VMEM((2 * rows, model), F32),
            pltpu.VMEM((2, model, 1152), BF16),
            pltpu.VMEM((2, 5, 2 * rows, 384), BF16),
            pltpu.SemaphoreType.DMA((n_blocks(fast),)),
            pltpu.SemaphoreType.DMA((13,)),
        ],
        compiler_params=params(),
        name="project_back",
    )(place, x_own, x_recv, cosine, sine, dhp, weights, *fields)


def tables(quarters, prompt, step, groups, plen):
    half = HDIM // 2
    places = []
    for quarter in quarters:
        places.append((quarter * prompt + jnp.arange(prompt)).astype(F32))
        places.append(jnp.tile((plen + quarter * step + jnp.arange(step)).astype(F32), groups))
    lanes = jnp.arange(2 * HDIM)
    frequency = 10000.0 ** (-(lanes % half).astype(F32) / half)
    angle = jnp.concatenate(places)[:, None] * frequency[None, :]
    return jnp.cos(angle), jnp.sin(angle) * jnp.where(lanes % HDIM < half, -1.0, 1.0)[None, :]


def own_continuation_mask(quarters, step):
    offset = jnp.arange(2 * step) % step
    cont = jnp.arange(2 * step) // step
    places = jnp.concatenate([quarter * step + offset for quarter in quarters])
    number = jnp.tile(cont, 4)
    rows = 4 * step
    allowed = (places[:, None] <= places[None, :rows]) & (number[:, None] == number[None, :rows])
    mask = jnp.where(allowed, 0.0, NEGATIVE).astype(F32)
    return mask, mask.T


def on_device(
    fast,
    prompt_tokens,
    continuation_tokens,
    prompt_index,
    attention_gain,
    query_weight,
    key_weight,
    value_weight,
    output_weight,
    feedforward_gain,
    gate_weight,
    up_weight,
    down_weight,
    prompt_cotangent,
    continuation_cotangent,
):
    z, x, y, c = [lax.axis_index(name).astype(jnp.int32) for name in ("z", "x", "y", "c")]
    place = jnp.stack([z, x, y, c])
    prompts, prompt_rows, model = prompt_tokens.shape
    conts, step, _ = continuation_tokens.shape
    groups = conts // prompts
    plen = 4 * prompt_rows
    rows = prompt_rows + groups * step
    lay = Layout(rows, prompt_rows, step)
    shard_rows, columns = query_weight.shape
    hid = gate_weight.shape[1]
    local = 2 * y + c
    other = 2 * y + (1 - c)
    quarters = [jnp.minimum(t, 3 - t) if low else jnp.maximum(t, 3 - t) for t in (local, other) for low in (1, 0)]

    gains = [attention_gain[:, None], feedforward_gain[:, None], jnp.zeros((shard_rows, 62), BF16)]
    first = [query_weight, value_weight, key_weight]
    first = jnp.where(c == 0, jnp.concatenate(first + gains, 1), jnp.concatenate(gains + first, 1))
    wide = [gate_weight, up_weight]
    down, out, gap = down_weight.T, output_weight.T, jnp.zeros((shard_rows, 64), BF16)
    rest = jnp.where(c == 0, jnp.concatenate(wide + [down, out, gap], 1), jnp.concatenate(wide + [down, gap, out], 1))

    def swap(data):
        return lax.ppermute(data, ("y", "c"), [(0, 3), (3, 0), (1, 2), (2, 1)])

    if fast:
        x_own, x_send = pack(place, prompt_index, prompt_tokens, continuation_tokens, 1)
        x_recv = swap(x_send)
        dy_own, *dy_sends = pack(after(place, x_send), prompt_index, prompt_cotangent, continuation_cotangent, 2)
        first = after(first, dy_sends[0])
        got = gather_line(first)
        line = stack_line(first, after(got, rest))
        got = gather_near(line)
        rest = after(rest, *line)
        rest_got = gather_line(rest)
        dy_first = swap(after(dy_sends[0], *line))
        cosine, sine = tables(after(tuple(quarters[:2]), *line), prompt_rows, step, groups, plen)
        own_mask, row_mask = own_continuation_mask(after(tuple(quarters), *line), step)
        plane = stack_near(line, after(got, cosine, sine, own_mask, row_mask, x_recv, dy_first, rest_got[0], rest_got[1]))
        far = gather_far(plane)
        dy_second = swap(after(dy_sends[1], *plane))
        dy_recv = (dy_first, dy_second)
        first_pieces = gather_core(plane, far)
        rest_line = stack_line(rest, after(rest_got, *far))
        rest_got = gather_near(rest_line)
        q, k, v, gains, weights = project(
            fast, place, x_own, x_recv, cosine, sine, after(first_pieces, dy_second, *rest_line)
        )
        rest_got = after(rest_got, q)
        k, v = after((k, v), *rest_got)
        k_other, v_other = over("c", k), over("c", v)
        rest_plane = stack_near(rest_line, after(rest_got, q))
        rest_far = gather_far(rest_plane)
        mixed, lse = attend(lay, place, q, k, v, k_other, v_other, after(row_mask, *rest_plane))
        rest_plane = after(rest_plane, mixed)
        core_plane = [over("c", piece) for piece in rest_plane]
        rest_far = after(rest_far, mixed, *core_plane)
        core_far = [over("c", piece) for piece in rest_far]
        rest_pieces = (rest_plane[0], rest_far[0], rest_plane[1], rest_far[1])
        rest_pieces += (core_plane[0], core_far[0], core_plane[1], core_far[1])
    else:
        x_own, x_send = pack(place, prompt_index, prompt_tokens, continuation_tokens, 1)
        dy_own, *dy_sends = pack(place, prompt_index, prompt_cotangent, continuation_cotangent, 2)
        x_recv, dy_recv = swap(x_send), [swap(piece) for piece in dy_sends]
        first_pieces, rest_pieces = gather_any(first), gather_any(rest)
        cosine, sine = tables(quarters[:2], prompt_rows, step, groups, plen)
        own_mask, row_mask = own_continuation_mask(quarters, step)
        q, k, v, gains, weights = project(fast, place, x_own, x_recv, cosine, sine, first_pieces)
        k_other, v_other = over("c", k), over("c", v)
        mixed, lse = attend(lay, place, q, k, v, k_other, v_other, row_mask)
    made = middle(fast, place, mixed, x_own, x_recv, dy_own, dy_recv, gains, rest_pieces, hid)
    out_own, out_send, dhp, dmixed = made[:4]
    grads = made[4:]

    def back(half, mask):
        return attend_back(lay, place, half, q, k, v, k_other, v_other, mixed, dmixed, lse, mask)

    def collect(made):
        return [[m[i] for m in made] for i in range(3)] + [[over("c", m[i]) for m in made] for i in (3, 4)]

    if fast:
        rest_sum = Reduction(grads, True)
        sums = rest_sum.far_sums()
        rest_sum.far(sums)
        done = [back(0, after(own_mask, *sums))]
        rest_sum.gate(done[0][0])
        sums = rest_sum.near_sums()
        rest_sum.near(sums)
        out_recv = swap(after(out_send, *sums))
        done.append(back(1, after(own_mask, *sums)))
        rest_sum.gate(done[1][0])
        sums = rest_sum.line_sums()
        rest_sum.line(sums)
        fields = sum(collect(done), [])
        made = project_back(fast, place, x_own, x_recv, cosine, sine, after(dhp, out_recv, *sums), weights, fields)
        dx_own, dx_sends = made[0], made[1:3]
        first_sum = Reduction(after(made[3:], rest_sum.got[0], rest_sum.got[1]), False)
        out_prompt, out_cont = unpack(place, prompt_index, out_own, after(out_recv, dx_own), prompt_rows, step, BF16)
        sums = first_sum.far_sums()
        first_sum.far(sums)
        dx_first = swap(dx_sends[0])
        rest_sum.gate(out_prompt, dx_first, *sums)
        rest_grad = rest_sum.result()
        placed = scatter(after(place, rest_grad), prompt_index, True, (dx_own,), prompt_rows, step)
        first_sum.gate(rest_grad, *placed)
        sums = first_sum.near_sums()
        first_sum.near(sums)
        sums = first_sum.line_sums()
        first_sum.line(sums)
        dx_recv = (dx_first, swap(after(dx_sends[1], placed[0], *sums)))
        first_grad = first_sum.result()
    else:
        out_recv = swap(out_send)
        rest_grad = reduce_any(grads[0])
        fields = sum(collect([back(half, own_mask) for half in range(2)]), [])
        made = project_back(fast, place, x_own, x_recv, cosine, sine, dhp, weights, fields)
        dx_own, dx_recv = made[0], (swap(made[1]), swap(made[2]))
        placed = scatter(place, prompt_index, True, (dx_own,), prompt_rows, step)
        first_grad = reduce_any(made[3])
        out_prompt, out_cont = unpack(place, prompt_index, out_own, out_recv, prompt_rows, step, BF16)
    dx_prompt, dx_cont = scatter(place, prompt_index, False, dx_recv, prompt_rows, step, placed)
    first_grad = jnp.where(c == 0, first_grad[:, : 3 * columns], first_grad[:, 64:])
    start = 3 * hid
    gain_grads = jnp.where(c == 0, rest_grad[:, start + columns : start + columns + 2], rest_grad[:, start : start + 2])
    out_grad = jnp.where(c == 0, rest_grad[:, start : start + columns], rest_grad[:, start + 64 :])
    return (
        out_prompt,
        out_cont,
        dx_prompt,
        dx_cont,
        gain_grads[:, 0],
        first_grad[:, :columns],
        first_grad[:, 2 * columns :],
        first_grad[:, columns : 2 * columns],
        out_grad.T,
        gain_grads[:, 1],
        rest_grad[:, :hid],
        rest_grad[:, hid : 2 * hid],
        rest_grad[:, 2 * hid : start].T,
    )


def solution(mesh):
    parts = mesh.shape["dp"]
    grid = Mesh(mesh.devices.reshape(parts // 2, 2, 2, 2), ("z", "x", "y", "c"))
    dp, tensor = ("z", "x"), ("y", "c")
    fast = parts == 8
    tokens, columns, rows, vector = P(dp, tensor, None), P(dp, tensor), P(tensor, dp), P(dp)
    in_specs = (
        tokens,
        tokens,
        vector,
        vector,
        columns,
        columns,
        columns,
        rows,
        vector,
        columns,
        columns,
        rows,
        tokens,
        tokens,
    )
    out_specs = (
        tokens,
        tokens,
        tokens,
        tokens,
        vector,
        columns,
        columns,
        columns,
        rows,
        vector,
        columns,
        columns,
        rows,
    )
    return jax.shard_map(
        functools.partial(on_device, fast), mesh=grid, in_specs=in_specs, out_specs=out_specs, check_vma=False
    )
```
